32 devices in a mesh: groups: 2 (over y), along: 4 (over z), cross: 2 (over x), sub: 2 (over core).
Axes of the slice: x: 2, y: 2, z: 4, core: 2. Of those that a mesh axis runs over, the one named last changes fastest.
Arguments:
- state_zero: float32 [12, 64, 512], P(None, ('groups', 'along'), ('cross', 'sub')), parts along dimension 1, may hold values from -6 to 6
- storm_field: float32 [12, 64, 512], P(None, ('groups', 'along'), ('cross', 'sub')), parts along dimension 1, may hold values from -6 to 6
- wet_mask: int32 [2, 64, 512], P(None, ('groups', 'along'), ('cross', 'sub')), parts along dimension 1, may hold values 0 or 1
- dune_mask: int32 [2, 64, 512], P(None, ('groups', 'along'), ('cross', 'sub')), parts along dimension 1, may hold values 0 or 1
- class_ids: int32 [64, 512], P(('groups', 'along'), ('cross', 'sub')), parts along dimension 0, may hold values from 0 to 7
- w_one: float32 [32, 128], replicated, may hold values from -1 to 1
- b_one: float32 [128], replicated, may hold values from -3 to 3
- w_two: float32 [128, 128], replicated, may hold values from -0.5 to 0.5
- b_two: float32 [128], replicated, may hold values from -3 to 3
- w_out: float32 [128, 8], replicated, may hold values from -0.5 to 0.5
- b_out: float32 [8], replicated, may hold values from -3 to 3
- final_cotangent: float32 [12, 64, 512], P(None, ('groups', 'along'), ('cross', 'sub')), parts along dimension 1, may hold values from -6 to 6
Outputs:
- grad_state: float32 [12, 64, 512], P(None, ('groups', 'along'), ('cross', 'sub')), parts along dimension 1
- grad_w_one: float32 [64, 128], P('groups'), parts along dimension 0
- grad_b_one: float32 [256], P('groups'), parts along dimension 0
- grad_w_two: float32 [256, 128], P('groups'), parts along dimension 0
- grad_b_two: float32 [256], P('groups'), parts along dimension 0
- grad_w_out: float32 [256, 8], P('groups'), parts along dimension 0
- grad_b_out: float32 [16], P('groups'), parts along dimension 0
The draws below stay inside these ranges and needn't reach their ends.
There are 2 independent parts, one for each index of `groups`. The reference program is written for one: setup_inputs(seed, part) draws one part's arguments, and reference() takes and returns one part's arrays. A program takes and returns all parts, laid end to end along the dimension named above; an argument that names none is the same for every part. Nothing has to cross between parts.
All inputs are finite; a program needn't handle non-finite values. No bound on the sum of `wet_mask` or of `dune_mask` on one device may be relied on, other than what follows from the above.
Results may differ from the reference program's by a relative error of at most 0.0001.
Values sent between devices are 32-bit elements; how exact they have to be, the bound alone decides.
A program may use at most 64 MiB of HBM per device.

```python
import math
import jax
import jax.numpy as jnp
from jax import lax

FIELDS = 12
FEAT = 32
HIDDEN_SIZE = 128
CLASSES = 8
STORM = 12
STEPS = 2
NA = 32
NC = 512


def touch_ends(array, stream_key, smallest, high):
    index_at = [jax.random.randint(jax.random.fold_in(stream_key, axis), (), 0, length) for axis, length in enumerate(array.shape)]
    main_axis = array.shape.index(max(array.shape))
    neighbour = index_at[:main_axis] + [(index_at[main_axis] + 1) % array.shape[main_axis]] + index_at[main_axis + 1:]
    return array.at[tuple(index_at)].set(smallest).at[tuple(neighbour)].set(high)


def block_levels(stream_key, shape, shards, smallest, top_value):
    factor_of = 1.0
    for position, parts in shards:
        draws = jax.random.uniform(jax.random.fold_in(jax.random.fold_in(stream_key, 6), position), (parts,), jnp.float32, smallest / len(shards), top_value / len(shards))
        factor_of = factor_of * jnp.repeat(jnp.exp(draws), shape[position] // parts).reshape((-1,) + (1,) * (len(shape) - 1 - position))
    return factor_of


def centred(own_key, shape, deviation, limit, pieces=(), kind=jnp.bfloat16):
    entries = deviation * jax.random.normal(own_key, shape, jnp.float32)
    if pieces:
        entries = entries * block_levels(own_key, shape, pieces, -0.22, 0.18)
    return jnp.clip(entries, -limit, limit).astype(kind)


def setup_inputs(seed: int = 0, part: int = 0) -> dict:
    arg_keys = jax.random.split(jax.random.key(seed), 13)
    part_splits = jax.random.split(jax.random.fold_in(arg_keys[12], part), 13)
    return {
        "state_zero": centred(part_splits[0], (FIELDS, NA, NC), 1.0, 6.0, ((1, 4), (2, 4)), jnp.float32),
        "storm_field": centred(part_splits[1], (STORM, NA, NC), 1.0, 6.0, ((1, 4), (2, 4)), jnp.float32),
        "wet_mask": touch_ends((jax.random.randint(part_splits[2], (STEPS, NA, NC), 0, 4) < 3).astype(jnp.int32), jax.random.fold_in(part_splits[2], 1), 0, 1),
        "dune_mask": touch_ends((jax.random.randint(part_splits[3], (STEPS, NA, NC), 0, 4) < 1).astype(jnp.int32), jax.random.fold_in(part_splits[3], 1), 0, 1),
        "class_ids": touch_ends(jax.random.randint(part_splits[4], (NA, NC), 0, CLASSES), jax.random.fold_in(part_splits[4], 1), 0, CLASSES - 1).astype(jnp.int32),
        "w_one": centred(arg_keys[5], (FEAT, HIDDEN_SIZE), FEAT ** -0.5, 1.0, (), jnp.float32),
        "b_one": centred(arg_keys[6], (HIDDEN_SIZE,), 0.5, 3.0, (), jnp.float32),
        "w_two": centred(arg_keys[7], (HIDDEN_SIZE, HIDDEN_SIZE), HIDDEN_SIZE ** -0.5, 0.5, (), jnp.float32),
        "b_two": centred(arg_keys[8], (HIDDEN_SIZE,), 0.5, 3.0, (), jnp.float32),
        "w_out": centred(arg_keys[9], (HIDDEN_SIZE, CLASSES), HIDDEN_SIZE ** -0.5, 0.5, (), jnp.float32),
        "b_out": centred(arg_keys[10], (CLASSES,), 0.5, 3.0, (), jnp.float32),
        "final_cotangent": centred(part_splits[11], (FIELDS, NA, NC), 1.0, 6.0, ((1, 4), (2, 4)), jnp.float32),
    }


highest = lax.Precision.HIGHEST
diffusion = 0.15
advection = 0.2
friction = 0.05
pickup_gain = 0.5
settling = 0.2
bed_diffusion = 0.1

def layer_stack(weights, features):
    w_one, b_one, w_two, b_two, w_out, b_out = weights
    hidden_one = jax.nn.silu(jnp.einsum('fh,frc->hrc', w_one, features, precision=highest) + b_one[:, None, None])
    hidden_two = jax.nn.silu(jnp.einsum('hk,hrc->krc', w_two, hidden_one, precision=highest) + b_two[:, None, None])
    return jnp.einsum('ko,krc->orc', w_out, hidden_two, precision=highest) + b_out[:, None, None]

def closure(weights, features, block_rows):
    stack_fn = jax.checkpoint(layer_stack)
    total_rows = features.shape[1]
    if total_rows <= block_rows:
        return stack_fn(weights, features)
    covered = total_rows // block_rows * block_rows
    stacked = jnp.moveaxis(features[:, :covered].reshape(features.shape[0], covered // block_rows, block_rows, features.shape[2]), 1, 0)

    def one_block(block_piece):
        return stack_fn(weights, block_piece)
    mapped = lax.map(one_block, stacked)
    result = jnp.moveaxis(mapped, 0, 1).reshape(mapped.shape[1], covered, features.shape[2])
    if total_rows > covered:
        result = jnp.concatenate([result, stack_fn(weights, features[:, covered:])], axis=1)
    return result

def advance(weights, padded, wet_cells, dune_cells, class_cells, storm_cells, block_rows):
    centre = padded[:, 1:-1, 1:-1]
    north_cells = padded[:, :-2, 1:-1]
    south_cells = padded[:, 2:, 1:-1]
    west_cells = padded[:, 1:-1, :-2]
    east_cells = padded[:, 1:-1, 2:]
    features = jnp.concatenate([centre[:4], north_cells[:4], south_cells[:4], west_cells[:4], east_cells[:4], storm_cells], axis=0)
    outputs = closure(weights, features, block_rows)
    chooser = (class_cells.astype(jnp.float32)[None] == jnp.arange(outputs.shape[0], dtype=jnp.float32)[:, None, None]).astype(jnp.float32)
    pickup = jax.nn.softplus(lax.optimization_barrier(jnp.sum(outputs * chooser, axis=0))) * (1.0 - dune_cells)
    laplace = north_cells + south_cells + west_cells + east_cells - 4.0 * centre
    along_diff = south_cells - north_cells
    cross_diff = east_cells - west_cells
    sediment = centre[4:]
    depth_tend = diffusion * laplace[0] - advection * (along_diff[1] + cross_diff[2])
    along_tend = diffusion * laplace[1] - advection * along_diff[0] - friction * centre[1]
    cross_tend = diffusion * laplace[2] - advection * cross_diff[0] - friction * centre[2]
    bed_tend = bed_diffusion * laplace[3] - pickup_gain * pickup + settling * lax.optimization_barrier(jnp.sum(sediment, axis=0))
    sediment_tend = diffusion * laplace[4:] - advection * (centre[1] * along_diff[4:] + centre[2] * cross_diff[4:]) + pickup_gain * pickup * chooser - settling * sediment
    tendency = jnp.concatenate([jnp.stack([depth_tend, along_tend, cross_tend, bed_tend]), sediment_tend], axis=0)
    return centre + wet_cells[None] * tendency

def reference(state_zero, storm_field, wet_mask, dune_mask, class_ids, w_one, b_one, w_two, b_two, w_out, b_out, final_cotangent):
    weights = (w_one, b_one, w_two, b_two, w_out, b_out)
    wet_float = wet_mask.astype(jnp.float32)
    dune_float = dune_mask.astype(jnp.float32)

    def unrolled(start, params):
        current = start
        for step_index in range(STEPS):
            padded = jnp.pad(current, ((0, 0), (1, 1), (1, 1)))
            current = advance(params, padded, wet_float[step_index], dune_float[step_index], class_ids, storm_field, 8)
        return current
    final_state, pullback = jax.vjp(unrolled, state_zero, weights)
    grad_state, grads = pullback(final_cotangent)
    factor = 1.0 / math.sqrt(state_zero.shape[1] * state_zero.shape[2])
    return (grad_state, grads[0] * factor, grads[1] * factor, grads[2] * factor, grads[3] * factor, grads[4] * factor, grads[5] * factor)
```

```python
import functools
import math

import jax
import jax.numpy as jnp
from jax import lax
from jax.experimental import pallas as pl
from jax.experimental.pallas import tpu as pltpu
from jax.sharding import PartitionSpec as P

MESH = pl.DeviceIdType.MESH
f32 = jnp.float32
bf16 = jnp.bfloat16
diffusion = 0.15
advection = 0.2
friction = 0.05
pickup_gain = 0.5
settling = 0.2
bed_diffusion = 0.1

ROW_B1 = 32
ROWS_ONE = 40
ROW_B2 = 128
ROW_WO = 136
ROW_BO = 144
ROWS_TWO = 152
LANES = 256
CHUNKS = 4


def split(x):
    high = x.astype(bf16)
    low = (x - high.astype(f32)).astype(bf16)
    return high, low


def mm(a, b):
    return lax.dot_general(a, b, (((1,), (0,)), ((), ())), preferred_element_type=f32)


def mm_nt(a, b):
    return lax.dot_general(a, b, (((1,), (1,)), ((), ())), preferred_element_type=f32)


def kernel(
    nal, ncr, nsu, factor,
    state_hbm, cid_hbm, w1_hbm, b1_hbm, w2_hbm, b2_hbm, wo_hbm, bo_hbm,
    storm_hbm, wet_hbm, dune_hbm, cot_hbm,
    gstate_ref, dst_one, dst_two,
    state_ref, cid_ref, w1_ref, b1_ref, w2_ref, b2_ref, wo_ref, bo_ref,
    storm_ref, wet_ref, dune_ref, cot_ref, load_sem,
    snd_row, snd_col, rcv_row, rcv_col, send_sem, recv_sem,
    feat_ref, dfeat_ref, z_ref, dz_ref,
    b1b_ref, b2b_ref, wsel_ref,
    fh_ref, fl_ref, h1h_ref, h1l_ref, h2h_ref, h2l_ref,
    act1_ref, q2_ref, d1h_ref, d1l_ref, d2h_ref, d2l_ref, drh_ref, drl_ref,
    acc_one, rcv_a_one, src_b_one, rcv_b_one,
    acc_two, rcv_a_two, src_b_two, rcv_b_two,
    sa_send, sa_recv, sb_send, sb_recv, sc_send, sc_recv,
):
    ncs = ncr * nsu
    g = lax.axis_index("groups")
    al = lax.axis_index("along")
    cr = lax.axis_index("cross")
    su = lax.axis_index("sub")
    cs = cr * nsu + su

    def dev(a, c):
        return (g, a, c // nsu, c % nsu)

    has_dst = (al > 0, al < nal - 1, cs > 0, cs < ncs - 1)
    has_src = (al < nal - 1, al > 0, cs < ncs - 1, cs > 0)
    dst_dev = (
        dev(al - 1, cs), dev(al + 1, cs), dev(al, cs - 1), dev(al, cs + 1),
    )

    loads = [
        pltpu.make_async_copy(src, dst, load_sem.at[i])
        for i, (src, dst) in enumerate((
            (state_hbm, state_ref), (cid_hbm, cid_ref), (w1_hbm, w1_ref), (b1_hbm, b1_ref),
            (w2_hbm, w2_ref), (b2_hbm, b2_ref), (wo_hbm, wo_ref), (bo_hbm, bo_ref),
            (storm_hbm, storm_ref), (wet_hbm, wet_ref), (dune_hbm, dune_ref), (cot_hbm, cot_ref),
        ))
    ]
    loads[0].start()
    rcv_row[...] = jnp.zeros_like(rcv_row)
    rcv_col[...] = jnp.zeros_like(rcv_col)

    barrier = pltpu.get_barrier_semaphore()
    near_only = nal <= 4 and ncs <= 4
    if near_only:
        for d in range(4):
            @pl.when(has_dst[d])
            def _():
                pl.semaphore_signal(barrier, inc=1, device_id=dst_dev[d], device_id_type=MESH)
    else:
        for j in range(1, ncs):
            pl.semaphore_signal(
                barrier, inc=1, device_id=dev(al, lax.rem(cs + j, ncs)), device_id_type=MESH
            )
        for j in range(1, nal):
            pl.semaphore_signal(
                barrier, inc=1, device_id=dev(lax.rem(al + j, nal), cs), device_id_type=MESH
            )
    for load in loads[1:]:
        load.start()

    row = lax.broadcasted_iota(jnp.int32, (8, 128), 0)
    lane = lax.broadcasted_iota(jnp.int32, (8, 128), 1)

    def copy_of(k, d):
        if d < 2:
            src, dst = snd_row.at[k, d], rcv_row.at[k, d]
        else:
            src, dst = snd_col.at[k, d - 2], rcv_col.at[k, d - 2]
        return pltpu.make_async_remote_copy(
            src_ref=src, dst_ref=dst, send_sem=send_sem.at[k, d], recv_sem=recv_sem.at[k, d],
            device_id=dst_dev[d], device_id_type=MESH,
        )

    def fill(k, xn, xs, xw, xe):
        west = jnp.zeros((8, 128), f32)
        east = jnp.zeros((8, 128), f32)
        for f in range(12):
            snd_row[k, 0, f:f + 1, :] = xn[f][0:1, :]
            snd_row[k, 1, f:f + 1, :] = xs[f][7:8, :]
            west = jnp.where(lane == f, pltpu.roll(xw[f], f, 1) if f else xw[f], west)
            east = jnp.where(lane == f, pltpu.roll(xe[f], f + 1, 1), east)
        snd_col[k, 0] = west
        snd_col[k, 1] = east

    def launch(k):
        for d in range(4):
            @pl.when(has_dst[d])
            def _():
                copy_of(k, d).start()

    def finish(k):
        for d in range(4):
            @pl.when(has_src[d])
            def _():
                copy_of(k, d).wait_recv()

    def finish_sends(k):
        for d in range(4):
            @pl.when(has_dst[d])
            def _():
                copy_of(k, d).wait_send()

    def south_of(x, f, k):
        return jnp.where(row == 7, rcv_row[k, 0, f:f + 1, :], pltpu.roll(x, 7, 0))

    def north_of(x, f, k):
        return jnp.where(row == 0, rcv_row[k, 1, f:f + 1, :], pltpu.roll(x, 1, 0))

    def east_of(x, f, k):
        return jnp.where(lane == 127, pltpu.roll(rcv_col[k, 0], 127 - f, 1), pltpu.roll(x, 127, 1))

    def west_of(x, f, k):
        halo = rcv_col[k, 1]
        return jnp.where(lane == 0, pltpu.roll(halo, 128 - f, 1) if f else halo, pltpu.roll(x, 1, 1))

    loads[0].wait()
    V0 = [state_ref[f] for f in range(12)]
    fill(0, V0, V0, V0, V0)
    if near_only:
        beside = (al + nal - 1) // nal + (2 * nal - 2 - al) // nal
        beside = beside + (cs + ncs - 1) // ncs + (2 * ncs - 2 - cs) // ncs
        pl.semaphore_wait(barrier, beside)
    else:
        pl.semaphore_wait(barrier, ncs - 1 + nal - 1)
    launch(0)
    for load in loads[1:]:
        load.wait()

    w1 = w1_ref[...]
    w1t = jnp.transpose(jnp.concatenate([w1, jnp.zeros((96, 128), f32)], axis=0))[:, :32]
    w1th, w1tl = split(w1t)
    w1t_cat = jnp.concatenate([w1th, w1tl, w1th], axis=1)
    w1h, w1l = split(w1)
    w1_hh = jnp.concatenate([w1h, w1h], axis=1)
    w2 = w2_ref[...]
    w2h, w2l = split(w2)
    w2_hh = jnp.concatenate([w2h, w2h], axis=1)
    w2th, w2tl = split(jnp.transpose(w2))
    w2t_hh = jnp.concatenate([w2th, w2th], axis=1)
    b1b_ref[...] = jnp.transpose(jnp.broadcast_to(b1_ref[...], (128, 128)))
    b2b_ref[...] = jnp.transpose(jnp.broadcast_to(b2_ref[...], (128, 128)))
    cid = cid_ref[...]
    wo = wo_ref[...]
    wo_t = jnp.transpose(jnp.concatenate([wo, jnp.zeros((120, 128), f32)], axis=0))[:, :8]
    for r in range(8):
        onehot = (lax.broadcasted_iota(jnp.int32, (8, 128), 0) == cid[r:r + 1, :]).astype(f32)
        wsel_ref[:, r * 128:(r + 1) * 128] = lax.dot_general(
            wo_t, onehot, (((1,), (0,)), ((), ())),
            precision=lax.Precision.HIGHEST, preferred_element_type=f32,
        )
    bsel = jnp.zeros((8, 128), f32)
    for k in range(8):
        bsel = jnp.where(cid == k, bo_ref[0:1, k:k + 1], bsel)
    for f in range(12):
        feat_ref[(20 + f) * 8:(21 + f) * 8, :] = storm_ref[f]
    wets = [wet_ref[t].astype(f32) for t in range(2)]
    wash = [1.0 - dune_ref[t].astype(f32) for t in range(2)]

    def forward(t, V, k):
        near = []
        for f in range(12):
            n, s = north_of(V[f], f, k), south_of(V[f], f, k)
            w, e = west_of(V[f], f, k), east_of(V[f], f, k)
            near.append((n, s, w, e))
            if f < 4:
                feat_ref[f * 8:(f + 1) * 8, :] = V[f]
                feat_ref[(4 + f) * 8:(5 + f) * 8, :] = n
                feat_ref[(8 + f) * 8:(9 + f) * 8, :] = s
                feat_ref[(12 + f) * 8:(13 + f) * 8, :] = w
                feat_ref[(16 + f) * 8:(17 + f) * 8, :] = e
        for c in range(CHUNKS):
            at = pl.ds(c * LANES, LANES)
            F = jnp.concatenate(
                [feat_ref[pl.ds(2 * c + i, 32, stride=8), :] for i in range(2)], axis=1
            )
            Fh, Fl = split(F)
            fh_ref[t, :, at] = Fh
            fl_ref[t, :, at] = Fl
            v = mm(w1t_cat, jnp.concatenate([Fh, Fh, Fl], axis=0))
            bias = b1b_ref[...]
            v = v + jnp.concatenate([bias, bias], axis=1)
            sig = 0.5 + 0.5 * jnp.tanh(0.5 * v)
            h = v * sig
            act1_ref[t, :, at] = sig + h * (1.0 - sig)
            Hh, Hl = split(h)
            h1h_ref[t, :, at] = Hh
            h1l_ref[t, :, at] = Hl
            v = mm(w2t_hh, jnp.concatenate([Hh, Hl], axis=0)) + mm(w2tl, Hh)
            bias = b2b_ref[...]
            v = v + jnp.concatenate([bias, bias], axis=1)
            sig = 0.5 + 0.5 * jnp.tanh(0.5 * v)
            h = v * sig
            wsel = wsel_ref[:, at]
            q2_ref[t, :, at] = wsel * (sig + h * (1.0 - sig))
            z = jnp.sum(wsel * h, axis=0, keepdims=True)
            Hh, Hl = split(h)
            h2h_ref[t, :, at] = Hh
            h2l_ref[t, :, at] = Hl
            for i in range(2):
                z_ref[2 * c + i:2 * c + i + 1, :] = z[:, i * 128:(i + 1) * 128]
        return near, z_ref[...] + bsel

    def adjoint_two(t, z, lam):
        G = [wets[t] * lam[f] for f in range(12)]
        picked = G[4]
        for k in range(1, 8):
            picked = jnp.where(cid == k, G[4 + k], picked)
        gate = 1.0 / (1.0 + jnp.exp(-z))
        dz = pickup_gain * (picked - G[3]) * wash[t] * gate
        dz_ref[...] = dz
        for c in range(CHUNKS):
            at = pl.ds(c * LANES, LANES)
            drow = jnp.concatenate(
                [dz_ref[2 * c + i:2 * c + i + 1, :] for i in range(2)], axis=1
            )
            Dh, Dl = split(q2_ref[t, :, at] * drow)
            d2h_ref[t, :, at] = Dh
            d2l_ref[t, :, at] = Dl
        return G, dz

    def adjoint_one(t):
        for c in range(CHUNKS):
            at = pl.ds(c * LANES, LANES)
            Dh, Dl = d2h_ref[t, :, at], d2l_ref[t, :, at]
            d1 = mm(w2_hh, jnp.concatenate([Dh, Dl], axis=0)) + mm(w2l, Dh)
            Dh, Dl = split(d1 * act1_ref[t, :, at])
            d1h_ref[t, :, at] = Dh
            d1l_ref[t, :, at] = Dl

    def adjoint_cells(t, G, near, V, lam):
        for c in range(CHUNKS):
            at = pl.ds(c * LANES, LANES)
            Dh, Dl = d1h_ref[t, :, at], d1l_ref[t, :, at]
            dF = mm(w1_hh, jnp.concatenate([Dh, Dl], axis=0)) + mm(w1l, Dh)
            for i in range(2):
                dfeat_ref[pl.ds(2 * c + i, 32, stride=8), :] = dF[:, i * 128:(i + 1) * 128]
        D = [dfeat_ref[f * 8:(f + 1) * 8, :] for f in range(20)]
        lap = [bed_diffusion if f == 3 else diffusion for f in range(12)]
        lg = [lap[f] * G[f] for f in range(12)]
        c = [lam[f] - 4.0 * lg[f] for f in range(12)]
        alongs = jnp.zeros((8, 128), f32)
        crosses = jnp.zeros((8, 128), f32)
        along_part = [advection * G[1], advection * G[0], None, None]
        cross_part = [advection * G[2], None, advection * G[0], None]
        for k in range(8):
            n, s, w, e = near[4 + k]
            alongs = alongs + (s - n) * G[4 + k]
            crosses = crosses + (e - w) * G[4 + k]
            c[4 + k] = c[4 + k] + settling * (G[3] - G[4 + k])
            ag = advection * G[4 + k]
            along_part.append(V[1] * ag)
            cross_part.append(V[2] * ag)
        c[1] = c[1] - friction * G[1] - advection * alongs
        c[2] = c[2] - friction * G[2] - advection * crosses
        to = [[], [], [], []]
        for f in range(12):
            for d, part, sign in ((0, along_part, 1), (1, along_part, -1), (2, cross_part, 1), (3, cross_part, -1)):
                x = lg[f]
                if part[f] is not None:
                    x = x + part[f] if sign > 0 else x - part[f]
                if f < 4:
                    x = x + D[4 + 4 * d + f]
                to[d].append(x)
            if f < 4:
                c[f] = c[f] + D[f]
        return c, to

    def gather(c, to, k):
        return [
            c[f] + south_of(to[0][f], f, k) + north_of(to[1][f], f, k)
            + east_of(to[2][f], f, k) + west_of(to[3][f], f, k)
            for f in range(12)
        ]

    def keep(ref, start, part, first):
        at = pl.ds(start, part.shape[0])
        ref[at, :] = part if first else ref[at, :] + part

    def weights_two(t, dz, first):
        chooser_rows = []
        for r in range(8):
            onehot = lax.broadcasted_iota(jnp.int32, (8, 128), 0) == cid[r:r + 1, :]
            chooser_rows.append(jnp.where(onehot, dz[r:r + 1, :], 0.0))
        dr = jnp.concatenate(chooser_rows, axis=1)
        dbo = jnp.broadcast_to(jnp.sum(dr, axis=1, keepdims=True), (8, 128))
        pad = jnp.zeros((8, 1024), f32)
        drh, drl = split(jnp.concatenate([dr, pad], axis=0))
        top = mm_nt(jnp.concatenate([drh, drl], axis=0), h2h_ref[t])
        dwo = top[:8] + top[16:24] + mm_nt(drh, h2l_ref[t])[:8]
        lhs = jnp.concatenate([h1h_ref[t], jnp.ones((16, 1024), bf16), h1l_ref[t]], axis=0)
        top = mm_nt(lhs, d2h_ref[t])
        low = mm_nt(lhs[:144], d2l_ref[t])
        keep(acc_two, 0, top[:128] + top[144:272] + low[:128], first)
        keep(acc_two, ROW_B2, top[128:136] + low[128:136], first)
        keep(acc_two, ROW_WO, dwo, first)
        keep(acc_two, ROW_BO, dbo, first)

    def weights_one(t, first):
        lhs = jnp.concatenate([fh_ref[t], jnp.ones((16, 1024), bf16), fl_ref[t]], axis=0)
        top = mm_nt(lhs, d1h_ref[t])
        low = mm_nt(lhs[:48], d1l_ref[t])
        keep(acc_one, 0, top[:32] + top[48:80] + low[:32], first)
        keep(acc_one, ROW_B1, top[32:40] + low[32:40], first)

    finish(0)
    near0, z0 = forward(0, V0, 0)
    soft = jnp.maximum(z0, 0.0) + jnp.log(1.0 + jnp.exp(-jnp.abs(z0)))
    pickup = soft * wash[0]
    V1 = []
    lap = []
    for f in range(12):
        n, s, w, e = near0[f]
        lap.append(n + s + w + e - 4.0 * V0[f])
    total = V0[4]
    for k in range(1, 8):
        total = total + V0[4 + k]
    ad = [near0[f][1] - near0[f][0] for f in range(12)]
    cd = [near0[f][3] - near0[f][2] for f in range(12)]
    tend = [
        diffusion * lap[0] - advection * (ad[1] + cd[2]),
        diffusion * lap[1] - advection * ad[0] - friction * V0[1],
        diffusion * lap[2] - advection * cd[0] - friction * V0[2],
        bed_diffusion * lap[3] - pickup_gain * pickup + settling * total,
    ]
    for k in range(8):
        x = diffusion * lap[4 + k] - advection * (V0[1] * ad[4 + k] + V0[2] * cd[4 + k])
        x = x + jnp.where(cid == k, pickup_gain * pickup, 0.0) - settling * V0[4 + k]
        tend.append(x)
    V1 = [V0[f] + wets[0] * tend[f] for f in range(12)]
    fill(1, V1, V1, V1, V1)
    launch(1)
    finish(1)

    near1, z1 = forward(1, V1, 1)
    lam2 = [cot_ref[f] for f in range(12)]
    G1, dz1 = adjoint_two(1, z1, lam2)
    adjoint_one(1)
    c1, to1 = adjoint_cells(1, G1, near1, V1, lam2)
    fill(2, *to1)
    launch(2)
    for ref, used in ((acc_one, ROWS_ONE), (acc_two, ROWS_TWO)):
        if ref.shape[0] > used:
            ref[used:, :] = jnp.zeros((ref.shape[0] - used, 128), f32)
    weights_two(1, dz1, True)
    weights_one(1, True)
    finish(2)
    lam1 = gather(c1, to1, 2)

    class Sum:
        def __init__(self, which, acc, rcv_a, src_b, rcv_b, full):
            self.which, self.acc, self.rcv_a, self.src_b = which, acc, rcv_a, src_b
            self.rcv_b, self.full = rcv_b, full
            self.rows = src_b.shape[0]
            self.mine = pl.ds(pl.multiple_of(cs * self.rows, 8), self.rows)

        def copy_a(self, j):
            peer = lax.rem(cs + j, ncs)
            return pltpu.make_async_remote_copy(
                src_ref=self.acc.at[pl.ds(pl.multiple_of(peer * self.rows, 8), self.rows), :],
                dst_ref=self.rcv_a.at[j],
                send_sem=sa_send.at[self.which, j], recv_sem=sa_recv.at[self.which, j],
                device_id=dev(al, peer), device_id_type=MESH,
            )

        def copy_b(self, j):
            return pltpu.make_async_remote_copy(
                src_ref=self.src_b, dst_ref=self.rcv_b.at[al],
                send_sem=sb_send.at[self.which, j], recv_sem=sb_recv.at[self.which, j],
                device_id=dev(lax.rem(al + j, nal), cs), device_id_type=MESH,
            )

        def copy_c(self, j):
            return pltpu.make_async_remote_copy(
                src_ref=self.full.at[self.mine, :], dst_ref=self.full.at[self.mine, :],
                send_sem=sc_send.at[self.which, j], recv_sem=sc_recv.at[self.which, j],
                device_id=dev(al, lax.rem(cs + j, ncs)), device_id_type=MESH,
            )

        def first(self):
            for j in range(1, ncs):
                self.copy_a(j).start()

        def second(self):
            total = self.acc[self.mine, :]
            for j in range(1, ncs):
                self.copy_a(j).wait_recv()
                total = total + self.rcv_a[j]
            self.src_b[...] = total
            self.rcv_b[al] = total
            for j in range(1, nal):
                self.copy_b(j).start()

        def third(self):
            for j in range(1, nal):
                self.copy_b(j).wait_recv()
            total = self.rcv_b[0]
            for j in range(1, nal):
                total = total + self.rcv_b[j]
            self.full[self.mine, :] = total * factor
            for j in range(1, ncs):
                self.copy_c(j).start()

        def fourth(self):
            for j in range(1, ncs):
                self.copy_c(j).wait_recv()

        def sends(self):
            for j in range(1, ncs):
                self.copy_a(j).wait_send()
                self.copy_c(j).wait_send()
            for j in range(1, nal):
                self.copy_b(j).wait_send()

    sum_two = Sum(0, acc_two, rcv_a_two, src_b_two, rcv_b_two, dst_two)
    sum_one = Sum(1, acc_one, rcv_a_one, src_b_one, rcv_b_one, dst_one)

    G0, dz0 = adjoint_two(0, z0, lam1)
    weights_two(0, dz0, False)
    sum_two.first()
    adjoint_one(0)
    weights_one(0, False)
    sum_one.first()
    c0, to0 = adjoint_cells(0, G0, near0, V0, lam1)
    fill(3, *to0)
    launch(3)
    sum_two.second()
    sum_one.second()
    finish(3)
    last = gather(c0, to0, 3)
    for f in range(12):
        gstate_ref[f] = last[f]
    sum_two.third()
    sum_one.third()
    sum_two.fourth()
    sum_one.fourth()
    for k in range(4):
        finish_sends(k)
    sum_two.sends()
    sum_one.sends()


def unpack(
    state_ref, one_ref, two_ref,
    gs_hbm, gw1_hbm, gb1_hbm, gw2_hbm, gb2_hbm, gwo_hbm, gbo_hbm, gbo_ref, sem,
):
    wide = jnp.concatenate([two_ref[ROW_BO:ROW_BO + 8, :], jnp.zeros((120, 128), f32)], axis=0)
    pairs = (
        (two_ref.at[0:128], gw2_hbm), (state_ref, gs_hbm), (one_ref.at[0:32], gw1_hbm),
        (two_ref.at[ROW_WO:ROW_WO + 8], gwo_hbm), (one_ref.at[ROW_B1:ROW_B1 + 1], gb1_hbm),
        (two_ref.at[ROW_B2:ROW_B2 + 1], gb2_hbm), (gbo_ref, gbo_hbm),
    )
    copies = [pltpu.make_async_copy(src, dst, sem.at[i]) for i, (src, dst) in enumerate(pairs)]
    for copy in copies[:6]:
        copy.start()
    gbo_ref[...] = jnp.transpose(wide)[0:1, :8]
    copies[6].start()
    for copy in copies:
        copy.wait()


def solution(mesh):
    nal, ncr, nsu = mesh.shape["along"], mesh.shape["cross"], mesh.shape["sub"]
    ncs = ncr * nsu
    rows_one = 8 * (-(-ROWS_ONE // (8 * ncs)))
    rows_two = 8 * (-(-ROWS_TWO // (8 * ncs)))

    def per_device(state, storm, wet, dune, cid, w1, b1, w2, b2, wo, bo, cot):
        rows, cols = state.shape[1], state.shape[2]
        factor = 1.0 / math.sqrt(rows * nal * cols * ncs)
        vmem = pl.BlockSpec(memory_space=pltpu.VMEM)
        hbm = pl.BlockSpec(memory_space=pl.ANY)
        operands = (
            state, cid, w1, b1.reshape(1, 128), w2, b2.reshape(1, 128), wo.T, bo.reshape(1, 8),
            storm, wet, dune, cot,
        )
        dma = pltpu.SemaphoreType.DMA
        big = lambda n, kind: pltpu.VMEM((2, n, 1024), kind)
        summed = lambda n: [
            pltpu.VMEM((ncs * n, 128), f32),
            pltpu.VMEM((ncs, n, 128), f32),
            pltpu.VMEM((n, 128), f32),
            pltpu.VMEM((nal, n, 128), f32),
        ]
        out = pl.pallas_call(
            functools.partial(kernel, nal, ncr, nsu, factor),
            out_shape=(
                pltpu.VMEM((12, 8, 128), f32),
                pltpu.VMEM((ncs * rows_one, 128), f32),
                pltpu.VMEM((ncs * rows_two, 128), f32),
            ),
            in_specs=[hbm] * 12,
            out_specs=(vmem,) * 3,
            scratch_shapes=[
                *[pltpu.VMEM(x.shape, x.dtype) for x in operands],
                dma((12,)),
                pltpu.VMEM((4, 2, 16, 128), f32),
                pltpu.VMEM((4, 2, 8, 128), f32),
                pltpu.VMEM((4, 2, 16, 128), f32),
                pltpu.VMEM((4, 2, 8, 128), f32),
                dma((4, 4)), dma((4, 4)),
                pltpu.VMEM((256, 128), f32),
                pltpu.VMEM((256, 128), f32),
                pltpu.VMEM((8, 128), f32),
                pltpu.VMEM((8, 128), f32),
                pltpu.VMEM((128, 128), f32),
                pltpu.VMEM((128, 128), f32),
                pltpu.VMEM((128, 1024), f32),
                big(32, bf16), big(32, bf16), big(128, bf16), big(128, bf16), big(128, bf16), big(128, bf16),
                big(128, f32), big(128, f32), big(128, bf16), big(128, bf16), big(128, bf16), big(128, bf16),
                pltpu.VMEM((16, 1024), bf16), pltpu.VMEM((16, 1024), bf16),
                *summed(rows_one), *summed(rows_two),
                dma((2, ncs)), dma((2, ncs)), dma((2, nal)), dma((2, nal)), dma((2, ncs)), dma((2, ncs)),
            ],
            compiler_params=pltpu.CompilerParams(collective_id=0, has_side_effects=True),
        )(*operands)
        gs, gw1, gb1, gw2, gb2, gwo, gbo = pl.pallas_call(
            unpack,
            out_shape=(
                jax.ShapeDtypeStruct((12, 8, 128), f32),
                jax.ShapeDtypeStruct((32, 128), f32),
                jax.ShapeDtypeStruct((1, 128), f32),
                jax.ShapeDtypeStruct((128, 128), f32),
                jax.ShapeDtypeStruct((1, 128), f32),
                jax.ShapeDtypeStruct((8, 128), f32),
                jax.ShapeDtypeStruct((1, 8), f32),
            ),
            in_specs=[vmem] * 3,
            out_specs=(hbm,) * 7,
            scratch_shapes=[pltpu.VMEM((1, 8), f32), dma((7,))],
        )(*[pltpu.with_memory_space_constraint(x, pltpu.VMEM) for x in out])
        return gs, gw1, gb1.reshape(128), gw2, gb2.reshape(128), gwo.T, gbo.reshape(8)

    tile = P(None, ("groups", "along"), ("cross", "sub"))
    return jax.shard_map(
        per_device,
        mesh=mesh,
        in_specs=(
            tile, tile, tile, tile, P(("groups", "along"), ("cross", "sub")),
            P(), P(), P(), P(), P(), P(), tile,
        ),
        out_specs=(
            tile, P("groups", None), P("groups"), P("groups", None), P("groups"),
            P("groups", None), P("groups"),
        ),
        check_vma=False,
    )
```

```python
import functools
import math

import jax
import jax.numpy as jnp
from jax import lax
from jax.experimental import pallas as pl
from jax.experimental.pallas import tpu as pltpu
from jax.sharding import PartitionSpec as P

MESH = pl.DeviceIdType.MESH
f32 = jnp.float32
bf16 = jnp.bfloat16
diffusion = 0.15
advection = 0.2
friction = 0.05
pickup_gain = 0.5
settling = 0.2
bed_diffusion = 0.1

ROW_W1 = 128
ROW_WO = 160
ROW_BIAS = 168
ROWS = 176
ROW_OF_UNIT = (1, 2, 3, 4, 5, 6, 0, 7)
INNER = 6
OWN = 8
STRIP = 8
NEXT = 16
STORM = 28
COL_STORM = 32
COL_MASK = 44


def split(x):
    high = x.astype(bf16)
    low = (x - high.astype(f32)).astype(bf16)
    return high, low


def mm(a, b):
    return lax.dot_general(a, b, (((1,), (0,)), ((), ())), preferred_element_type=f32)


def mm_nt(a, b):
    return lax.dot_general(a, b, (((1,), (1,)), ((), ())), preferred_element_type=f32)


def silu(v):
    sig = 0.5 + 0.5 * jnp.tanh(0.5 * v)
    return sig, v * sig


def softplus(z):
    return jnp.maximum(z, 0.0) + jnp.log(1.0 + jnp.exp(-jnp.abs(z)))


def kernel(
    nal, ncr, nsu, factor,
    state_hbm, cid_hbm, w1_hbm, b1_hbm, w2_hbm, b2_hbm, wo_hbm, bo_hbm,
    storm_hbm, wet_hbm, dune_hbm, cot_hbm,
    gstate_ref, full_ref,
    state_ref, cid_ref, w1_ref, b1_ref, w2_ref, b2_ref, wo_ref, bo_ref,
    storm_ref, wet_ref, dune_ref, cot_ref, load_sem,
    snd0_row, snd0_col, rcv0_row, rcv0_col, rcv_diag,
    snd_row, snd_col, rcv_row, rcv_col, ring_row, ring_col,
    edge_send, edge_recv, diag_send, diag_recv, relay_sem,
    feat_ref, dfeat_ref, fx_ref, z_ref, zx_ref, dz_ref, cidx_ref, wetx_ref, dunex_ref,
    b1b_ref, b2b_ref, wsel_ref,
    fh_ref, fl_ref, h1h_ref, h1l_ref, h2h_ref, h2l_ref,
    act1_ref, q2_ref, d1h_ref, d1l_ref, d2h_ref, d2l_ref,
    acc_ref, rcv_a, src_b, rcv_b,
    sum_send, sa_recv, sb_recv, sc_recv,
):
    ncs = ncr * nsu
    g = lax.axis_index("groups")
    al = lax.axis_index("along")
    cr = lax.axis_index("cross")
    su = lax.axis_index("sub")
    cs = cr * nsu + su

    def dev(a, c):
        return (g, a, c // nsu, c % nsu)

    has_dst = (al > 0, al < nal - 1, cs > 0, cs < ncs - 1)
    has_src = (al < nal - 1, al > 0, cs < ncs - 1, cs > 0)
    dst_dev = (
        dev(al - 1, cs), dev(al + 1, cs), dev(al, cs - 1), dev(al, cs + 1),
    )
    corners = ((0, 2), (0, 3), (1, 2), (1, 3))
    diag_dst = [jnp.logical_and(has_dst[a], has_dst[c]) for a, c in corners]
    diag_src = [jnp.logical_and(has_src[a], has_src[c]) for a, c in corners]
    diag_dev = [dev(al + (1 if a else -1), cs + (1 if c == 3 else -1)) for a, c in corners]

    loads = [
        pltpu.make_async_copy(src, dst, load_sem.at[i])
        for i, (src, dst) in enumerate((
            (state_hbm, state_ref), (storm_hbm, storm_ref), (wet_hbm, wet_ref), (dune_hbm, dune_ref),
            (cid_hbm, cid_ref), (w1_hbm, w1_ref), (b1_hbm, b1_ref), (w2_hbm, w2_ref),
            (b2_hbm, b2_ref), (wo_hbm, wo_ref), (bo_hbm, bo_ref), (cot_hbm, cot_ref),
        ))
    ]
    for load in loads[:5]:
        load.start()
    for ref in (rcv0_row, rcv0_col, rcv_diag, rcv_row, rcv_col):
        ref[...] = jnp.zeros_like(ref)

    barrier = pltpu.get_barrier_semaphore()
    near_only = nal <= 4 and ncs <= 4
    for e in range(4):
        @pl.when(diag_dst[e])
        def _():
            pl.semaphore_signal(barrier, inc=1, device_id=diag_dev[e], device_id_type=MESH)
    if near_only:
        for d in range(4):
            @pl.when(has_dst[d])
            def _():
                pl.semaphore_signal(barrier, inc=1, device_id=dst_dev[d], device_id_type=MESH)
    else:
        for j in range(1, ncs):
            pl.semaphore_signal(
                barrier, inc=1, device_id=dev(al, lax.rem(cs + j, ncs)), device_id_type=MESH
            )
        for j in range(1, nal):
            pl.semaphore_signal(
                barrier, inc=1, device_id=dev(lax.rem(al + j, nal), cs), device_id_type=MESH
            )
    for load in loads[5:]:
        load.start()
    beside_al = (al + nal - 1) // nal + (2 * nal - 2 - al) // nal
    beside_cs = (cs + ncs - 1) // ncs + (2 * ncs - 2 - cs) // ncs

    row = lax.broadcasted_iota(jnp.int32, (8, 128), 0)
    lane = lax.broadcasted_iota(jnp.int32, (8, 128), 1)
    field = lax.broadcasted_iota(jnp.int32, (16, 128), 0)
    lane16 = lax.broadcasted_iota(jnp.int32, (16, 128), 1)

    def turn(x, shift, axis):
        shift = shift % x.shape[axis]
        return pltpu.roll(x, shift, axis) if shift else x

    def copy0_of(d):
        src, dst = (snd0_row, rcv0_row) if d < 2 else (snd0_col, rcv0_col)
        return pltpu.make_async_remote_copy(
            src_ref=src.at[d % 2], dst_ref=dst.at[d % 2], send_sem=edge_send.at[d],
            recv_sem=edge_recv.at[0, d], device_id=dst_dev[d], device_id_type=MESH,
        )

    def diag_of(e):
        return pltpu.make_async_remote_copy(
            src_ref=snd0_row.at[e // 2, pl.ds(0, 16)], dst_ref=rcv_diag.at[e],
            send_sem=diag_send.at[e], recv_sem=diag_recv.at[e],
            device_id=diag_dev[e], device_id_type=MESH,
        )

    def copy_of(k, d):
        src, dst = (snd_row, rcv_row) if d < 2 else (snd_col, rcv_col)
        return pltpu.make_async_remote_copy(
            src_ref=src.at[k - 1, d % 2], dst_ref=dst.at[k - 1, d % 2], send_sem=edge_send.at[d],
            recv_sem=edge_recv.at[k % 2, d], device_id=dst_dev[d], device_id_type=MESH,
        )

    def each(flags, action):
        for i in range(4):
            @pl.when(flags[i])
            def _():
                action(i)

    def fill(k, xn, xs, xw, xe):
        west = jnp.zeros((8, 128), f32)
        east = jnp.zeros((8, 128), f32)
        for f in range(12):
            snd_row[k - 1, 0, f:f + 1, :] = xn[f][0:1, :]
            snd_row[k - 1, 1, f:f + 1, :] = xs[f][7:8, :]
            west = jnp.where(lane == f, turn(xw[f], f, 1), west)
            east = jnp.where(lane == f, turn(xe[f], f + 1, 1), east)
        snd_col[k - 1, 0] = west
        snd_col[k - 1, 1] = east

    class Halo:
        def __init__(self, rows, cols):
            self.rows, self.cols = rows, cols

        def south(self, x, f):
            return jnp.where(row == 7, self.rows[0, f:f + 1, :], turn(x, 7, 0))

        def north(self, x, f):
            return jnp.where(row == 0, self.rows[1, f:f + 1, :], turn(x, 1, 0))

        def east(self, x, f):
            return jnp.where(lane == 127, turn(self.cols[0], 127 - f, 1), turn(x, 127, 1))

        def west(self, x, f):
            return jnp.where(lane == 0, turn(self.cols[1], -f, 1), turn(x, 1, 1))

        def around(self, x, f):
            return self.north(x, f), self.south(x, f), self.west(x, f), self.east(x, f)

    for load in loads[:5]:
        load.wait()
    V0 = [state_ref[f * 8:(f + 1) * 8, :] for f in range(12)]
    storm = [storm_ref[f * 8:(f + 1) * 8, :] for f in range(12)]
    wets = [wet_ref[t * 8:(t + 1) * 8, :].astype(f32) for t in range(2)]
    dunes = [dune_ref[t * 8:(t + 1) * 8, :].astype(f32) for t in range(2)]
    wash = [1.0 - dunes[t] for t in range(2)]
    cid = cid_ref[...]
    masks = [wets[0], dunes[0], cid.astype(f32)]
    for d, edge, inner in ((0, 0, 1), (1, 7, 6)):
        for f in range(12):
            snd0_row[d, f:f + 1, :] = V0[f][edge:edge + 1, :]
            snd0_row[d, NEXT + f:NEXT + f + 1, :] = V0[f][inner:inner + 1, :]
            snd0_row[d, STORM + f:STORM + f + 1, :] = storm[f][edge:edge + 1, :]
        for m in range(3):
            snd0_row[d, 12 + m:13 + m, :] = masks[m][edge:edge + 1, :]
        snd0_row[d, 15:16, :] = jnp.zeros((1, 128), f32)
    for d, edge, inner in ((0, 0, 1), (1, 127, 126)):
        out = jnp.zeros((8, 128), f32)
        for x, at, c in (
            [(V0[f], f, edge) for f in range(12)] + [(V0[f], NEXT + f, inner) for f in range(12)]
            + [(storm[f], COL_STORM + f, edge) for f in range(12)]
            + [(masks[m], COL_MASK + m, edge) for m in range(3)]
        ):
            out = jnp.where(lane == at, turn(x, at - c, 1), out)
        snd0_col[d] = out
    if near_only:
        pl.semaphore_wait(barrier, beside_al + beside_cs + beside_al * beside_cs)
    else:
        pl.semaphore_wait(barrier, ncs - 1 + nal - 1 + beside_al * beside_cs)
    each(has_dst, lambda d: copy0_of(d).start())
    each(diag_dst, lambda e: diag_of(e).start())
    for load in loads[5:]:
        load.wait()

    w1 = w1_ref[...]
    w1t = jnp.transpose(jnp.concatenate([w1, jnp.zeros((96, 128), f32)], axis=0))[:, :32]
    w1th, w1tl = split(w1t)
    w1t_cat = jnp.concatenate([w1th, w1tl, w1th], axis=1)
    w1h, w1l = split(w1)
    w1_hh = jnp.concatenate([w1h, w1h], axis=1)
    w2 = w2_ref[...]
    w2h, w2l = split(w2)
    w2_hh = jnp.concatenate([w2h, w2h], axis=1)
    w2th, w2tl = split(jnp.transpose(w2))
    w2t_hh = jnp.concatenate([w2th, w2th], axis=1)
    b1b_ref[...] = jnp.transpose(jnp.broadcast_to(b1_ref[...], (128, 128)))
    b2b_ref[...] = jnp.transpose(jnp.broadcast_to(b2_ref[...], (128, 128)))
    wo_t = jnp.transpose(jnp.concatenate([wo_ref[...], jnp.zeros((120, 128), f32)], axis=0))[:, :8]

    def choose(unit, ids):
        onehot = (row == ids).astype(f32)
        wsel_ref[:, unit * 128:(unit + 1) * 128] = lax.dot_general(
            wo_t, onehot, (((1,), (0,)), ((), ())),
            precision=lax.Precision.HIGHEST, preferred_element_type=f32,
        )

    def bias_of(ids):
        b = jnp.zeros((8, 128), f32)
        for k in range(8):
            b = jnp.where(ids == k, bo_ref[0:1, k:k + 1], b)
        return b

    for u in range(OWN):
        choose(u, cid[ROW_OF_UNIT[u]:ROW_OF_UNIT[u] + 1, :])
    bsel = bias_of(cid)

    def twice(x, n):
        return jnp.concatenate([x] * n, axis=1) if n > 1 else x

    def layers(t, unit, feats, kept):
        n = len(feats)
        at = pl.ds(unit * 128, n * 128)
        F = jnp.concatenate(feats, axis=1) if n > 1 else feats[0]
        Fh, Fl = split(F)
        v = mm(w1t_cat, jnp.concatenate([Fh, Fh, Fl], axis=0)) + twice(b1b_ref[...], n)
        sig, h = silu(v)
        Hh, Hl = split(h)
        if kept:
            fh_ref[t, :, at] = Fh
            fl_ref[t, :, at] = Fl
            act1_ref[t, :, at] = sig + h * (1.0 - sig)
            h1h_ref[t, :, at] = Hh
            h1l_ref[t, :, at] = Hl
        v = mm(w2t_hh, jnp.concatenate([Hh, Hl], axis=0)) + mm(w2tl, Hh) + twice(b2b_ref[...], n)
        sig, h = silu(v)
        wsel = wsel_ref[:, at]
        if kept:
            q2_ref[t, :, at] = wsel * (sig + h * (1.0 - sig))
            Hh, Hl = split(h)
            h2h_ref[t, :, at] = Hh
            h2l_ref[t, :, at] = Hl
        z = jnp.sum(wsel * h, axis=0, keepdims=True)
        return [z[:, i * 128:(i + 1) * 128] for i in range(n)]

    def put_features(V, near):
        for f in range(4):
            for part, x in enumerate((V[f],) + tuple(near[f])):
                feat_ref[(4 * part + f) * 8:(4 * part + f + 1) * 8, :] = x

    def own_layers(t, first, last):
        for u in range(first, last, 2):
            rows = ROW_OF_UNIT[u:u + 2]
            feats = [feat_ref[pl.ds(r, 32, stride=8), :] for r in rows]
            for r, z in zip(rows, layers(t, u, feats, True)):
                z_ref[r:r + 1, :] = z

    feat_ref[160:256, :] = storm_ref[...]
    put_features(V0, [
        (turn(V0[f], 1, 0), turn(V0[f], 7, 0), turn(V0[f], 1, 1), turn(V0[f], 127, 1)) for f in range(4)
    ])
    own_layers(0, 0, INNER)
    for ref in (zx_ref, cidx_ref, wetx_ref, dunex_ref):
        ref[...] = jnp.zeros_like(ref)
    spare = acc_ref.shape[0] - ROWS
    if spare:
        acc_ref[ROWS:, :] = jnp.zeros((spare, 128), f32)

    each(has_src, lambda d: copy0_of(d).wait_recv())
    each(diag_src, lambda e: diag_of(e).wait_recv())
    if near_only:
        each(has_dst, lambda d: pl.semaphore_signal(
            relay_sem, inc=1, device_id=dst_dev[d], device_id_type=MESH))

    halo0 = Halo(rcv0_row, rcv0_col)
    near0 = [halo0.around(V0[f], f) for f in range(12)]
    put_features(V0, near0)
    sides = jnp.concatenate(
        [rcv0_col[1], rcv0_col[0], snd0_col[0], snd0_col[1], jnp.zeros((96, 128), f32)], axis=0
    )
    T = jnp.transpose(sides)
    SE, SW, NE, NW = [rcv_diag[e] for e in range(4)]
    RS, RN = rcv0_row[0, 0:16, :], rcv0_row[1, 0:16, :]
    group = lane16 // 8
    V, far = T[0:16], T[NEXT:NEXT + 16]
    plus, minus = turn(V, 16, 1), turn(V, -16, 1)
    N, S = turn(V, 1, 1), turn(V, -1, 1)
    for at, x, c in ((0, NW, 127), (8, NE, 0), (16, RN, 0), (24, RN, 127)):
        N = jnp.where(lane16 == at, turn(x, at - c, 1), N)
    for at, x, c in ((7, SW, 127), (15, SE, 0), (23, RS, 0), (31, RS, 127)):
        S = jnp.where(lane16 == at, turn(x, at - c, 1), S)
    W = jnp.where(group == 1, minus, jnp.where(group == 2, plus, far))
    E = jnp.where(group == 0, minus, jnp.where(group == 3, plus, far))
    outer = [(V, N, S, W, E)]
    for V, N, S, west, east in (
        (RN, rcv0_row[1, NEXT:NEXT + 16, :], snd0_row[0, 0:16, :], NW, NE),
        (RS, snd0_row[1, 0:16, :], rcv0_row[0, NEXT:NEXT + 16, :], SW, SE),
    ):
        W = jnp.where(lane16 == 0, turn(west, 1, 1), turn(V, 1, 1))
        E = jnp.where(lane16 == 127, turn(east, 127, 1), turn(V, 127, 1))
        outer.append((V, N, S, W, E))
    storms = [T[COL_STORM:COL_STORM + 12], rcv0_row[1, STORM:STORM + 12, :], rcv0_row[0, STORM:STORM + 12, :]]
    mask_rows = [
        [T[COL_MASK + m:COL_MASK + m + 1] for m in range(3)],
        [rcv0_row[1, 12 + m:13 + m, :] for m in range(3)],
        [rcv0_row[0, 12 + m:13 + m, :] for m in range(3)],
    ]
    for w in range(3):
        for part in range(5):
            fx_ref[w, 4 * part:4 * part + 4, :] = outer[w][part][0:4]
        fx_ref[w, 20:32, :] = storms[w]
        wetx_ref[w:w + 1, :] = mask_rows[w][0]
        dunex_ref[w:w + 1, :] = mask_rows[w][1]
        ids = mask_rows[w][2].astype(jnp.int32)
        cidx_ref[w:w + 1, :] = ids
        choose(STRIP + w, ids)
    cidx = cidx_ref[...]
    own_layers(0, INNER, OWN)
    zx_ref[0:1, :] = layers(0, STRIP, [fx_ref[0]], True)[0]
    zx_ref[1:2, :], zx_ref[2:3, :] = layers(0, STRIP + 1, [fx_ref[1], fx_ref[2]], False)
    zx = zx_ref[...] + bias_of(cidx)
    pickx = pickup_gain * softplus(zx) * (1.0 - dunex_ref[...])

    def from_strip(x, start):
        return jnp.sum(jnp.where(lane == start + row, x, 0.0), axis=1, keepdims=True)

    inside = jnp.logical_and(row > 0, row < 7)
    at_west = jnp.logical_and(inside, lane == 0)
    at_east = jnp.logical_and(inside, lane == 127)
    z0 = z_ref[...] + bsel
    z0 = jnp.where(at_west, from_strip(zx[0:1, :], 16), z0)
    z0 = jnp.where(at_east, from_strip(zx[0:1, :], 24), z0)

    def advanced(w):
        V, N, S, W, E = outer[w]
        pick, wet = pickx[w:w + 1, :], wetx_ref[w:w + 1, :]
        lap = N + S + W + E - 4.0 * V
        ad, cd = S - N, E - W
        spread = jnp.where(field == 3, bed_diffusion, diffusion) * lap
        sediment = spread - advection * (V[1:2] * ad + V[2:3] * cd) - settling * V
        sediment = sediment + jnp.where(field - 4 == cidx[w:w + 1, :], pick, 0.0)
        total = jnp.sum(
            jnp.where(jnp.logical_and(field >= 4, field < 12), V, 0.0), axis=0, keepdims=True
        )
        first = jnp.where(field == 0, -advection * (ad[1:2] + cd[2:3]), settling * total - pick)
        first = jnp.where(field == 1, -advection * ad[0:1] - friction * V[1:2], first)
        first = jnp.where(field == 2, -advection * cd[0:1] - friction * V[2:3], first)
        return V + wet * jnp.where(field < 4, spread + first, sediment)

    ring_row[1] = advanced(1)
    ring_row[0] = advanced(2)
    back = jnp.transpose(jnp.concatenate([advanced(0), jnp.zeros((112, 128), f32)], axis=0))
    ring_col[1] = back[0:8]
    ring_col[0] = back[8:16]

    pickup = softplus(z0) * wash[0]
    lap = []
    for f in range(12):
        n, s, w, e = near0[f]
        lap.append(n + s + w + e - 4.0 * V0[f])
    total = V0[4]
    for k in range(1, 8):
        total = total + V0[4 + k]
    ad = [near0[f][1] - near0[f][0] for f in range(12)]
    cd = [near0[f][3] - near0[f][2] for f in range(12)]
    tend = [
        diffusion * lap[0] - advection * (ad[1] + cd[2]),
        diffusion * lap[1] - advection * ad[0] - friction * V0[1],
        diffusion * lap[2] - advection * cd[0] - friction * V0[2],
        bed_diffusion * lap[3] - pickup_gain * pickup + settling * total,
    ]
    for k in range(8):
        x = diffusion * lap[4 + k] - advection * (V0[1] * ad[4 + k] + V0[2] * cd[4 + k])
        x = x + jnp.where(cid == k, pickup_gain * pickup, 0.0) - settling * V0[4 + k]
        tend.append(x)
    V1 = [V0[f] + wets[0] * tend[f] for f in range(12)]

    halo1 = Halo(ring_row, ring_col)
    near1 = [halo1.around(V1[f], f) for f in range(12)]
    put_features(V1, near1)
    own_layers(1, 0, OWN)
    z1 = z_ref[...] + bsel
    lam2 = [cot_ref[f * 8:(f + 1) * 8, :] for f in range(12)]

    def closure_cotangent(t, gate, lam):
        G = [None] * 3 + [wets[t] * lam[f] for f in range(3, 12)]
        picked = G[4]
        for k in range(1, 8):
            picked = jnp.where(cid == k, G[4 + k], picked)
        return pickup_gain * (picked - G[3]) * wash[t] * gate

    def sigmoid(z):
        return 1.0 / (1.0 + jnp.exp(-z))

    def pairs(units):
        return [units[i:i + 2] for i in range(0, len(units), 2)]

    def adjoint_two(t, units, drows):
        for part in pairs(list(zip(units, drows))):
            at = pl.ds(part[0][0] * 128, len(part) * 128)
            drow = jnp.concatenate([d for _, d in part], axis=1)
            Dh, Dl = split(q2_ref[t, :, at] * drow)
            d2h_ref[t, :, at] = Dh
            d2l_ref[t, :, at] = Dl

    def adjoint_one(t, units):
        for part in pairs(units):
            at = pl.ds(part[0] * 128, len(part) * 128)
            Dh, Dl = d2h_ref[t, :, at], d2l_ref[t, :, at]
            d1 = mm(w2_hh, jnp.concatenate([Dh, Dl], axis=0)) + mm(w2l, Dh)
            Dh, Dl = split(d1 * act1_ref[t, :, at])
            d1h_ref[t, :, at] = Dh
            d1l_ref[t, :, at] = Dl

    def feature_cotangent(t, units):
        out = []
        for part in pairs(units):
            at = pl.ds(part[0] * 128, len(part) * 128)
            Dh, Dl = d1h_ref[t, :, at], d1l_ref[t, :, at]
            dF = mm(w1_hh, jnp.concatenate([Dh, Dl], axis=0)) + mm(w1l, Dh)
            for i, u in enumerate(part):
                one = dF[:, i * 128:(i + 1) * 128]
                if u < OWN:
                    dfeat_ref[pl.ds(ROW_OF_UNIT[u], 32, stride=8), :] = one
                else:
                    out.append(one)
        return out

    def adjoint_cells(D, G, near, V, lam):
        lap = [bed_diffusion if f == 3 else diffusion for f in range(12)]
        lg = [lap[f] * G[f] for f in range(12)]
        c = [lam[f] - 4.0 * lg[f] for f in range(12)]
        alongs = jnp.zeros((8, 128), f32)
        crosses = jnp.zeros((8, 128), f32)
        along_part = [advection * G[1], advection * G[0], None, None]
        cross_part = [advection * G[2], None, advection * G[0], None]
        for k in range(8):
            n, s, w, e = near[4 + k]
            alongs = alongs + (s - n) * G[4 + k]
            crosses = crosses + (e - w) * G[4 + k]
            c[4 + k] = c[4 + k] + settling * (G[3] - G[4 + k])
            ag = advection * G[4 + k]
            along_part.append(V[1] * ag)
            cross_part.append(V[2] * ag)
        c[1] = c[1] - friction * G[1] - advection * alongs
        c[2] = c[2] - friction * G[2] - advection * crosses
        to = [[], [], [], []]
        for f in range(12):
            for d, part, sign in ((0, along_part, 1), (1, along_part, -1), (2, cross_part, 1), (3, cross_part, -1)):
                x = lg[f]
                if part[f] is not None:
                    x = x + part[f] if sign > 0 else x - part[f]
                if f < 4:
                    x = x + D[4 + 4 * d + f]
                to[d].append(x)
            if f < 4:
                c[f] = c[f] + D[f]
        return c, to

    def gather(c, to, halo):
        return [
            c[f] + halo.south(to[0][f], f) + halo.north(to[1][f], f)
            + halo.east(to[2][f], f) + halo.west(to[3][f], f)
            for f in range(12)
        ]

    def keep(start, part, first):
        at = pl.ds(start, part.shape[0])
        acc_ref[at, :] = part if first else acc_ref[at, :] + part

    def weights_two(t, units, ids, drows, first):
        at = pl.ds(units[0] * 128, len(units) * 128)
        width = len(units) * 128
        dr = jnp.concatenate(
            [jnp.where(row == k, d, 0.0) for k, d in zip(ids, drows)], axis=1
        )
        dbo = jnp.sum(
            jnp.where(row == lane, jnp.sum(dr, axis=1, keepdims=True), 0.0), axis=0, keepdims=True
        )
        drh, drl = split(jnp.concatenate([dr, jnp.zeros((8, width), f32)], axis=0))
        top = mm_nt(jnp.concatenate([drh, drl], axis=0), h2h_ref[t, :, at])
        dwo = top[:8] + top[16:24] + mm_nt(drh, h2l_ref[t, :, at])[:8]
        lhs = jnp.concatenate([h1h_ref[t, :, at], jnp.ones((16, width), bf16), h1l_ref[t, :, at]], axis=0)
        top = mm_nt(lhs, d2h_ref[t, :, at])
        low = mm_nt(lhs[:144], d2l_ref[t, :, at])
        keep(0, top[:128] + top[144:272] + low[:128], first)
        keep(ROW_WO, dwo, first)
        bias = jnp.where(row == 1, top[128:136] + low[128:136], jnp.where(row == 2, dbo, 0.0))
        keep(ROW_BIAS, bias, first)

    def weights_one(t, units, first):
        at = pl.ds(units[0] * 128, len(units) * 128)
        width = len(units) * 128
        lhs = jnp.concatenate([fh_ref[t, :, at], jnp.ones((16, width), bf16), fl_ref[t, :, at]], axis=0)
        top = mm_nt(lhs, d1h_ref[t, :, at])
        low = mm_nt(lhs[:48], d1l_ref[t, :, at])
        keep(ROW_W1, top[:32] + top[48:80] + low[:32], first)
        keep(ROW_BIAS, jnp.where(row == 0, top[32:40] + low[32:40], 0.0), False)

    def rows_of(x, units):
        return [x[ROW_OF_UNIT[u]:ROW_OF_UNIT[u] + 1, :] for u in units]

    all_units = list(range(OWN))
    inner_units = list(range(INNER))
    edge_units = [INNER, INNER + 1, STRIP]

    G1 = [wets[1] * lam2[f] for f in range(12)]
    dz1 = closure_cotangent(1, sigmoid(z1), lam2)
    dz_ref[...] = dz1
    drows1 = rows_of(dz_ref, all_units)
    adjoint_two(1, all_units, drows1)
    adjoint_one(1, all_units)
    feature_cotangent(1, all_units)
    D1 = [dfeat_ref[f * 8:(f + 1) * 8, :] for f in range(20)]
    c1, to1 = adjoint_cells(D1, G1, near1, V1, lam2)
    fill(1, *to1)
    each(has_dst, lambda d: copy0_of(d).wait_send())
    if near_only:
        pl.semaphore_wait(relay_sem, beside_al + beside_cs)
    each(has_dst, lambda d: copy_of(1, d).start())

    gate0 = sigmoid(z0)
    weights_two(1, all_units, rows_of(cid, all_units), drows1, True)
    weights_one(1, all_units, True)
    lam1 = [
        c1[f] + turn(to1[0][f], 7, 0) + turn(to1[1][f], 1, 0) + turn(to1[2][f], 127, 1) + turn(to1[3][f], 1, 1)
        for f in range(12)
    ]
    dz0 = closure_cotangent(0, gate0, lam1)
    dz0 = jnp.where(jnp.logical_and(lane > 0, lane < 127), dz0, 0.0)
    dz_ref[...] = dz0
    drows0 = rows_of(dz_ref, inner_units)
    adjoint_two(0, inner_units, drows0)
    weights_two(0, inner_units, rows_of(cid, inner_units), drows0, False)
    adjoint_one(0, inner_units)
    weights_one(0, inner_units, False)
    feature_cotangent(0, inner_units)

    each(has_src, lambda d: copy_of(1, d).wait_recv())
    lam1 = gather(c1, to1, Halo(rcv_row.at[0], rcv_col.at[0]))
    dz0 = closure_cotangent(0, gate0, lam1)
    dstrip = jnp.where(lane == 16 + row, dz0[:, 0:1], jnp.where(lane == 24 + row, dz0[:, 127:128], 0.0))
    dstrip = jnp.sum(jnp.where(inside, dstrip, 0.0), axis=0, keepdims=True)
    drows0 = [dz0[0:1, :], dz0[7:8, :], dstrip]
    ids0 = [cid[0:1, :], cid[7:8, :], cidx_ref[0:1, :]]
    adjoint_two(0, edge_units, drows0)
    weights_two(0, edge_units, ids0, drows0, False)
    adjoint_one(0, edge_units)
    weights_one(0, edge_units, False)

    size = src_b.shape[0]
    mine = pl.ds(pl.multiple_of(cs * size, 8), size)

    def copy_a(j):
        peer = lax.rem(cs + j, ncs)
        return pltpu.make_async_remote_copy(
            src_ref=acc_ref.at[pl.ds(pl.multiple_of(peer * size, 8), size), :],
            dst_ref=rcv_a.at[j - 1], send_sem=sum_send.at[j - 1], recv_sem=sa_recv.at[j - 1],
            device_id=dev(al, peer), device_id_type=MESH,
        )

    def copy_b(j):
        return pltpu.make_async_remote_copy(
            src_ref=src_b, dst_ref=rcv_b.at[al], send_sem=sum_send.at[j - 1],
            recv_sem=sb_recv.at[j - 1],
            device_id=dev(lax.rem(al + j, nal), cs), device_id_type=MESH,
        )

    def copy_c(j):
        return pltpu.make_async_remote_copy(
            src_ref=full_ref.at[mine, :], dst_ref=full_ref.at[mine, :],
            send_sem=sum_send.at[j - 1], recv_sem=sc_recv.at[j - 1],
            device_id=dev(al, lax.rem(cs + j, ncs)), device_id_type=MESH,
        )

    for j in range(1, ncs):
        copy_a(j).start()

    strip_back = feature_cotangent(0, edge_units)[0]
    turned = jnp.transpose(jnp.concatenate([strip_back, jnp.zeros((96, 128), f32)], axis=0))
    at_w, at_e = turned[16:24], turned[24:32]
    D0 = []
    for f in range(20):
        x = dfeat_ref[f * 8:(f + 1) * 8, :]
        x = jnp.where(at_west, turn(at_w, -f, 1), x)
        D0.append(jnp.where(at_east, turn(at_e, 127 - f, 1), x))
    G0 = [wets[0] * lam1[f] for f in range(12)]
    c0, to0 = adjoint_cells(D0, G0, near0, V0, lam1)
    fill(2, *to0)
    each(has_dst, lambda d: copy_of(1, d).wait_send())
    each(has_dst, lambda d: copy_of(2, d).start())

    total = acc_ref[mine, :]
    for j in range(1, ncs):
        copy_a(j).wait_recv()
        total = total + rcv_a[j - 1]
    src_b[...] = total
    rcv_b[al] = total
    for j in range(1, ncs):
        copy_a(j).wait_send()
    for j in range(1, nal):
        copy_b(j).start()
    each(has_src, lambda d: copy_of(2, d).wait_recv())
    last = gather(c0, to0, Halo(rcv_row.at[1], rcv_col.at[1]))
    for f in range(12):
        gstate_ref[f] = last[f]
    each(has_dst, lambda d: copy_of(2, d).wait_send())
    each(diag_dst, lambda e: diag_of(e).wait_send())
    for j in range(1, nal):
        copy_b(j).wait_recv()
    total = rcv_b[0]
    for j in range(1, nal):
        total = total + rcv_b[j]
    full_ref[mine, :] = total * factor
    for j in range(1, nal):
        copy_b(j).wait_send()
    for j in range(1, ncs):
        copy_c(j).start()
    for j in range(1, ncs):
        copy_c(j).wait_recv()
    for j in range(1, ncs):
        copy_c(j).wait_send()


def unpack(
    state_ref, full_ref,
    gs_hbm, gw1_hbm, gb1_hbm, gw2_hbm, gb2_hbm, gwo_hbm, gbo_hbm, gbo_ref, sem,
):
    gbo_ref[...] = full_ref[ROW_BIAS + 2:ROW_BIAS + 3, 0:8]
    parts = (
        (full_ref.at[0:128], gw2_hbm), (state_ref, gs_hbm), (full_ref.at[ROW_W1:ROW_W1 + 32], gw1_hbm),
        (full_ref.at[ROW_WO:ROW_WO + 8], gwo_hbm), (full_ref.at[ROW_BIAS:ROW_BIAS + 1], gb1_hbm),
        (full_ref.at[ROW_BIAS + 1:ROW_BIAS + 2], gb2_hbm), (gbo_ref, gbo_hbm),
    )
    copies = [pltpu.make_async_copy(src, dst, sem.at[i]) for i, (src, dst) in enumerate(parts)]
    for copy in copies:
        copy.start()
    for copy in copies:
        copy.wait()


def solution(mesh):
    nal, ncr, nsu = mesh.shape["along"], mesh.shape["cross"], mesh.shape["sub"]
    ncs = ncr * nsu
    size = 8 * (-(-ROWS // (8 * ncs)))

    def per_device(state, storm, wet, dune, cid, w1, b1, w2, b2, wo, bo, cot):
        rows, cols = state.shape[1], state.shape[2]
        factor = 1.0 / math.sqrt(rows * nal * cols * ncs)
        vmem = pl.BlockSpec(memory_space=pltpu.VMEM)
        hbm = pl.BlockSpec(memory_space=pl.ANY)
        flat = lambda x: x.reshape(-1, 128)
        operands = (
            flat(state), cid, w1, b1.reshape(1, 128), w2, b2.reshape(1, 128), wo.T, bo.reshape(1, 8),
            flat(storm), flat(wet), flat(dune), flat(cot),
        )
        dma = pltpu.SemaphoreType.DMA
        tile = pltpu.VMEM((8, 128), f32)
        big = lambda n, kind: pltpu.VMEM((2, n, (OWN + 1) * 128), kind)
        out = pl.pallas_call(
            functools.partial(kernel, nal, ncr, nsu, factor),
            out_shape=(pltpu.VMEM((12, 8, 128), f32), pltpu.VMEM((ncs * size, 128), f32)),
            in_specs=[hbm] * 12,
            out_specs=(vmem,) * 2,
            scratch_shapes=[
                *[pltpu.VMEM(x.shape, x.dtype) for x in operands],
                dma((12,)),
                pltpu.VMEM((2, 40, 128), f32),
                pltpu.VMEM((2, 8, 128), f32),
                pltpu.VMEM((2, 40, 128), f32),
                pltpu.VMEM((2, 8, 128), f32),
                pltpu.VMEM((4, 16, 128), f32),
                pltpu.VMEM((2, 2, 16, 128), f32),
                pltpu.VMEM((2, 2, 8, 128), f32),
                pltpu.VMEM((2, 2, 16, 128), f32),
                pltpu.VMEM((2, 2, 8, 128), f32),
                pltpu.VMEM((2, 16, 128), f32),
                pltpu.VMEM((2, 8, 128), f32),
                dma((4,)), dma((2, 4)), dma((4,)), dma((4,)), pltpu.SemaphoreType.REGULAR,
                pltpu.VMEM((256, 128), f32),
                pltpu.VMEM((256, 128), f32),
                pltpu.VMEM((3, 32, 128), f32),
                tile, tile, tile, pltpu.VMEM((8, 128), jnp.int32), tile, tile,
                pltpu.VMEM((128, 128), f32),
                pltpu.VMEM((128, 128), f32),
                pltpu.VMEM((128, (OWN + 3) * 128), f32),
                big(32, bf16), big(32, bf16), big(128, bf16), big(128, bf16), big(128, bf16), big(128, bf16),
                big(128, f32), big(128, f32), big(128, bf16), big(128, bf16), big(128, bf16), big(128, bf16),
                pltpu.VMEM((ncs * size, 128), f32),
                pltpu.VMEM((ncs - 1, size, 128), f32),
                pltpu.VMEM((size, 128), f32),
                pltpu.VMEM((nal, size, 128), f32),
                dma((max(ncs, nal) - 1,)), dma((ncs - 1,)), dma((nal - 1,)), dma((ncs - 1,)),
            ],
            compiler_params=pltpu.CompilerParams(collective_id=0, has_side_effects=True),
        )(*operands)
        gs, gw1, gb1, gw2, gb2, gwo, gbo = pl.pallas_call(
            unpack,
            out_shape=(
                jax.ShapeDtypeStruct((12, 8, 128), f32),
                jax.ShapeDtypeStruct((32, 128), f32),
                jax.ShapeDtypeStruct((1, 128), f32),
                jax.ShapeDtypeStruct((128, 128), f32),
                jax.ShapeDtypeStruct((1, 128), f32),
                jax.ShapeDtypeStruct((8, 128), f32),
                jax.ShapeDtypeStruct((1, 8), f32),
            ),
            in_specs=[vmem] * 2,
            out_specs=(hbm,) * 7,
            scratch_shapes=[pltpu.VMEM((1, 8), f32), dma((7,))],
        )(*[pltpu.with_memory_space_constraint(x, pltpu.VMEM) for x in out])
        return gs, gw1, gb1.reshape(128), gw2, gb2.reshape(128), gwo.T, gbo.reshape(8)

    tile = P(None, ("groups", "along"), ("cross", "sub"))
    return jax.shard_map(
        per_device,
        mesh=mesh,
        in_specs=(
            tile, tile, tile, tile, P(("groups", "along"), ("cross", "sub")),
            P(), P(), P(), P(), P(), P(), tile,
        ),
        out_specs=(
            tile, P("groups", None), P("groups"), P("groups", None), P("groups"),
            P("groups", None), P("groups"),
        ),
        check_vma=False,
    )
```

```python
import functools
import math

import jax
import jax.numpy as jnp
from jax import lax
from jax.experimental import pallas as pl
from jax.experimental.pallas import tpu as pltpu
from jax.sharding import PartitionSpec as P

MESH = pl.DeviceIdType.MESH
f32 = jnp.float32
bf16 = jnp.bfloat16
diffusion = 0.15
advection = 0.2
friction = 0.05
pickup_gain = 0.5
settling = 0.2
bed_diffusion = 0.1

ROW_W1 = 128
ROW_WO = 160
ROW_BIAS = 168
ROWS = 176
ROW_OF_UNIT = (1, 2, 3, 4, 5, 6, 0, 7)
INNER = 6
OWN = 8
STRIP = 8
NEXT = 16
STORM = 28
COL_STORM = 32
COL_MASK = 44


def split(x):
    high = x.astype(bf16)
    low = (x - high.astype(f32)).astype(bf16)
    return high, low


def mm(a, b):
    return lax.dot_general(a, b, (((1,), (0,)), ((), ())), preferred_element_type=f32)


def mm_nt(a, b):
    return lax.dot_general(a, b, (((1,), (1,)), ((), ())), preferred_element_type=f32)


def silu(v):
    sig = 0.5 + 0.5 * jnp.tanh(0.5 * v)
    return sig, v * sig


def softplus(z):
    return jnp.maximum(z, 0.0) + jnp.log(1.0 + jnp.exp(-jnp.abs(z)))


def kernel(
    nal, ncr, nsu, near_only, direct, factor,
    state_hbm, cid_hbm, w1_hbm, b1_hbm, w2_hbm, b2_hbm, wo_hbm, bo_hbm,
    storm_hbm, wet_hbm, dune_hbm, cot_hbm,
    gstate_ref, full_ref,
    state_ref, cid_ref, w1_ref, b1_ref, w2_ref, b2_ref, wo_ref, bo_ref,
    storm_ref, wet_ref, dune_ref, cot_ref, load_sem,
    snd0_row, snd0_col, rcv0_row, rcv0_col, rcv_diag,
    snd_row, snd_col, rcv_row, rcv_col, ring_row, ring_col,
    edge_send, edge_recv, diag_send, diag_recv, relay_sem,
    feat_ref, dfeat_ref, fx_ref, z_ref, zx_ref, dz_ref, cidx_ref, wetx_ref, dunex_ref,
    b1b_ref, b2b_ref, wsel_ref,
    fh_ref, fl_ref, h1h_ref, h1l_ref, h2h_ref, h2l_ref,
    act1_ref, q2_ref, d1h_ref, d1l_ref, d2h_ref, d2l_ref,
    acc_ref, rcv_a, src_b, rcv_b,
    sum_send, sa_recv, sb_recv, sc_recv,
):
    ncs = ncr * nsu
    g = lax.axis_index("groups")
    al = lax.axis_index("along")
    cr = lax.axis_index("cross")
    su = lax.axis_index("sub")
    cs = cr * nsu + su

    def dev(a, c):
        return (g, a, c // nsu, c % nsu)

    has_dst = (al > 0, al < nal - 1, cs > 0, cs < ncs - 1)
    has_src = (al < nal - 1, al > 0, cs < ncs - 1, cs > 0)
    dst_dev = (
        dev(al - 1, cs), dev(al + 1, cs), dev(al, cs - 1), dev(al, cs + 1),
    )
    corners = ((0, 2), (0, 3), (1, 2), (1, 3))
    diag_dst = [jnp.logical_and(has_dst[a], has_dst[c]) for a, c in corners]
    diag_src = [jnp.logical_and(has_src[a], has_src[c]) for a, c in corners]
    diag_dev = [dev(al + (1 if a else -1), cs + (1 if c == 3 else -1)) for a, c in corners]

    loads = [
        pltpu.make_async_copy(src, dst, load_sem.at[i])
        for i, (src, dst) in enumerate((
            (state_hbm, state_ref), (storm_hbm, storm_ref), (wet_hbm, wet_ref), (dune_hbm, dune_ref),
            (cid_hbm, cid_ref), (w1_hbm, w1_ref), (b1_hbm, b1_ref), (w2_hbm, w2_ref),
            (b2_hbm, b2_ref), (wo_hbm, wo_ref), (bo_hbm, bo_ref), (cot_hbm, cot_ref),
        ))
    ]
    for load in loads[:5]:
        load.start()
    for ref in (rcv0_row, rcv0_col, rcv_diag, rcv_row, rcv_col):
        ref[...] = jnp.zeros_like(ref)

    barrier = pltpu.get_barrier_semaphore()
    for e in range(4):
        @pl.when(diag_dst[e])
        def _():
            pl.semaphore_signal(barrier, inc=1, device_id=diag_dev[e], device_id_type=MESH)
    if near_only:
        for d in range(4):
            @pl.when(has_dst[d])
            def _():
                pl.semaphore_signal(barrier, inc=1, device_id=dst_dev[d], device_id_type=MESH)
    else:
        for j in range(1, ncs):
            pl.semaphore_signal(
                barrier, inc=1, device_id=dev(al, lax.rem(cs + j, ncs)), device_id_type=MESH
            )
        for j in range(1, nal):
            pl.semaphore_signal(
                barrier, inc=1, device_id=dev(lax.rem(al + j, nal), cs), device_id_type=MESH
            )
    for load in loads[5:]:
        load.start()
    beside_al = (al + nal - 1) // nal + (2 * nal - 2 - al) // nal
    beside_cs = (cs + ncs - 1) // ncs + (2 * ncs - 2 - cs) // ncs

    row = lax.broadcasted_iota(jnp.int32, (8, 128), 0)
    lane = lax.broadcasted_iota(jnp.int32, (8, 128), 1)
    field = lax.broadcasted_iota(jnp.int32, (16, 128), 0)
    lane16 = lax.broadcasted_iota(jnp.int32, (16, 128), 1)

    def turn(x, shift, axis):
        shift = shift % x.shape[axis]
        return pltpu.roll(x, shift, axis) if shift else x

    def copy0_of(d):
        src, dst = (snd0_row, rcv0_row) if d < 2 else (snd0_col, rcv0_col)
        return pltpu.make_async_remote_copy(
            src_ref=src.at[d % 2], dst_ref=dst.at[d % 2], send_sem=edge_send.at[d],
            recv_sem=edge_recv.at[0, d], device_id=dst_dev[d], device_id_type=MESH,
        )

    def diag_of(e):
        return pltpu.make_async_remote_copy(
            src_ref=snd0_row.at[e // 2, pl.ds(0, 16)], dst_ref=rcv_diag.at[e],
            send_sem=diag_send.at[e], recv_sem=diag_recv.at[e],
            device_id=diag_dev[e], device_id_type=MESH,
        )

    def copy_of(k, d):
        src, dst = (snd_row, rcv_row) if d < 2 else (snd_col, rcv_col)
        return pltpu.make_async_remote_copy(
            src_ref=src.at[k - 1, d % 2], dst_ref=dst.at[k - 1, d % 2], send_sem=edge_send.at[d],
            recv_sem=edge_recv.at[k % 2, d], device_id=dst_dev[d], device_id_type=MESH,
        )

    beside = beside_al + beside_cs + beside_al * beside_cs

    def relay(k):
        if near_only:
            for flags, devices in ((has_dst, dst_dev), (diag_dst, diag_dev)):
                each(flags, lambda i: pl.semaphore_signal(
                    relay_sem.at[k], inc=1, device_id=devices[i], device_id_type=MESH))

    def relayed(k):
        if near_only:
            pl.semaphore_wait(relay_sem.at[k], beside)

    def each(flags, action):
        for i in range(4):
            @pl.when(flags[i])
            def _():
                action(i)

    def fill(k, xn, xs, xw, xe):
        west = jnp.zeros((8, 128), f32)
        east = jnp.zeros((8, 128), f32)
        for f in range(12):
            snd_row[k - 1, 0, f:f + 1, :] = xn[f][0:1, :]
            snd_row[k - 1, 1, f:f + 1, :] = xs[f][7:8, :]
            west = jnp.where(lane == f, turn(xw[f], f, 1), west)
            east = jnp.where(lane == f, turn(xe[f], f + 1, 1), east)
        snd_col[k - 1, 0] = west
        snd_col[k - 1, 1] = east

    class Halo:
        def __init__(self, rows, cols):
            self.rows, self.cols = rows, cols

        def south(self, x, f):
            return jnp.where(row == 7, self.rows[0, f:f + 1, :], turn(x, 7, 0))

        def north(self, x, f):
            return jnp.where(row == 0, self.rows[1, f:f + 1, :], turn(x, 1, 0))

        def east(self, x, f):
            return jnp.where(lane == 127, turn(self.cols[0], 127 - f, 1), turn(x, 127, 1))

        def west(self, x, f):
            return jnp.where(lane == 0, turn(self.cols[1], -f, 1), turn(x, 1, 1))

        def around(self, x, f):
            return self.north(x, f), self.south(x, f), self.west(x, f), self.east(x, f)

    for load in loads[:5]:
        load.wait()
    V0 = [state_ref[f * 8:(f + 1) * 8, :] for f in range(12)]
    storm = [storm_ref[f * 8:(f + 1) * 8, :] for f in range(12)]
    wets = [wet_ref[t * 8:(t + 1) * 8, :].astype(f32) for t in range(2)]
    dunes = [dune_ref[t * 8:(t + 1) * 8, :].astype(f32) for t in range(2)]
    wash = [1.0 - dunes[t] for t in range(2)]
    cid = cid_ref[...]
    masks = [wets[0], dunes[0], cid.astype(f32)]
    for d, edge, inner in ((0, 0, 1), (1, 7, 6)):
        for f in range(12):
            snd0_row[d, f:f + 1, :] = V0[f][edge:edge + 1, :]
            snd0_row[d, NEXT + f:NEXT + f + 1, :] = V0[f][inner:inner + 1, :]
            snd0_row[d, STORM + f:STORM + f + 1, :] = storm[f][edge:edge + 1, :]
        for m in range(3):
            snd0_row[d, 12 + m:13 + m, :] = masks[m][edge:edge + 1, :]
        snd0_row[d, 15:16, :] = jnp.zeros((1, 128), f32)
    for d, edge, inner in ((0, 0, 1), (1, 127, 126)):
        out = jnp.zeros((8, 128), f32)
        for x, at, c in (
            [(V0[f], f, edge) for f in range(12)] + [(V0[f], NEXT + f, inner) for f in range(12)]
            + [(storm[f], COL_STORM + f, edge) for f in range(12)]
            + [(masks[m], COL_MASK + m, edge) for m in range(3)]
        ):
            out = jnp.where(lane == at, turn(x, at - c, 1), out)
        snd0_col[d] = out
    if near_only:
        pl.semaphore_wait(barrier, beside)
    else:
        pl.semaphore_wait(barrier, ncs - 1 + nal - 1 + beside_al * beside_cs)
    each(has_dst, lambda d: copy0_of(d).start())
    each(diag_dst, lambda e: diag_of(e).start())
    for load in loads[5:]:
        load.wait()

    w1 = w1_ref[...]
    w1t = jnp.transpose(jnp.concatenate([w1, jnp.zeros((96, 128), f32)], axis=0))[:, :32]
    w1th, w1tl = split(w1t)
    w1t_cat = jnp.concatenate([w1th, w1tl, w1th], axis=1)
    w1h, w1l = split(w1)
    w1_hh = jnp.concatenate([w1h, w1h], axis=1)
    w2 = w2_ref[...]
    w2h, w2l = split(w2)
    w2_hh = jnp.concatenate([w2h, w2h], axis=1)
    w2th, w2tl = split(jnp.transpose(w2))
    w2t_hh = jnp.concatenate([w2th, w2th], axis=1)
    b1b_ref[...] = jnp.transpose(jnp.broadcast_to(b1_ref[...], (128, 128)))
    b2b_ref[...] = jnp.transpose(jnp.broadcast_to(b2_ref[...], (128, 128)))
    wo_t = jnp.transpose(jnp.concatenate([wo_ref[...], jnp.zeros((120, 128), f32)], axis=0))[:, :8]

    def choose(unit, ids):
        onehot = (row == ids).astype(f32)
        wsel_ref[:, unit * 128:(unit + 1) * 128] = lax.dot_general(
            wo_t, onehot, (((1,), (0,)), ((), ())),
            precision=lax.Precision.HIGHEST, preferred_element_type=f32,
        )

    def bias_of(ids):
        b = jnp.zeros((8, 128), f32)
        for k in range(8):
            b = jnp.where(ids == k, bo_ref[0:1, k:k + 1], b)
        return b

    for u in range(OWN):
        choose(u, cid[ROW_OF_UNIT[u]:ROW_OF_UNIT[u] + 1, :])
    bsel = bias_of(cid)

    def twice(x, n):
        return jnp.concatenate([x] * n, axis=1) if n > 1 else x

    def layers(t, unit, feats, kept):
        n = len(feats)
        at = pl.ds(unit * 128, n * 128)
        F = jnp.concatenate(feats, axis=1) if n > 1 else feats[0]
        Fh, Fl = split(F)
        v = mm(w1t_cat, jnp.concatenate([Fh, Fh, Fl], axis=0)) + twice(b1b_ref[...], n)
        sig, h = silu(v)
        Hh, Hl = split(h)
        if kept:
            fh_ref[t, :, at] = Fh
            fl_ref[t, :, at] = Fl
            act1_ref[t, :, at] = sig + h * (1.0 - sig)
            h1h_ref[t, :, at] = Hh
            h1l_ref[t, :, at] = Hl
        v = mm(w2t_hh, jnp.concatenate([Hh, Hl], axis=0)) + mm(w2tl, Hh) + twice(b2b_ref[...], n)
        sig, h = silu(v)
        wsel = wsel_ref[:, at]
        if kept:
            q2_ref[t, :, at] = wsel * (sig + h * (1.0 - sig))
            Hh, Hl = split(h)
            h2h_ref[t, :, at] = Hh
            h2l_ref[t, :, at] = Hl
        z = jnp.sum(wsel * h, axis=0, keepdims=True)
        return [z[:, i * 128:(i + 1) * 128] for i in range(n)]

    def put_features(V, near):
        for f in range(4):
            for part, x in enumerate((V[f],) + tuple(near[f])):
                feat_ref[(4 * part + f) * 8:(4 * part + f + 1) * 8, :] = x

    def own_layers(t, first, last):
        for u in range(first, last, 2):
            rows = ROW_OF_UNIT[u:u + 2]
            feats = [feat_ref[pl.ds(r, 32, stride=8), :] for r in rows]
            for r, z in zip(rows, layers(t, u, feats, True)):
                z_ref[r:r + 1, :] = z

    feat_ref[160:256, :] = storm_ref[...]
    put_features(V0, [
        (turn(V0[f], 1, 0), turn(V0[f], 7, 0), turn(V0[f], 1, 1), turn(V0[f], 127, 1)) for f in range(4)
    ])
    own_layers(0, 0, INNER)
    for ref in (zx_ref, cidx_ref, wetx_ref, dunex_ref):
        ref[...] = jnp.zeros_like(ref)
    spare = acc_ref.shape[0] - ROWS
    if spare:
        acc_ref[ROWS:, :] = jnp.zeros((spare, 128), f32)

    each(has_src, lambda d: copy0_of(d).wait_recv())
    each(diag_src, lambda e: diag_of(e).wait_recv())
    relay(0)

    halo0 = Halo(rcv0_row, rcv0_col)
    near0 = [halo0.around(V0[f], f) for f in range(12)]
    put_features(V0, near0)
    sides = jnp.concatenate(
        [rcv0_col[1], rcv0_col[0], snd0_col[0], snd0_col[1], jnp.zeros((96, 128), f32)], axis=0
    )
    T = jnp.transpose(sides)
    SE, SW, NE, NW = [rcv_diag[e] for e in range(4)]
    RS, RN = rcv0_row[0, 0:16, :], rcv0_row[1, 0:16, :]
    group = lane16 // 8
    V, far = T[0:16], T[NEXT:NEXT + 16]
    plus, minus = turn(V, 16, 1), turn(V, -16, 1)
    N, S = turn(V, 1, 1), turn(V, -1, 1)
    for at, x, c in ((0, NW, 127), (8, NE, 0), (16, RN, 0), (24, RN, 127)):
        N = jnp.where(lane16 == at, turn(x, at - c, 1), N)
    for at, x, c in ((7, SW, 127), (15, SE, 0), (23, RS, 0), (31, RS, 127)):
        S = jnp.where(lane16 == at, turn(x, at - c, 1), S)
    W = jnp.where(group == 1, minus, jnp.where(group == 2, plus, far))
    E = jnp.where(group == 0, minus, jnp.where(group == 3, plus, far))
    outer = [(V, N, S, W, E)]
    for V, N, S, west, east in (
        (RN, rcv0_row[1, NEXT:NEXT + 16, :], snd0_row[0, 0:16, :], NW, NE),
        (RS, snd0_row[1, 0:16, :], rcv0_row[0, NEXT:NEXT + 16, :], SW, SE),
    ):
        W = jnp.where(lane16 == 0, turn(west, 1, 1), turn(V, 1, 1))
        E = jnp.where(lane16 == 127, turn(east, 127, 1), turn(V, 127, 1))
        outer.append((V, N, S, W, E))
    storms = [T[COL_STORM:COL_STORM + 12], rcv0_row[1, STORM:STORM + 12, :], rcv0_row[0, STORM:STORM + 12, :]]
    mask_rows = [
        [T[COL_MASK + m:COL_MASK + m + 1] for m in range(3)],
        [rcv0_row[1, 12 + m:13 + m, :] for m in range(3)],
        [rcv0_row[0, 12 + m:13 + m, :] for m in range(3)],
    ]
    for w in range(3):
        for part in range(5):
            fx_ref[w, 4 * part:4 * part + 4, :] = outer[w][part][0:4]
        fx_ref[w, 20:32, :] = storms[w]
        wetx_ref[w:w + 1, :] = mask_rows[w][0]
        dunex_ref[w:w + 1, :] = mask_rows[w][1]
        ids = mask_rows[w][2].astype(jnp.int32)
        cidx_ref[w:w + 1, :] = ids
        choose(STRIP + w, ids)
    cidx = cidx_ref[...]
    own_layers(0, INNER, OWN)
    zx_ref[0:1, :] = layers(0, STRIP, [fx_ref[0]], True)[0]
    zx_ref[1:2, :], zx_ref[2:3, :] = layers(0, STRIP + 1, [fx_ref[1], fx_ref[2]], False)
    zx = zx_ref[...] + bias_of(cidx)
    pickx = pickup_gain * softplus(zx) * (1.0 - dunex_ref[...])

    def from_strip(x, start):
        return jnp.sum(jnp.where(lane == start + row, x, 0.0), axis=1, keepdims=True)

    inside = jnp.logical_and(row > 0, row < 7)
    at_west = jnp.logical_and(inside, lane == 0)
    at_east = jnp.logical_and(inside, lane == 127)
    z0 = z_ref[...] + bsel
    z0 = jnp.where(at_west, from_strip(zx[0:1, :], 16), z0)
    z0 = jnp.where(at_east, from_strip(zx[0:1, :], 24), z0)

    def advanced(w):
        V, N, S, W, E = outer[w]
        pick, wet = pickx[w:w + 1, :], wetx_ref[w:w + 1, :]
        lap = N + S + W + E - 4.0 * V
        ad, cd = S - N, E - W
        spread = jnp.where(field == 3, bed_diffusion, diffusion) * lap
        sediment = spread - advection * (V[1:2] * ad + V[2:3] * cd) - settling * V
        sediment = sediment + jnp.where(field - 4 == cidx[w:w + 1, :], pick, 0.0)
        total = jnp.sum(
            jnp.where(jnp.logical_and(field >= 4, field < 12), V, 0.0), axis=0, keepdims=True
        )
        first = jnp.where(field == 0, -advection * (ad[1:2] + cd[2:3]), settling * total - pick)
        first = jnp.where(field == 1, -advection * ad[0:1] - friction * V[1:2], first)
        first = jnp.where(field == 2, -advection * cd[0:1] - friction * V[2:3], first)
        return V + wet * jnp.where(field < 4, spread + first, sediment)

    ring_row[1] = advanced(1)
    ring_row[0] = advanced(2)
    back = jnp.transpose(jnp.concatenate([advanced(0), jnp.zeros((112, 128), f32)], axis=0))
    ring_col[1] = back[0:8]
    ring_col[0] = back[8:16]

    pickup = softplus(z0) * wash[0]
    lap = []
    for f in range(12):
        n, s, w, e = near0[f]
        lap.append(n + s + w + e - 4.0 * V0[f])
    total = V0[4]
    for k in range(1, 8):
        total = total + V0[4 + k]
    ad = [near0[f][1] - near0[f][0] for f in range(12)]
    cd = [near0[f][3] - near0[f][2] for f in range(12)]
    tend = [
        diffusion * lap[0] - advection * (ad[1] + cd[2]),
        diffusion * lap[1] - advection * ad[0] - friction * V0[1],
        diffusion * lap[2] - advection * cd[0] - friction * V0[2],
        bed_diffusion * lap[3] - pickup_gain * pickup + settling * total,
    ]
    for k in range(8):
        x = diffusion * lap[4 + k] - advection * (V0[1] * ad[4 + k] + V0[2] * cd[4 + k])
        x = x + jnp.where(cid == k, pickup_gain * pickup, 0.0) - settling * V0[4 + k]
        tend.append(x)
    V1 = [V0[f] + wets[0] * tend[f] for f in range(12)]

    halo1 = Halo(ring_row, ring_col)
    near1 = [halo1.around(V1[f], f) for f in range(12)]
    put_features(V1, near1)
    own_layers(1, 0, OWN)
    relayed(0)
    relay(1)
    z1 = z_ref[...] + bsel
    lam2 = [cot_ref[f * 8:(f + 1) * 8, :] for f in range(12)]

    def closure_cotangent(t, gate, lam):
        G = [None] * 3 + [wets[t] * lam[f] for f in range(3, 12)]
        picked = G[4]
        for k in range(1, 8):
            picked = jnp.where(cid == k, G[4 + k], picked)
        return pickup_gain * (picked - G[3]) * wash[t] * gate

    def sigmoid(z):
        return 1.0 / (1.0 + jnp.exp(-z))

    def pairs(units):
        return [units[i:i + 2] for i in range(0, len(units), 2)]

    def adjoint_two(t, units, drows):
        for part in pairs(list(zip(units, drows))):
            at = pl.ds(part[0][0] * 128, len(part) * 128)
            drow = jnp.concatenate([d for _, d in part], axis=1)
            Dh, Dl = split(q2_ref[t, :, at] * drow)
            d2h_ref[t, :, at] = Dh
            d2l_ref[t, :, at] = Dl

    def adjoint_one(t, units):
        for part in pairs(units):
            at = pl.ds(part[0] * 128, len(part) * 128)
            Dh, Dl = d2h_ref[t, :, at], d2l_ref[t, :, at]
            d1 = mm(w2_hh, jnp.concatenate([Dh, Dl], axis=0)) + mm(w2l, Dh)
            Dh, Dl = split(d1 * act1_ref[t, :, at])
            d1h_ref[t, :, at] = Dh
            d1l_ref[t, :, at] = Dl

    def feature_cotangent(t, units):
        out = []
        for part in pairs(units):
            at = pl.ds(part[0] * 128, len(part) * 128)
            Dh, Dl = d1h_ref[t, :, at], d1l_ref[t, :, at]
            dF = mm(w1_hh, jnp.concatenate([Dh, Dl], axis=0)) + mm(w1l, Dh)
            for i, u in enumerate(part):
                one = dF[:, i * 128:(i + 1) * 128]
                if u < OWN:
                    dfeat_ref[pl.ds(ROW_OF_UNIT[u], 32, stride=8), :] = one
                else:
                    out.append(one)
        return out

    def adjoint_cells(D, G, near, V, lam):
        lap = [bed_diffusion if f == 3 else diffusion for f in range(12)]
        lg = [lap[f] * G[f] for f in range(12)]
        c = [lam[f] - 4.0 * lg[f] for f in range(12)]
        alongs = jnp.zeros((8, 128), f32)
        crosses = jnp.zeros((8, 128), f32)
        along_part = [advection * G[1], advection * G[0], None, None]
        cross_part = [advection * G[2], None, advection * G[0], None]
        for k in range(8):
            n, s, w, e = near[4 + k]
            alongs = alongs + (s - n) * G[4 + k]
            crosses = crosses + (e - w) * G[4 + k]
            c[4 + k] = c[4 + k] + settling * (G[3] - G[4 + k])
            ag = advection * G[4 + k]
            along_part.append(V[1] * ag)
            cross_part.append(V[2] * ag)
        c[1] = c[1] - friction * G[1] - advection * alongs
        c[2] = c[2] - friction * G[2] - advection * crosses
        to = [[], [], [], []]
        for f in range(12):
            for d, part, sign in ((0, along_part, 1), (1, along_part, -1), (2, cross_part, 1), (3, cross_part, -1)):
                x = lg[f]
                if part[f] is not None:
                    x = x + part[f] if sign > 0 else x - part[f]
                if f < 4:
                    x = x + D[4 + 4 * d + f]
                to[d].append(x)
            if f < 4:
                c[f] = c[f] + D[f]
        return c, to

    def gather(c, to, halo):
        return [
            c[f] + halo.south(to[0][f], f) + halo.north(to[1][f], f)
            + halo.east(to[2][f], f) + halo.west(to[3][f], f)
            for f in range(12)
        ]

    def keep(start, part, first):
        at = pl.ds(start, part.shape[0])
        acc_ref[at, :] = part if first else acc_ref[at, :] + part

    def weights_two(t, units, ids, drows, first):
        at = pl.ds(units[0] * 128, len(units) * 128)
        width = len(units) * 128
        dr = jnp.concatenate(
            [jnp.where(row == k, d, 0.0) for k, d in zip(ids, drows)], axis=1
        )
        dbo = jnp.sum(
            jnp.where(row == lane, jnp.sum(dr, axis=1, keepdims=True), 0.0), axis=0, keepdims=True
        )
        drh, drl = split(jnp.concatenate([dr, jnp.zeros((8, width), f32)], axis=0))
        top = mm_nt(jnp.concatenate([drh, drl], axis=0), h2h_ref[t, :, at])
        dwo = top[:8] + top[16:24] + mm_nt(drh, h2l_ref[t, :, at])[:8]
        lhs = jnp.concatenate([h1h_ref[t, :, at], jnp.ones((16, width), bf16), h1l_ref[t, :, at]], axis=0)
        top = mm_nt(lhs, d2h_ref[t, :, at])
        low = mm_nt(lhs[:144], d2l_ref[t, :, at])
        keep(0, top[:128] + top[144:272] + low[:128], first)
        keep(ROW_WO, dwo, first)
        bias = jnp.where(row == 1, top[128:136] + low[128:136], jnp.where(row == 2, dbo, 0.0))
        keep(ROW_BIAS, bias, first)

    def weights_one(t, units, first):
        at = pl.ds(units[0] * 128, len(units) * 128)
        width = len(units) * 128
        lhs = jnp.concatenate([fh_ref[t, :, at], jnp.ones((16, width), bf16), fl_ref[t, :, at]], axis=0)
        top = mm_nt(lhs, d1h_ref[t, :, at])
        low = mm_nt(lhs[:48], d1l_ref[t, :, at])
        keep(ROW_W1, top[:32] + top[48:80] + low[:32], first)
        keep(ROW_BIAS, jnp.where(row == 0, top[32:40] + low[32:40], 0.0), False)

    def rows_of(x, units):
        return [x[ROW_OF_UNIT[u]:ROW_OF_UNIT[u] + 1, :] for u in units]

    all_units = list(range(OWN))
    inner_units = list(range(INNER))
    edge_units = [INNER, INNER + 1, STRIP]

    G1 = [wets[1] * lam2[f] for f in range(12)]
    dz1 = closure_cotangent(1, sigmoid(z1), lam2)
    dz_ref[...] = dz1
    drows1 = rows_of(dz_ref, all_units)
    adjoint_two(1, all_units, drows1)
    adjoint_one(1, all_units)
    feature_cotangent(1, all_units)
    D1 = [dfeat_ref[f * 8:(f + 1) * 8, :] for f in range(20)]
    c1, to1 = adjoint_cells(D1, G1, near1, V1, lam2)
    fill(1, *to1)
    each(has_dst, lambda d: copy0_of(d).wait_send())
    each(has_dst, lambda d: copy_of(1, d).start())

    gate0 = sigmoid(z0)
    weights_two(1, all_units, rows_of(cid, all_units), drows1, True)
    weights_one(1, all_units, True)
    lam1 = [
        c1[f] + turn(to1[0][f], 7, 0) + turn(to1[1][f], 1, 0) + turn(to1[2][f], 127, 1) + turn(to1[3][f], 1, 1)
        for f in range(12)
    ]
    dz0 = closure_cotangent(0, gate0, lam1)
    dz0 = jnp.where(jnp.logical_and(lane > 0, lane < 127), dz0, 0.0)
    dz_ref[...] = dz0
    drows0 = rows_of(dz_ref, inner_units)
    adjoint_two(0, inner_units, drows0)
    weights_two(0, inner_units, rows_of(cid, inner_units), drows0, False)
    adjoint_one(0, inner_units)
    weights_one(0, inner_units, False)
    feature_cotangent(0, inner_units)

    each(has_src, lambda d: copy_of(1, d).wait_recv())
    relayed(1)
    lam1 = gather(c1, to1, Halo(rcv_row.at[0], rcv_col.at[0]))
    dz0 = closure_cotangent(0, gate0, lam1)
    dstrip = jnp.where(lane == 16 + row, dz0[:, 0:1], jnp.where(lane == 24 + row, dz0[:, 127:128], 0.0))
    dstrip = jnp.sum(jnp.where(inside, dstrip, 0.0), axis=0, keepdims=True)
    drows0 = [dz0[0:1, :], dz0[7:8, :], dstrip]
    ids0 = [cid[0:1, :], cid[7:8, :], cidx_ref[0:1, :]]
    adjoint_two(0, edge_units, drows0)
    weights_two(0, edge_units, ids0, drows0, False)
    adjoint_one(0, edge_units)
    weights_one(0, edge_units, False)

    size = src_b.shape[0]
    last_core = nsu - 1
    owner = su == last_core
    piece = al * ncr + cr if direct else cs
    mine = pl.ds(pl.multiple_of(piece * size, 8), size)
    spans = [(dz, dx) for dz in range(nal) for dx in range(ncr)]

    def chip_at(span):
        return lax.rem(al + span[0], nal), lax.rem(cr + span[1], ncr)

    def to_owner(k):
        a, c = chip_at(spans[k])
        slot = 2 * (k - 1) + su if k else 2 * (len(spans) - 1)
        at = pl.ds(pl.multiple_of((a * ncr + c) * size, 8), size)
        return pltpu.make_async_remote_copy(
            src_ref=acc_ref.at[at, :], dst_ref=rcv_a.at[slot], send_sem=sum_send.at[0],
            recv_sem=sa_recv.at[0], device_id=(g, a, c, last_core), device_id_type=MESH,
        )

    def from_owner(k, core):
        a, c = chip_at(spans[k])
        return pltpu.make_async_remote_copy(
            src_ref=full_ref.at[mine, :], dst_ref=full_ref.at[mine, :], send_sem=sum_send.at[1],
            recv_sem=sc_recv.at[0], device_id=(g, a, c, core), device_id_type=MESH,
        )

    def all_of(ref, sem):
        return pltpu.make_async_remote_copy(
            src_ref=ref, dst_ref=ref, send_sem=sem, recv_sem=sem,
            device_id=(g, al, cr, nsu - 1 - su), device_id_type=MESH,
        )

    def copy_a(j):
        peer = lax.rem(cs + j, ncs)
        return pltpu.make_async_remote_copy(
            src_ref=acc_ref.at[pl.ds(pl.multiple_of(peer * size, 8), size), :],
            dst_ref=rcv_a.at[j - 1], send_sem=sum_send.at[j - 1], recv_sem=sa_recv.at[j - 1],
            device_id=dev(al, peer), device_id_type=MESH,
        )

    def copy_b(j):
        return pltpu.make_async_remote_copy(
            src_ref=src_b, dst_ref=rcv_b.at[al], send_sem=sum_send.at[j - 1],
            recv_sem=sb_recv.at[j - 1],
            device_id=dev(lax.rem(al + j, nal), cs), device_id_type=MESH,
        )

    def copy_c(j):
        return pltpu.make_async_remote_copy(
            src_ref=full_ref.at[mine, :], dst_ref=full_ref.at[mine, :],
            send_sem=sum_send.at[j - 1], recv_sem=sc_recv.at[j - 1],
            device_id=dev(al, lax.rem(cs + j, ncs)), device_id_type=MESH,
        )

    others = len(spans) - 1
    if direct:
        for k in range(others, 0, -1):
            to_owner(k).start()

        @pl.when(jnp.logical_not(owner))
        def _():
            to_owner(0).start()
    else:
        for j in range(1, ncs):
            copy_a(j).start()

    strip_back = feature_cotangent(0, edge_units)[0]
    turned = jnp.transpose(jnp.concatenate([strip_back, jnp.zeros((96, 128), f32)], axis=0))
    at_w, at_e = turned[16:24], turned[24:32]
    D0 = []
    for f in range(20):
        x = dfeat_ref[f * 8:(f + 1) * 8, :]
        x = jnp.where(at_west, turn(at_w, -f, 1), x)
        D0.append(jnp.where(at_east, turn(at_e, 127 - f, 1), x))
    G0 = [wets[0] * lam1[f] for f in range(12)]
    c0, to0 = adjoint_cells(D0, G0, near0, V0, lam1)
    fill(2, *to0)
    each(has_dst, lambda d: copy_of(1, d).wait_send())
    each(has_dst, lambda d: copy_of(2, d).start())

    if direct:
        @pl.when(owner)
        def _():
            all_of(rcv_a, sa_recv.at[0]).wait_recv()
            total = acc_ref[mine, :]
            for j in range(rcv_a.shape[0]):
                total = total + rcv_a[j]
            full_ref[mine, :] = total * factor
            for k in range(others, -1, -1):
                for core in range(nsu):
                    if k or core != last_core:
                        from_owner(k, core).start()
    else:
        total = acc_ref[mine, :]
        for j in range(1, ncs):
            copy_a(j).wait_recv()
            total = total + rcv_a[j - 1]
        src_b[...] = total
        rcv_b[al] = total
        for j in range(1, ncs):
            copy_a(j).wait_send()
        for j in range(1, nal):
            copy_b(j).start()
    each(has_src, lambda d: copy_of(2, d).wait_recv())
    last = gather(c0, to0, Halo(rcv_row.at[1], rcv_col.at[1]))
    for f in range(12):
        gstate_ref[f] = last[f]
    each(has_dst, lambda d: copy_of(2, d).wait_send())
    each(diag_dst, lambda e: diag_of(e).wait_send())
    if direct:
        @pl.when(owner)
        def _():
            all_of(acc_ref.at[pl.ds(0, others * size), :], sum_send.at[0]).wait_send()
            all_of(full_ref.at[pl.ds(0, others * size), :], sc_recv.at[0]).wait_recv()
            all_of(rcv_a, sum_send.at[1]).wait_send()

        @pl.when(jnp.logical_not(owner))
        def _():
            all_of(acc_ref, sum_send.at[0]).wait_send()
            all_of(full_ref, sc_recv.at[0]).wait_recv()
    else:
        for j in range(1, nal):
            copy_b(j).wait_recv()
        total = rcv_b[0]
        for j in range(1, nal):
            total = total + rcv_b[j]
        full_ref[mine, :] = total * factor
        for j in range(1, nal):
            copy_b(j).wait_send()
        for j in range(1, ncs):
            copy_c(j).start()
        for j in range(1, ncs):
            copy_c(j).wait_recv()
        for j in range(1, ncs):
            copy_c(j).wait_send()


def unpack(
    state_ref, full_ref,
    gs_hbm, gw1_hbm, gb1_hbm, gw2_hbm, gb2_hbm, gwo_hbm, gbo_hbm, gbo_ref, sem,
):
    gbo_ref[...] = full_ref[ROW_BIAS + 2:ROW_BIAS + 3, 0:8]
    parts = (
        (full_ref.at[0:128], gw2_hbm), (state_ref, gs_hbm), (full_ref.at[ROW_W1:ROW_W1 + 32], gw1_hbm),
        (full_ref.at[ROW_WO:ROW_WO + 8], gwo_hbm), (full_ref.at[ROW_BIAS:ROW_BIAS + 1], gb1_hbm),
        (full_ref.at[ROW_BIAS + 1:ROW_BIAS + 2], gb2_hbm), (gbo_ref, gbo_hbm),
    )
    copies = [pltpu.make_async_copy(src, dst, sem.at[i]) for i, (src, dst) in enumerate(parts)]
    for copy in copies:
        copy.start()
    for copy in copies:
        copy.wait()


def solution(mesh):
    nal, ncr, nsu = mesh.shape["along"], mesh.shape["cross"], mesh.shape["sub"]
    ncs = ncr * nsu
    near_only = nal <= 4 and ncs <= 4
    direct = near_only and nsu == 2
    owners = nal * ncr if direct else ncs
    size = 8 * (-(-ROWS // (8 * owners)))

    def per_device(state, storm, wet, dune, cid, w1, b1, w2, b2, wo, bo, cot):
        rows, cols = state.shape[1], state.shape[2]
        factor = 1.0 / math.sqrt(rows * nal * cols * ncs)
        vmem = pl.BlockSpec(memory_space=pltpu.VMEM)
        hbm = pl.BlockSpec(memory_space=pl.ANY)
        flat = lambda x: x.reshape(-1, 128)
        operands = (
            flat(state), cid, w1, b1.reshape(1, 128), w2, b2.reshape(1, 128), wo.T, bo.reshape(1, 8),
            flat(storm), flat(wet), flat(dune), flat(cot),
        )
        dma = pltpu.SemaphoreType.DMA
        tile = pltpu.VMEM((8, 128), f32)
        big = lambda n, kind: pltpu.VMEM((2, n, (OWN + 1) * 128), kind)
        out = pl.pallas_call(
            functools.partial(kernel, nal, ncr, nsu, near_only, direct, factor),
            out_shape=(pltpu.VMEM((12, 8, 128), f32), pltpu.VMEM((owners * size, 128), f32)),
            in_specs=[hbm] * 12,
            out_specs=(vmem,) * 2,
            scratch_shapes=[
                *[pltpu.VMEM(x.shape, x.dtype) for x in operands],
                dma((12,)),
                pltpu.VMEM((2, 40, 128), f32),
                pltpu.VMEM((2, 8, 128), f32),
                pltpu.VMEM((2, 40, 128), f32),
                pltpu.VMEM((2, 8, 128), f32),
                pltpu.VMEM((4, 16, 128), f32),
                pltpu.VMEM((2, 2, 16, 128), f32),
                pltpu.VMEM((2, 2, 8, 128), f32),
                pltpu.VMEM((2, 2, 16, 128), f32),
                pltpu.VMEM((2, 2, 8, 128), f32),
                pltpu.VMEM((2, 16, 128), f32),
                pltpu.VMEM((2, 8, 128), f32),
                dma((4,)), dma((2, 4)), dma((4,)), dma((4,)), pltpu.SemaphoreType.REGULAR((2,)),
                pltpu.VMEM((256, 128), f32),
                pltpu.VMEM((256, 128), f32),
                pltpu.VMEM((3, 32, 128), f32),
                tile, tile, tile, pltpu.VMEM((8, 128), jnp.int32), tile, tile,
                pltpu.VMEM((128, 128), f32),
                pltpu.VMEM((128, 128), f32),
                pltpu.VMEM((128, (OWN + 3) * 128), f32),
                big(32, bf16), big(32, bf16), big(128, bf16), big(128, bf16), big(128, bf16), big(128, bf16),
                big(128, f32), big(128, f32), big(128, bf16), big(128, bf16), big(128, bf16), big(128, bf16),
                pltpu.VMEM((owners * size, 128), f32),
                pltpu.VMEM((nsu * owners - 1 if direct else ncs - 1, size, 128), f32),
                pltpu.VMEM((size, 128), f32),
                pltpu.VMEM((1 if direct else nal, size, 128), f32),
                dma((2 if direct else max(ncs, nal) - 1,)), dma((1 if direct else ncs - 1,)),
                dma((1 if direct else nal - 1,)), dma((1 if direct else ncs - 1,)),
            ],
            compiler_params=pltpu.CompilerParams(collective_id=0, has_side_effects=True),
        )(*operands)
        gs, gw1, gb1, gw2, gb2, gwo, gbo = pl.pallas_call(
            unpack,
            out_shape=(
                jax.ShapeDtypeStruct((12, 8, 128), f32),
                jax.ShapeDtypeStruct((32, 128), f32),
                jax.ShapeDtypeStruct((1, 128), f32),
                jax.ShapeDtypeStruct((128, 128), f32),
                jax.ShapeDtypeStruct((1, 128), f32),
                jax.ShapeDtypeStruct((8, 128), f32),
                jax.ShapeDtypeStruct((1, 8), f32),
            ),
            in_specs=[vmem] * 2,
            out_specs=(hbm,) * 7,
            scratch_shapes=[pltpu.VMEM((1, 8), f32), dma((7,))],
        )(*[pltpu.with_memory_space_constraint(x, pltpu.VMEM) for x in out])
        return gs, gw1, gb1.reshape(128), gw2, gb2.reshape(128), gwo.T, gbo.reshape(8)

    tile = P(None, ("groups", "along"), ("cross", "sub"))
    return jax.shard_map(
        per_device,
        mesh=mesh,
        in_specs=(
            tile, tile, tile, tile, P(("groups", "along"), ("cross", "sub")),
            P(), P(), P(), P(), P(), P(), tile,
        ),
        out_specs=(
            tile, P("groups", None), P("groups"), P("groups", None), P("groups"),
            P("groups", None), P("groups"),
        ),
        check_vma=False,
    )
```

```python
import functools
import math

import jax
import jax.numpy as jnp
from jax import lax
from jax.experimental import pallas as pl
from jax.experimental.pallas import tpu as pltpu
from jax.sharding import PartitionSpec as P

MESH = pl.DeviceIdType.MESH
f32 = jnp.float32
bf16 = jnp.bfloat16
diffusion = 0.15
advection = 0.2
friction = 0.05
pickup_gain = 0.5
settling = 0.2
bed_diffusion = 0.1

ROW_W1 = 128
ROW_WO = 160
ROW_BIAS = 168
ROWS = 176
ROW_OF_UNIT = (1, 2, 3, 4, 5, 6, 0, 7)
INNER = 6
OWN = 8
STRIP = 8
NEXT = 16
STORM = 28
COL_STORM = 32
COL_MASK = 44


def split(x):
    high = x.astype(bf16)
    low = (x - high.astype(f32)).astype(bf16)
    return high, low


def mm(a, b):
    return lax.dot_general(a, b, (((1,), (0,)), ((), ())), preferred_element_type=f32)


def mm_nt(a, b):
    return lax.dot_general(a, b, (((1,), (1,)), ((), ())), preferred_element_type=f32)


def beside(high, low, *extra):
    return jnp.concatenate([high, high, *extra, low], axis=1)


def bias_columns(spread):
    high = spread.astype(bf16)
    rest = spread - high.astype(f32)
    middle = rest.astype(bf16)
    low = (rest - middle.astype(f32)).astype(bf16)
    lane = lax.broadcasted_iota(jnp.int32, spread.shape, 1)
    out = jnp.zeros_like(spread)
    for i, part in enumerate((high, middle, low)):
        out = jnp.where(lane == i, part.astype(f32), out)
    return out[:, :16].astype(bf16)


def silu(u):
    a = 1.0 + jnp.tanh(u)
    return a, u * a


def slope(a, h):
    return h * (2.0 - a) + a


def softplus(z):
    return jnp.maximum(z, 0.0) + jnp.log(1.0 + jnp.exp(-jnp.abs(z)))


def kernel(
    nal, ncr, nsu, near_only, direct, factor,
    state_hbm, cid_hbm, w1_hbm, b1_hbm, w2_hbm, b2_hbm, wo_hbm, bo_hbm,
    storm_hbm, wet_hbm, dune_hbm, cot_hbm,
    gstate_ref, full_ref,
    state_ref, cid_ref, w1_ref, b1_ref, w2_ref, b2_ref, wo_ref, bo_ref,
    storm_ref, wet_ref, dune_ref, cot_ref, load_sem,
    snd0_row, snd0_col, rcv0_row, rcv0_col, rcv_diag,
    snd_row, snd_col, rcv_row, rcv_col, ring_row, ring_col,
    edge_send, edge_recv, diag_send, diag_recv, relay_sem,
    feat_ref, dfeat_ref, fx_ref, z_ref, zx_ref, dz_ref, cidx_ref, wetx_ref, dunex_ref,
    wsel_ref, h2f_ref,
    f_ref, h1_ref, h2_ref, act1_ref, q2_ref, d1_ref, d2_ref,
    acc_ref, rcv_a, src_b, rcv_b,
    sum_send, sa_recv, sb_recv, sc_recv,
):
    ncs = ncr * nsu
    g = lax.axis_index("groups")
    al = lax.axis_index("along")
    cr = lax.axis_index("cross")
    su = lax.axis_index("sub")
    cs = cr * nsu + su

    def dev(a, c):
        return (g, a, c // nsu, c % nsu)

    has_dst = (al > 0, al < nal - 1, cs > 0, cs < ncs - 1)
    has_src = (al < nal - 1, al > 0, cs < ncs - 1, cs > 0)
    dst_dev = (
        dev(al - 1, cs), dev(al + 1, cs), dev(al, cs - 1), dev(al, cs + 1),
    )
    corners = ((0, 2), (0, 3), (1, 2), (1, 3))
    diag_dst = [jnp.logical_and(has_dst[a], has_dst[c]) for a, c in corners]
    diag_src = [jnp.logical_and(has_src[a], has_src[c]) for a, c in corners]
    diag_dev = [dev(al + (1 if a else -1), cs + (1 if c == 3 else -1)) for a, c in corners]

    loads = [
        pltpu.make_async_copy(src, dst, load_sem.at[i])
        for i, (src, dst) in enumerate((
            (state_hbm, state_ref), (storm_hbm, storm_ref), (wet_hbm, wet_ref), (dune_hbm, dune_ref),
            (cid_hbm, cid_ref), (w1_hbm, w1_ref), (b1_hbm, b1_ref), (w2_hbm, w2_ref),
            (b2_hbm, b2_ref), (wo_hbm, wo_ref), (bo_hbm, bo_ref), (cot_hbm, cot_ref),
        ))
    ]
    for load in loads[:5]:
        load.start()
    for ref in (rcv0_row, rcv0_col, rcv_diag, rcv_row, rcv_col):
        ref[...] = jnp.zeros_like(ref)

    barrier = pltpu.get_barrier_semaphore()
    for e in range(4):
        @pl.when(diag_dst[e])
        def _():
            pl.semaphore_signal(barrier, inc=1, device_id=diag_dev[e], device_id_type=MESH)
    if near_only:
        for d in range(4):
            @pl.when(has_dst[d])
            def _():
                pl.semaphore_signal(barrier, inc=1, device_id=dst_dev[d], device_id_type=MESH)
    else:
        for j in range(1, ncs):
            pl.semaphore_signal(
                barrier, inc=1, device_id=dev(al, lax.rem(cs + j, ncs)), device_id_type=MESH
            )
        for j in range(1, nal):
            pl.semaphore_signal(
                barrier, inc=1, device_id=dev(lax.rem(al + j, nal), cs), device_id_type=MESH
            )
    for load in loads[5:]:
        load.start()
    beside_al = (al + nal - 1) // nal + (2 * nal - 2 - al) // nal
    beside_cs = (cs + ncs - 1) // ncs + (2 * ncs - 2 - cs) // ncs

    row = lax.broadcasted_iota(jnp.int32, (8, 128), 0)
    lane = lax.broadcasted_iota(jnp.int32, (8, 128), 1)
    field = lax.broadcasted_iota(jnp.int32, (16, 128), 0)
    lane16 = lax.broadcasted_iota(jnp.int32, (16, 128), 1)

    def turn(x, shift, axis):
        shift = shift % x.shape[axis]
        return pltpu.roll(x, shift, axis) if shift else x

    def copy0_of(d):
        src, dst = (snd0_row, rcv0_row) if d < 2 else (snd0_col, rcv0_col)
        return pltpu.make_async_remote_copy(
            src_ref=src.at[d % 2], dst_ref=dst.at[d % 2], send_sem=edge_send.at[d],
            recv_sem=edge_recv.at[0, d], device_id=dst_dev[d], device_id_type=MESH,
        )

    def diag_of(e):
        return pltpu.make_async_remote_copy(
            src_ref=snd0_row.at[e // 2, pl.ds(0, 16)], dst_ref=rcv_diag.at[e],
            send_sem=diag_send.at[e], recv_sem=diag_recv.at[e],
            device_id=diag_dev[e], device_id_type=MESH,
        )

    def copy_of(k, d):
        src, dst = (snd_row, rcv_row) if d < 2 else (snd_col, rcv_col)
        return pltpu.make_async_remote_copy(
            src_ref=src.at[k - 1, d % 2], dst_ref=dst.at[k - 1, d % 2], send_sem=edge_send.at[d],
            recv_sem=edge_recv.at[k % 2, d], device_id=dst_dev[d], device_id_type=MESH,
        )

    around = beside_al + beside_cs + beside_al * beside_cs

    def relay(k):
        if near_only:
            for flags, devices in ((has_dst, dst_dev), (diag_dst, diag_dev)):
                each(flags, lambda i: pl.semaphore_signal(
                    relay_sem.at[k], inc=1, device_id=devices[i], device_id_type=MESH))

    def relayed(k):
        if near_only:
            pl.semaphore_wait(relay_sem.at[k], around)

    def each(flags, action):
        for i in range(4):
            @pl.when(flags[i])
            def _():
                action(i)

    def fill(k, xn, xs, xw, xe):
        west = jnp.zeros((8, 128), f32)
        east = jnp.zeros((8, 128), f32)
        for f in range(12):
            snd_row[k - 1, 0, f:f + 1, :] = xn[f][0:1, :]
            snd_row[k - 1, 1, f:f + 1, :] = xs[f][7:8, :]
            west = jnp.where(lane == f, turn(xw[f], f, 1), west)
            east = jnp.where(lane == f, turn(xe[f], f + 1, 1), east)
        snd_col[k - 1, 0] = west
        snd_col[k - 1, 1] = east

    class Halo:
        def __init__(self, rows, cols):
            self.rows, self.cols = rows, cols

        def south(self, x, f):
            return jnp.where(row == 7, self.rows[0, f:f + 1, :], turn(x, 7, 0))

        def north(self, x, f):
            return jnp.where(row == 0, self.rows[1, f:f + 1, :], turn(x, 1, 0))

        def east(self, x, f):
            return jnp.where(lane == 127, turn(self.cols[0], 127 - f, 1), turn(x, 127, 1))

        def west(self, x, f):
            return jnp.where(lane == 0, turn(self.cols[1], -f, 1), turn(x, 1, 1))

        def around(self, x, f):
            return self.north(x, f), self.south(x, f), self.west(x, f), self.east(x, f)

    for load in loads[:5]:
        load.wait()
    V0 = [state_ref[f * 8:(f + 1) * 8, :] for f in range(12)]
    storm = [storm_ref[f * 8:(f + 1) * 8, :] for f in range(12)]
    wets = [wet_ref[t * 8:(t + 1) * 8, :].astype(f32) for t in range(2)]
    dunes = [dune_ref[t * 8:(t + 1) * 8, :].astype(f32) for t in range(2)]
    wash = [1.0 - dunes[t] for t in range(2)]
    cid = cid_ref[...]
    masks = [wets[0], dunes[0], cid.astype(f32)]
    for d, edge, inner in ((0, 0, 1), (1, 7, 6)):
        for f in range(12):
            snd0_row[d, f:f + 1, :] = V0[f][edge:edge + 1, :]
            snd0_row[d, NEXT + f:NEXT + f + 1, :] = V0[f][inner:inner + 1, :]
            snd0_row[d, STORM + f:STORM + f + 1, :] = storm[f][edge:edge + 1, :]
        for m in range(3):
            snd0_row[d, 12 + m:13 + m, :] = masks[m][edge:edge + 1, :]
        snd0_row[d, 15:16, :] = jnp.zeros((1, 128), f32)
    for d, edge, inner in ((0, 0, 1), (1, 127, 126)):
        out = jnp.zeros((8, 128), f32)
        for x, at, c in (
            [(V0[f], f, edge) for f in range(12)] + [(V0[f], NEXT + f, inner) for f in range(12)]
            + [(storm[f], COL_STORM + f, edge) for f in range(12)]
            + [(masks[m], COL_MASK + m, edge) for m in range(3)]
        ):
            out = jnp.where(lane == at, turn(x, at - c, 1), out)
        snd0_col[d] = out
    if near_only:
        pl.semaphore_wait(barrier, around)
    else:
        pl.semaphore_wait(barrier, ncs - 1 + nal - 1 + beside_al * beside_cs)
    each(has_dst, lambda d: copy0_of(d).start())
    each(diag_dst, lambda e: diag_of(e).start())
    for load in loads[5:]:
        load.wait()

    w1 = w1_ref[...]
    w1t = jnp.transpose(jnp.concatenate([w1, jnp.zeros((96, 128), f32)], axis=0))[:, :32]
    w2 = w2_ref[...]
    w1_cat = beside(*split(w1))
    w2_cat = beside(*split(0.5 * w2))
    b1_cols = bias_columns(0.5 * jnp.transpose(jnp.broadcast_to(b1_ref[...], (128, 128))))
    b2_cols = bias_columns(0.5 * jnp.transpose(jnp.broadcast_to(b2_ref[...], (128, 128))))
    w1t_cat = beside(*split(0.5 * w1t), b1_cols)
    w2t_cat = beside(*split(0.5 * jnp.transpose(w2)), b2_cols)
    wo_t = jnp.transpose(jnp.concatenate([wo_ref[...], jnp.zeros((120, 128), f32)], axis=0))[:, :8]

    def choose(unit, ids):
        onehot = (row == ids).astype(f32)
        wsel_ref[:, unit * 128:(unit + 1) * 128] = lax.dot_general(
            wo_t, onehot, (((1,), (0,)), ((), ())),
            precision=lax.Precision.HIGHEST, preferred_element_type=f32,
        )

    def bias_of(ids):
        b = jnp.zeros((8, 128), f32)
        for k in range(8):
            b = jnp.where(ids == k, bo_ref[0:1, k:k + 1], b)
        return b

    for u in range(OWN):
        choose(u, cid[ROW_OF_UNIT[u]:ROW_OF_UNIT[u] + 1, :])
    bsel = bias_of(cid)

    all_units = list(range(OWN))
    inner_units = list(range(INNER))
    edge_units = [INNER, INNER + 1, STRIP]

    def pairs(units):
        return [units[i:i + 2] for i in range(0, len(units), 2)]

    def layers(t, unit, feats, kept):
        n = len(feats)
        at = pl.ds(unit * 128, n * 128)
        ones = jnp.ones((16, n * 128), bf16)
        F = jnp.concatenate(feats, axis=1) if n > 1 else feats[0]
        Fh, Fl = split(F)
        a, h = silu(mm(w1t_cat, jnp.concatenate([Fh, Fl, ones, Fh], axis=0)))
        Hh, Hl = split(h)
        if kept:
            f_ref[t, 0:32, at] = Fh
            f_ref[t, 32:64, at] = Fl
            act1_ref[t, :, at] = slope(a, h)
            h1_ref[t, 0:128, at] = Hh
            h1_ref[t, 128:256, at] = Hl
        a, h = silu(mm(w2t_cat, jnp.concatenate([Hh, Hl, ones, Hh], axis=0)))
        wsel = wsel_ref[:, at]
        if kept:
            q2_ref[t, :, at] = wsel * slope(a, h)
            h2f_ref[t, :, at] = h
        z = jnp.sum(wsel * h, axis=0, keepdims=True)
        return [z[:, i * 128:(i + 1) * 128] for i in range(n)]

    def settle(t, units):
        for part in pairs(units):
            at = pl.ds(part[0] * 128, len(part) * 128)
            Hh, Hl = split(h2f_ref[t, :, at])
            h2_ref[t, 0:128, at] = Hh
            h2_ref[t, 128:256, at] = Hl

    def put_features(V, near):
        for f in range(4):
            for part, x in enumerate((V[f],) + tuple(near[f])):
                feat_ref[(4 * part + f) * 8:(4 * part + f + 1) * 8, :] = x

    def own_layers(t, first, last):
        for u in range(first, last, 2):
            rows = ROW_OF_UNIT[u:u + 2]
            feats = [feat_ref[pl.ds(r, 32, stride=8), :] for r in rows]
            for r, z in zip(rows, layers(t, u, feats, True)):
                z_ref[r:r + 1, :] = z

    feat_ref[160:256, :] = storm_ref[...]
    put_features(V0, [
        (turn(V0[f], 1, 0), turn(V0[f], 7, 0), turn(V0[f], 1, 1), turn(V0[f], 127, 1)) for f in range(4)
    ])
    own_layers(0, 0, INNER)
    settle(0, inner_units)
    for ref, rows in ((f_ref, 64), (h1_ref, 256)):
        ref[:, rows:rows + 16, :] = jnp.ones((2, 16, ref.shape[2]), bf16)
    for ref in (zx_ref, cidx_ref, wetx_ref, dunex_ref):
        ref[...] = jnp.zeros_like(ref)
    spare = acc_ref.shape[0] - ROWS
    if spare:
        acc_ref[ROWS:, :] = jnp.zeros((spare, 128), f32)

    each(has_src, lambda d: copy0_of(d).wait_recv())
    each(diag_src, lambda e: diag_of(e).wait_recv())
    relay(0)

    halo0 = Halo(rcv0_row, rcv0_col)
    near0 = [halo0.around(V0[f], f) for f in range(12)]
    put_features(V0, near0)
    sides = jnp.concatenate(
        [rcv0_col[1], rcv0_col[0], snd0_col[0], snd0_col[1], jnp.zeros((96, 128), f32)], axis=0
    )
    T = jnp.transpose(sides)
    SE, SW, NE, NW = [rcv_diag[e] for e in range(4)]
    RS, RN = rcv0_row[0, 0:16, :], rcv0_row[1, 0:16, :]
    group = lane16 // 8
    V, far = T[0:16], T[NEXT:NEXT + 16]
    plus, minus = turn(V, 16, 1), turn(V, -16, 1)
    N, S = turn(V, 1, 1), turn(V, -1, 1)
    for at, x, c in ((0, NW, 127), (8, NE, 0), (16, RN, 0), (24, RN, 127)):
        N = jnp.where(lane16 == at, turn(x, at - c, 1), N)
    for at, x, c in ((7, SW, 127), (15, SE, 0), (23, RS, 0), (31, RS, 127)):
        S = jnp.where(lane16 == at, turn(x, at - c, 1), S)
    W = jnp.where(group == 1, minus, jnp.where(group == 2, plus, far))
    E = jnp.where(group == 0, minus, jnp.where(group == 3, plus, far))
    outer = [(V, N, S, W, E)]
    for V, N, S, west, east in (
        (RN, rcv0_row[1, NEXT:NEXT + 16, :], snd0_row[0, 0:16, :], NW, NE),
        (RS, snd0_row[1, 0:16, :], rcv0_row[0, NEXT:NEXT + 16, :], SW, SE),
    ):
        W = jnp.where(lane16 == 0, turn(west, 1, 1), turn(V, 1, 1))
        E = jnp.where(lane16 == 127, turn(east, 127, 1), turn(V, 127, 1))
        outer.append((V, N, S, W, E))
    storms = [T[COL_STORM:COL_STORM + 12], rcv0_row[1, STORM:STORM + 12, :], rcv0_row[0, STORM:STORM + 12, :]]
    mask_rows = [
        [T[COL_MASK + m:COL_MASK + m + 1] for m in range(3)],
        [rcv0_row[1, 12 + m:13 + m, :] for m in range(3)],
        [rcv0_row[0, 12 + m:13 + m, :] for m in range(3)],
    ]
    for w in range(3):
        for part in range(5):
            fx_ref[w, 4 * part:4 * part + 4, :] = outer[w][part][0:4]
        fx_ref[w, 20:32, :] = storms[w]
        wetx_ref[w:w + 1, :] = mask_rows[w][0]
        dunex_ref[w:w + 1, :] = mask_rows[w][1]
        ids = mask_rows[w][2].astype(jnp.int32)
        cidx_ref[w:w + 1, :] = ids
        choose(STRIP + w, ids)
    cidx = cidx_ref[...]
    own_layers(0, INNER, OWN)
    zx_ref[0:1, :] = layers(0, STRIP, [fx_ref[0]], True)[0]
    zx_ref[1:2, :], zx_ref[2:3, :] = layers(0, STRIP + 1, [fx_ref[1], fx_ref[2]], False)
    zx = zx_ref[...] + bias_of(cidx)
    pickx = pickup_gain * softplus(zx) * (1.0 - dunex_ref[...])

    def from_strip(x, start):
        return jnp.sum(jnp.where(lane == start + row, x, 0.0), axis=1, keepdims=True)

    inside = jnp.logical_and(row > 0, row < 7)
    at_west = jnp.logical_and(inside, lane == 0)
    at_east = jnp.logical_and(inside, lane == 127)
    z0 = z_ref[...] + bsel
    z0 = jnp.where(at_west, from_strip(zx[0:1, :], 16), z0)
    z0 = jnp.where(at_east, from_strip(zx[0:1, :], 24), z0)

    def advanced(w):
        V, N, S, W, E = outer[w]
        pick, wet = pickx[w:w + 1, :], wetx_ref[w:w + 1, :]
        lap = N + S + W + E - 4.0 * V
        ad, cd = S - N, E - W
        spread = jnp.where(field == 3, bed_diffusion, diffusion) * lap
        sediment = spread - advection * (V[1:2] * ad + V[2:3] * cd) - settling * V
        sediment = sediment + jnp.where(field - 4 == cidx[w:w + 1, :], pick, 0.0)
        total = jnp.sum(
            jnp.where(jnp.logical_and(field >= 4, field < 12), V, 0.0), axis=0, keepdims=True
        )
        first = jnp.where(field == 0, -advection * (ad[1:2] + cd[2:3]), settling * total - pick)
        first = jnp.where(field == 1, -advection * ad[0:1] - friction * V[1:2], first)
        first = jnp.where(field == 2, -advection * cd[0:1] - friction * V[2:3], first)
        return V + wet * jnp.where(field < 4, spread + first, sediment)

    ring_row[1] = advanced(1)
    ring_row[0] = advanced(2)
    back = jnp.transpose(jnp.concatenate([advanced(0), jnp.zeros((112, 128), f32)], axis=0))
    ring_col[1] = back[0:8]
    ring_col[0] = back[8:16]

    pickup = softplus(z0) * wash[0]
    lap = []
    for f in range(12):
        n, s, w, e = near0[f]
        lap.append(n + s + w + e - 4.0 * V0[f])
    total = V0[4]
    for k in range(1, 8):
        total = total + V0[4 + k]
    ad = [near0[f][1] - near0[f][0] for f in range(12)]
    cd = [near0[f][3] - near0[f][2] for f in range(12)]
    tend = [
        diffusion * lap[0] - advection * (ad[1] + cd[2]),
        diffusion * lap[1] - advection * ad[0] - friction * V0[1],
        diffusion * lap[2] - advection * cd[0] - friction * V0[2],
        bed_diffusion * lap[3] - pickup_gain * pickup + settling * total,
    ]
    for k in range(8):
        x = diffusion * lap[4 + k] - advection * (V0[1] * ad[4 + k] + V0[2] * cd[4 + k])
        x = x + jnp.where(cid == k, pickup_gain * pickup, 0.0) - settling * V0[4 + k]
        tend.append(x)
    V1 = [V0[f] + wets[0] * tend[f] for f in range(12)]

    halo1 = Halo(ring_row, ring_col)
    near1 = [halo1.around(V1[f], f) for f in range(12)]
    put_features(V1, near1)
    own_layers(1, 0, OWN)
    relayed(0)
    relay(1)
    z1 = z_ref[...] + bsel
    lam2 = [cot_ref[f * 8:(f + 1) * 8, :] for f in range(12)]

    def closure_cotangent(t, gate, lam):
        G = [None] * 3 + [wets[t] * lam[f] for f in range(3, 12)]
        picked = G[4]
        for k in range(1, 8):
            picked = jnp.where(cid == k, G[4 + k], picked)
        return pickup_gain * (picked - G[3]) * wash[t] * gate

    def sigmoid(z):
        return 1.0 / (1.0 + jnp.exp(-z))

    def adjoint_two(t, units, drows):
        for part in pairs(list(zip(units, drows))):
            at = pl.ds(part[0][0] * 128, len(part) * 128)
            drow = 0.5 * jnp.concatenate([d for _, d in part], axis=1)
            Dh, Dl = split(q2_ref[t, :, at] * drow)
            d2_ref[t, 0:128, at] = Dh
            d2_ref[t, 128:256, at] = Dl

    def adjoint_one(t, units):
        for part in pairs(units):
            at = pl.ds(part[0] * 128, len(part) * 128)
            d1 = mm(w2_cat, jnp.concatenate([d2_ref[t, :, at], d2_ref[t, 0:128, at]], axis=0))
            Dh, Dl = split(d1 * act1_ref[t, :, at])
            d1_ref[t, 0:128, at] = Dh
            d1_ref[t, 128:256, at] = Dl

    def feature_cotangent(t, units):
        out = []
        for part in pairs(units):
            at = pl.ds(part[0] * 128, len(part) * 128)
            dF = mm(w1_cat, jnp.concatenate([d1_ref[t, :, at], d1_ref[t, 0:128, at]], axis=0))
            for i, u in enumerate(part):
                one = dF[:, i * 128:(i + 1) * 128]
                if u < OWN:
                    dfeat_ref[pl.ds(ROW_OF_UNIT[u], 32, stride=8), :] = one
                else:
                    out.append(one)
        return out

    def adjoint_cells(D, G, near, V, lam):
        lap = [bed_diffusion if f == 3 else diffusion for f in range(12)]
        lg = [lap[f] * G[f] for f in range(12)]
        c = [lam[f] - 4.0 * lg[f] for f in range(12)]
        alongs = jnp.zeros((8, 128), f32)
        crosses = jnp.zeros((8, 128), f32)
        along_part = [advection * G[1], advection * G[0], None, None]
        cross_part = [advection * G[2], None, advection * G[0], None]
        for k in range(8):
            n, s, w, e = near[4 + k]
            alongs = alongs + (s - n) * G[4 + k]
            crosses = crosses + (e - w) * G[4 + k]
            c[4 + k] = c[4 + k] + settling * (G[3] - G[4 + k])
            ag = advection * G[4 + k]
            along_part.append(V[1] * ag)
            cross_part.append(V[2] * ag)
        c[1] = c[1] - friction * G[1] - advection * alongs
        c[2] = c[2] - friction * G[2] - advection * crosses
        to = [[], [], [], []]
        for f in range(12):
            for d, part, sign in ((0, along_part, 1), (1, along_part, -1), (2, cross_part, 1), (3, cross_part, -1)):
                x = lg[f]
                if part[f] is not None:
                    x = x + part[f] if sign > 0 else x - part[f]
                if f < 4:
                    x = x + D[4 + 4 * d + f]
                to[d].append(x)
            if f < 4:
                c[f] = c[f] + D[f]
        return c, to

    def gather(c, to, halo):
        return [
            c[f] + halo.south(to[0][f], f) + halo.north(to[1][f], f)
            + halo.east(to[2][f], f) + halo.west(to[3][f], f)
            for f in range(12)
        ]

    def keep(start, part, first):
        at = pl.ds(start, part.shape[0])
        acc_ref[at, :] = part if first else acc_ref[at, :] + part

    def weights_two(t, units, ids, drows, first):
        at = pl.ds(units[0] * 128, len(units) * 128)
        width = len(units) * 128
        dr = jnp.concatenate(
            [jnp.where(row == k, d, 0.0) for k, d in zip(ids, drows)], axis=1
        )
        dbo = jnp.sum(
            jnp.where(row == lane, jnp.sum(dr, axis=1, keepdims=True), 0.0), axis=0, keepdims=True
        )
        drh, drl = split(jnp.concatenate([dr, jnp.zeros((8, width), f32)], axis=0))
        top = mm_nt(jnp.concatenate([drh, drl], axis=0), h2_ref[t, :, at])
        dwo = top[:8, :128] + top[16:24, :128] + top[:8, 128:]
        top = mm_nt(h1_ref[t, :, at], d2_ref[t, :, at])
        keep(0, top[:128, :128] + top[128:256, :128] + top[:128, 128:], first)
        keep(ROW_WO, dwo, first)
        ones = top[256:264, :128] + top[256:264, 128:]
        keep(ROW_BIAS, jnp.where(row == 1, ones, jnp.where(row == 2, dbo, 0.0)), first)

    def weights_one(t, units, first):
        at = pl.ds(units[0] * 128, len(units) * 128)
        top = mm_nt(f_ref[t, :, at], d1_ref[t, :, at])
        keep(ROW_W1, top[:32, :128] + top[32:64, :128] + top[:32, 128:], first)
        ones = top[64:72, :128] + top[64:72, 128:]
        keep(ROW_BIAS, jnp.where(row == 0, ones, 0.0), False)

    def rows_of(x, units):
        return [x[ROW_OF_UNIT[u]:ROW_OF_UNIT[u] + 1, :] for u in units]

    G1 = [wets[1] * lam2[f] for f in range(12)]
    dz1 = closure_cotangent(1, sigmoid(z1), lam2)
    dz_ref[...] = dz1
    drows1 = rows_of(dz_ref, all_units)
    adjoint_two(1, all_units, drows1)
    adjoint_one(1, all_units)
    feature_cotangent(1, all_units)
    D1 = [dfeat_ref[f * 8:(f + 1) * 8, :] for f in range(20)]
    c1, to1 = adjoint_cells(D1, G1, near1, V1, lam2)
    fill(1, *to1)
    each(has_dst, lambda d: copy0_of(d).wait_send())
    each(has_dst, lambda d: copy_of(1, d).start())

    gate0 = sigmoid(z0)
    settle(1, all_units)
    settle(0, edge_units)
    weights_two(1, all_units, rows_of(cid, all_units), drows1, True)
    weights_one(1, all_units, True)
    lam1 = [
        c1[f] + turn(to1[0][f], 7, 0) + turn(to1[1][f], 1, 0) + turn(to1[2][f], 127, 1) + turn(to1[3][f], 1, 1)
        for f in range(12)
    ]
    dz0 = closure_cotangent(0, gate0, lam1)
    dz0 = jnp.where(jnp.logical_and(lane > 0, lane < 127), dz0, 0.0)
    dz_ref[...] = dz0
    drows0 = rows_of(dz_ref, inner_units)
    adjoint_two(0, inner_units, drows0)
    weights_two(0, inner_units, rows_of(cid, inner_units), drows0, False)
    adjoint_one(0, inner_units)
    weights_one(0, inner_units, False)
    feature_cotangent(0, inner_units)

    each(has_src, lambda d: copy_of(1, d).wait_recv())
    relayed(1)
    lam1 = gather(c1, to1, Halo(rcv_row.at[0], rcv_col.at[0]))
    dz0 = closure_cotangent(0, gate0, lam1)
    dstrip = jnp.where(lane == 16 + row, dz0[:, 0:1], jnp.where(lane == 24 + row, dz0[:, 127:128], 0.0))
    dstrip = jnp.sum(jnp.where(inside, dstrip, 0.0), axis=0, keepdims=True)
    drows0 = [dz0[0:1, :], dz0[7:8, :], dstrip]
    ids0 = [cid[0:1, :], cid[7:8, :], cidx_ref[0:1, :]]
    adjoint_two(0, edge_units, drows0)
    weights_two(0, edge_units, ids0, drows0, False)
    adjoint_one(0, edge_units)
    weights_one(0, edge_units, False)

    size = src_b.shape[0]
    last_core = nsu - 1
    owner = su == last_core
    piece = al * ncr + cr if direct else cs
    mine = pl.ds(pl.multiple_of(piece * size, 8), size)
    spans = [(dz, dx) for dz in range(nal) for dx in range(ncr)]

    def chip_at(span):
        return lax.rem(al + span[0], nal), lax.rem(cr + span[1], ncr)

    def to_owner(k):
        a, c = chip_at(spans[k])
        slot = 2 * (k - 1) + su if k else 2 * (len(spans) - 1)
        at = pl.ds(pl.multiple_of((a * ncr + c) * size, 8), size)
        return pltpu.make_async_remote_copy(
            src_ref=acc_ref.at[at, :], dst_ref=rcv_a.at[slot], send_sem=sum_send.at[0],
            recv_sem=sa_recv.at[0], device_id=(g, a, c, last_core), device_id_type=MESH,
        )

    def from_owner(k, core):
        a, c = chip_at(spans[k])
        return pltpu.make_async_remote_copy(
            src_ref=full_ref.at[mine, :], dst_ref=full_ref.at[mine, :], send_sem=sum_send.at[1],
            recv_sem=sc_recv.at[0], device_id=(g, a, c, core), device_id_type=MESH,
        )

    def all_of(ref, sem):
        return pltpu.make_async_remote_copy(
            src_ref=ref, dst_ref=ref, send_sem=sem, recv_sem=sem,
            device_id=(g, al, cr, nsu - 1 - su), device_id_type=MESH,
        )

    def copy_a(j):
        peer = lax.rem(cs + j, ncs)
        return pltpu.make_async_remote_copy(
            src_ref=acc_ref.at[pl.ds(pl.multiple_of(peer * size, 8), size), :],
            dst_ref=rcv_a.at[j - 1], send_sem=sum_send.at[j - 1], recv_sem=sa_recv.at[j - 1],
            device_id=dev(al, peer), device_id_type=MESH,
        )

    def copy_b(j):
        return pltpu.make_async_remote_copy(
            src_ref=src_b, dst_ref=rcv_b.at[al], send_sem=sum_send.at[j - 1],
            recv_sem=sb_recv.at[j - 1],
            device_id=dev(lax.rem(al + j, nal), cs), device_id_type=MESH,
        )

    def copy_c(j):
        return pltpu.make_async_remote_copy(
            src_ref=full_ref.at[mine, :], dst_ref=full_ref.at[mine, :],
            send_sem=sum_send.at[j - 1], recv_sem=sc_recv.at[j - 1],
            device_id=dev(al, lax.rem(cs + j, ncs)), device_id_type=MESH,
        )

    others = len(spans) - 1
    if direct:
        for k in range(others, 0, -1):
            to_owner(k).start()

        @pl.when(jnp.logical_not(owner))
        def _():
            to_owner(0).start()
    else:
        for j in range(1, ncs):
            copy_a(j).start()

    strip_back = feature_cotangent(0, edge_units)[0]
    turned = jnp.transpose(jnp.concatenate([strip_back, jnp.zeros((96, 128), f32)], axis=0))
    at_w, at_e = turned[16:24], turned[24:32]
    D0 = []
    for f in range(20):
        x = dfeat_ref[f * 8:(f + 1) * 8, :]
        x = jnp.where(at_west, turn(at_w, -f, 1), x)
        D0.append(jnp.where(at_east, turn(at_e, 127 - f, 1), x))
    G0 = [wets[0] * lam1[f] for f in range(12)]
    c0, to0 = adjoint_cells(D0, G0, near0, V0, lam1)
    fill(2, *to0)
    each(has_dst, lambda d: copy_of(1, d).wait_send())
    each(has_dst, lambda d: copy_of(2, d).start())

    if direct:
        @pl.when(owner)
        def _():
            all_of(rcv_a, sa_recv.at[0]).wait_recv()
            total = acc_ref[mine, :]
            for j in range(rcv_a.shape[0]):
                total = total + rcv_a[j]
            full_ref[mine, :] = total * factor
            for k in range(others, -1, -1):
                for core in range(nsu):
                    if k or core != last_core:
                        from_owner(k, core).start()
    else:
        total = acc_ref[mine, :]
        for j in range(1, ncs):
            copy_a(j).wait_recv()
            total = total + rcv_a[j - 1]
        src_b[...] = total
        rcv_b[al] = total
        for j in range(1, ncs):
            copy_a(j).wait_send()
        for j in range(1, nal):
            copy_b(j).start()
    each(has_src, lambda d: copy_of(2, d).wait_recv())
    last = gather(c0, to0, Halo(rcv_row.at[1], rcv_col.at[1]))
    for f in range(12):
        gstate_ref[f] = last[f]
    each(has_dst, lambda d: copy_of(2, d).wait_send())
    each(diag_dst, lambda e: diag_of(e).wait_send())
    if direct:
        @pl.when(owner)
        def _():
            all_of(acc_ref.at[pl.ds(0, others * size), :], sum_send.at[0]).wait_send()
            all_of(full_ref.at[pl.ds(0, others * size), :], sc_recv.at[0]).wait_recv()
            all_of(rcv_a, sum_send.at[1]).wait_send()

        @pl.when(jnp.logical_not(owner))
        def _():
            all_of(acc_ref, sum_send.at[0]).wait_send()
            all_of(full_ref, sc_recv.at[0]).wait_recv()
    else:
        for j in range(1, nal):
            copy_b(j).wait_recv()
        total = rcv_b[0]
        for j in range(1, nal):
            total = total + rcv_b[j]
        full_ref[mine, :] = total * factor
        for j in range(1, nal):
            copy_b(j).wait_send()
        for j in range(1, ncs):
            copy_c(j).start()
        for j in range(1, ncs):
            copy_c(j).wait_recv()
        for j in range(1, ncs):
            copy_c(j).wait_send()


def unpack(
    state_ref, full_ref,
    gs_hbm, gw1_hbm, gb1_hbm, gw2_hbm, gb2_hbm, gwo_hbm, gbo_hbm, gbo_ref, sem,
):
    gbo_ref[...] = full_ref[ROW_BIAS + 2:ROW_BIAS + 3, 0:8]
    parts = (
        (full_ref.at[0:128], gw2_hbm), (state_ref, gs_hbm), (full_ref.at[ROW_W1:ROW_W1 + 32], gw1_hbm),
        (full_ref.at[ROW_WO:ROW_WO + 8], gwo_hbm), (full_ref.at[ROW_BIAS:ROW_BIAS + 1], gb1_hbm),
        (full_ref.at[ROW_BIAS + 1:ROW_BIAS + 2], gb2_hbm), (gbo_ref, gbo_hbm),
    )
    copies = [pltpu.make_async_copy(src, dst, sem.at[i]) for i, (src, dst) in enumerate(parts)]
    for copy in copies:
        copy.start()
    for copy in copies:
        copy.wait()


def solution(mesh):
    nal, ncr, nsu = mesh.shape["along"], mesh.shape["cross"], mesh.shape["sub"]
    ncs = ncr * nsu
    near_only = nal <= 4 and ncs <= 4
    direct = near_only and nsu == 2
    owners = nal * ncr if direct else ncs
    size = 8 * (-(-ROWS // (8 * owners)))

    def per_device(state, storm, wet, dune, cid, w1, b1, w2, b2, wo, bo, cot):
        rows, cols = state.shape[1], state.shape[2]
        factor = 1.0 / math.sqrt(rows * nal * cols * ncs)
        vmem = pl.BlockSpec(memory_space=pltpu.VMEM)
        hbm = pl.BlockSpec(memory_space=pl.ANY)
        flat = lambda x: x.reshape(-1, 128)
        operands = (
            flat(state), cid, w1, b1.reshape(1, 128), w2, b2.reshape(1, 128), wo.T, bo.reshape(1, 8),
            flat(storm), flat(wet), flat(dune), flat(cot),
        )
        dma = pltpu.SemaphoreType.DMA
        tile = pltpu.VMEM((8, 128), f32)
        big = lambda n, kind: pltpu.VMEM((2, n, (OWN + 1) * 128), kind)
        out = pl.pallas_call(
            functools.partial(kernel, nal, ncr, nsu, near_only, direct, factor),
            out_shape=(pltpu.VMEM((12, 8, 128), f32), pltpu.VMEM((owners * size, 128), f32)),
            in_specs=[hbm] * 12,
            out_specs=(vmem,) * 2,
            scratch_shapes=[
                *[pltpu.VMEM(x.shape, x.dtype) for x in operands],
                dma((12,)),
                pltpu.VMEM((2, 40, 128), f32),
                pltpu.VMEM((2, 8, 128), f32),
                pltpu.VMEM((2, 40, 128), f32),
                pltpu.VMEM((2, 8, 128), f32),
                pltpu.VMEM((4, 16, 128), f32),
                pltpu.VMEM((2, 2, 16, 128), f32),
                pltpu.VMEM((2, 2, 8, 128), f32),
                pltpu.VMEM((2, 2, 16, 128), f32),
                pltpu.VMEM((2, 2, 8, 128), f32),
                pltpu.VMEM((2, 16, 128), f32),
                pltpu.VMEM((2, 8, 128), f32),
                dma((4,)), dma((2, 4)), dma((4,)), dma((4,)), pltpu.SemaphoreType.REGULAR((2,)),
                pltpu.VMEM((256, 128), f32),
                pltpu.VMEM((256, 128), f32),
                pltpu.VMEM((3, 32, 128), f32),
                tile, tile, tile, pltpu.VMEM((8, 128), jnp.int32), tile, tile,
                pltpu.VMEM((128, (OWN + 3) * 128), f32), big(128, f32),
                big(80, bf16), big(272, bf16), big(256, bf16), big(128, f32), big(128, f32),
                big(256, bf16), big(256, bf16),
                pltpu.VMEM((owners * size, 128), f32),
                pltpu.VMEM((nsu * owners - 1 if direct else ncs - 1, size, 128), f32),
                pltpu.VMEM((size, 128), f32),
                pltpu.VMEM((1 if direct else nal, size, 128), f32),
                dma((2 if direct else max(ncs, nal) - 1,)), dma((1 if direct else ncs - 1,)),
                dma((1 if direct else nal - 1,)), dma((1 if direct else ncs - 1,)),
            ],
            compiler_params=pltpu.CompilerParams(collective_id=0, has_side_effects=True),
        )(*operands)
        gs, gw1, gb1, gw2, gb2, gwo, gbo = pl.pallas_call(
            unpack,
            out_shape=(
                jax.ShapeDtypeStruct((12, 8, 128), f32),
                jax.ShapeDtypeStruct((32, 128), f32),
                jax.ShapeDtypeStruct((1, 128), f32),
                jax.ShapeDtypeStruct((128, 128), f32),
                jax.ShapeDtypeStruct((1, 128), f32),
                jax.ShapeDtypeStruct((8, 128), f32),
                jax.ShapeDtypeStruct((1, 8), f32),
            ),
            in_specs=[vmem] * 2,
            out_specs=(hbm,) * 7,
            scratch_shapes=[pltpu.VMEM((1, 8), f32), dma((7,))],
        )(*[pltpu.with_memory_space_constraint(x, pltpu.VMEM) for x in out])
        return gs, gw1, gb1.reshape(128), gw2, gb2.reshape(128), gwo.T, gbo.reshape(8)

    tile = P(None, ("groups", "along"), ("cross", "sub"))
    return jax.shard_map(
        per_device,
        mesh=mesh,
        in_specs=(
            tile, tile, tile, tile, P(("groups", "along"), ("cross", "sub")),
            P(), P(), P(), P(), P(), P(), tile,
        ),
        out_specs=(
            tile, P("groups", None), P("groups"), P("groups", None), P("groups"),
            P("groups", None), P("groups"),
        ),
        check_vma=False,
    )
```

```python
import functools
import math

import jax
import jax.numpy as jnp
from jax import lax
from jax.experimental import pallas as pl
from jax.experimental.pallas import tpu as pltpu
from jax.sharding import PartitionSpec as P

MESH = pl.DeviceIdType.MESH
f32 = jnp.float32
bf16 = jnp.bfloat16
diffusion = 0.15
advection = 0.2
friction = 0.05
pickup_gain = 0.5
settling = 0.2
bed_diffusion = 0.1

ROW_W1 = 128
ROW_WO = 160
ROW_BIAS = 168
ROWS = 176
ROW_OF_UNIT = (1, 2, 3, 4, 5, 6, 0, 7)
INNER = 6
DEPTH = 1
OWN = 8
STRIP = 8
NEXT = 16
STORM = 28
COL_STORM = 32
COL_MASK = 44


def split(x):
    high = x.astype(bf16)
    low = (x - high.astype(f32)).astype(bf16)
    return high, low


def mm(a, b):
    return lax.dot_general(a, b, (((1,), (0,)), ((), ())), preferred_element_type=f32)


def mm_nt(a, b):
    return lax.dot_general(a, b, (((1,), (1,)), ((), ())), preferred_element_type=f32)


def beside(high, low, *extra):
    return jnp.concatenate([high, high, *extra, low], axis=1)


def bias_columns(spread):
    high = spread.astype(bf16)
    rest = spread - high.astype(f32)
    middle = rest.astype(bf16)
    low = (rest - middle.astype(f32)).astype(bf16)
    lane = lax.broadcasted_iota(jnp.int32, spread.shape, 1)
    out = jnp.zeros_like(spread)
    for i, part in enumerate((high, middle, low)):
        out = jnp.where(lane == i, part.astype(f32), out)
    return out[:, :16].astype(bf16)


def silu(u):
    a = 1.0 + jnp.tanh(u)
    return a, u * a


def slope(a, h):
    return h * (2.0 - a) + a


def softplus(z):
    return jnp.maximum(z, 0.0) + jnp.log(1.0 + jnp.exp(-jnp.abs(z)))


def kernel(
    nal, ncr, nsu, near_only, direct, factor,
    state_hbm, cid_hbm, w1_hbm, b1_hbm, w2_hbm, b2_hbm, wo_hbm, bo_hbm,
    storm_hbm, wet_hbm, dune_hbm, cot_hbm,
    gstate_ref, full_ref,
    state_ref, cid_ref, w1_ref, b1_ref, w2_ref, b2_ref, wo_ref, bo_ref,
    storm_ref, wet_ref, dune_ref, cot_ref, load_sem,
    snd0_row, snd0_col, in0_col, rcv0_row, rcv0_col, rcv_diag,
    snd_row, snd_col, rcv_row, rcv_col, ring_row, ring_col,
    edge_send, edge_recv, diag_send, diag_recv, relay_sem,
    feat_ref, dfeat_ref, fx_ref, z_ref, zx_ref, dz_ref, cidx_ref, wetx_ref, dunex_ref,
    wsel_ref, h2f_ref,
    f_ref, h1_ref, h2_ref, act1_ref, q2_ref, d1_ref, d2_ref,
    acc_ref, rcv_a, src_b, rcv_b,
    sum_send, sa_recv, sb_recv, sc_recv,
):
    ncs = ncr * nsu
    g = lax.axis_index("groups")
    al = lax.axis_index("along")
    cr = lax.axis_index("cross")
    su = lax.axis_index("sub")
    cs = cr * nsu + su

    def dev(a, c):
        return (g, a, c // nsu, c % nsu)

    has_dst = (al > 0, al < nal - 1, cs > 0, cs < ncs - 1)
    has_src = (al < nal - 1, al > 0, cs < ncs - 1, cs > 0)
    dst_dev = (
        dev(al - 1, cs), dev(al + 1, cs), dev(al, cs - 1), dev(al, cs + 1),
    )
    corners = ((0, 2), (0, 3), (1, 2), (1, 3))
    diag_dst = [jnp.logical_and(has_dst[a], has_dst[c]) for a, c in corners]
    diag_src = [jnp.logical_and(has_src[a], has_src[c]) for a, c in corners]
    diag_dev = [dev(al + (1 if a else -1), cs + (1 if c == 3 else -1)) for a, c in corners]

    loads = [
        pltpu.make_async_copy(src, dst, load_sem.at[i])
        for i, (src, dst) in enumerate((
            (state_hbm, state_ref), (storm_hbm, storm_ref), (wet_hbm, wet_ref), (dune_hbm, dune_ref),
            (cid_hbm, cid_ref), (w1_hbm, w1_ref), (b1_hbm, b1_ref), (w2_hbm, w2_ref),
            (b2_hbm, b2_ref), (wo_hbm, wo_ref), (bo_hbm, bo_ref), (cot_hbm, cot_ref),
        ))
    ]
    for load in loads[:5]:
        load.start()
    for ref in (rcv0_row, rcv0_col, rcv_diag, rcv_row, rcv_col):
        ref[...] = jnp.zeros_like(ref)

    barrier = pltpu.get_barrier_semaphore()
    for e in range(4):
        @pl.when(diag_dst[e])
        def _():
            pl.semaphore_signal(barrier, inc=1, device_id=diag_dev[e], device_id_type=MESH)
    if near_only:
        for d in range(4):
            @pl.when(has_dst[d])
            def _():
                pl.semaphore_signal(barrier, inc=1, device_id=dst_dev[d], device_id_type=MESH)
    else:
        for j in range(1, ncs):
            pl.semaphore_signal(
                barrier, inc=1, device_id=dev(al, lax.rem(cs + j, ncs)), device_id_type=MESH
            )
        for j in range(1, nal):
            pl.semaphore_signal(
                barrier, inc=1, device_id=dev(lax.rem(al + j, nal), cs), device_id_type=MESH
            )
    for load in loads[5:]:
        load.start()
    beside_al = (al + nal - 1) // nal + (2 * nal - 2 - al) // nal
    beside_cs = (cs + ncs - 1) // ncs + (2 * ncs - 2 - cs) // ncs

    row = lax.broadcasted_iota(jnp.int32, (8, 128), 0)
    lane = lax.broadcasted_iota(jnp.int32, (8, 128), 1)
    field = lax.broadcasted_iota(jnp.int32, (16, 128), 0)
    lane16 = lax.broadcasted_iota(jnp.int32, (16, 128), 1)

    def turn(x, shift, axis):
        shift = shift % x.shape[axis]
        return pltpu.roll(x, shift, axis) if shift else x

    def copy0_of(d):
        src, dst = (snd0_row, rcv0_row) if d < 2 else (snd0_col, rcv0_col)
        return pltpu.make_async_remote_copy(
            src_ref=src.at[d % 2], dst_ref=dst.at[d % 2], send_sem=edge_send.at[d],
            recv_sem=edge_recv.at[0, d], device_id=dst_dev[d], device_id_type=MESH,
        )

    def diag_of(e):
        return pltpu.make_async_remote_copy(
            src_ref=snd0_row.at[e // 2, pl.ds(0, 16)], dst_ref=rcv_diag.at[e],
            send_sem=diag_send.at[e], recv_sem=diag_recv.at[e],
            device_id=diag_dev[e], device_id_type=MESH,
        )

    def copy_of(k, d):
        src, dst = (snd_row, rcv_row) if d < 2 else (snd_col, rcv_col)
        return pltpu.make_async_remote_copy(
            src_ref=src.at[k - 1, d % 2], dst_ref=dst.at[k - 1, d % 2], send_sem=edge_send.at[d],
            recv_sem=edge_recv.at[k % 2, d], device_id=dst_dev[d], device_id_type=MESH,
        )

    around = beside_al + beside_cs + beside_al * beside_cs

    def relay(k):
        if near_only:
            for flags, devices in ((has_dst, dst_dev), (diag_dst, diag_dev)):
                each(flags, lambda i: pl.semaphore_signal(
                    relay_sem.at[k], inc=1, device_id=devices[i], device_id_type=MESH))

    def relayed(k):
        if near_only:
            pl.semaphore_wait(relay_sem.at[k], around)

    def each(flags, action):
        for i in range(4):
            @pl.when(flags[i])
            def _():
                action(i)

    def fill(k, xn, xs, xw, xe):
        west = jnp.zeros((8, 128), f32)
        east = jnp.zeros((8, 128), f32)
        for f in range(12):
            snd_row[k - 1, 0, f:f + 1, :] = xn[f][0:1, :]
            snd_row[k - 1, 1, f:f + 1, :] = xs[f][7:8, :]
            west = jnp.where(lane == f, turn(xw[f], f, 1), west)
            east = jnp.where(lane == f, turn(xe[f], f + 1, 1), east)
        snd_col[k - 1, 0] = west
        snd_col[k - 1, 1] = east

    class Halo:
        def __init__(self, rows, cols):
            self.rows, self.cols = rows, cols

        def south(self, x, f):
            return jnp.where(row == 7, self.rows[0, f:f + 1, :], turn(x, 7, 0))

        def north(self, x, f):
            return jnp.where(row == 0, self.rows[1, f:f + 1, :], turn(x, 1, 0))

        def east(self, x, f):
            return jnp.where(lane == 127, turn(self.cols[0], 127 - f, 1), turn(x, 127, 1))

        def west(self, x, f):
            return jnp.where(lane == 0, turn(self.cols[1], -f, 1), turn(x, 1, 1))

        def around(self, x, f):
            return self.north(x, f), self.south(x, f), self.west(x, f), self.east(x, f)

    for load in loads[:5]:
        load.wait()
    V0 = [state_ref[f * 8:(f + 1) * 8, :] for f in range(12)]
    storm = [storm_ref[f * 8:(f + 1) * 8, :] for f in range(12)]
    wets = [wet_ref[t * 8:(t + 1) * 8, :].astype(f32) for t in range(2)]
    dunes = [dune_ref[t * 8:(t + 1) * 8, :].astype(f32) for t in range(2)]
    wash = [1.0 - dunes[t] for t in range(2)]
    cid = cid_ref[...]
    masks = [wets[0], dunes[0], cid.astype(f32)]
    for d, edge, inner in ((0, 0, 1), (1, 7, 6)):
        for f in range(12):
            snd0_row[d, f:f + 1, :] = V0[f][edge:edge + 1, :]
            snd0_row[d, NEXT + f:NEXT + f + 1, :] = V0[f][inner:inner + 1, :]
            snd0_row[d, STORM + f:STORM + f + 1, :] = storm[f][edge:edge + 1, :]
        for m in range(3):
            snd0_row[d, 12 + m:13 + m, :] = masks[m][edge:edge + 1, :]
        snd0_row[d, 15:16, :] = jnp.zeros((1, 128), f32)

    def column(edge, inner):
        out = jnp.zeros((8, 128), f32)
        for x, at, c in (
            [(V0[f], f, edge) for f in range(12)] + [(V0[f], NEXT + f, inner) for f in range(12)]
            + [(storm[f], COL_STORM + f, edge) for f in range(12)]
            + [(masks[m], COL_MASK + m, edge) for m in range(3)]
        ):
            out = jnp.where(lane == at, turn(x, at - c, 1), out)
        return out

    snd0_col[0] = column(0, 1)
    snd0_col[1] = column(127, 126)
    if near_only:
        pl.semaphore_wait(barrier, around)
    else:
        pl.semaphore_wait(barrier, ncs - 1 + nal - 1 + beside_al * beside_cs)
    each(has_dst, lambda d: copy0_of(d).start())
    each(diag_dst, lambda e: diag_of(e).start())
    for load in loads[5:]:
        load.wait()

    w1 = w1_ref[...]
    w1t = jnp.transpose(jnp.concatenate([w1, jnp.zeros((96, 128), f32)], axis=0))[:, :32]
    w2 = w2_ref[...]
    w1_cat = beside(*split(w1))
    w2_cat = beside(*split(0.5 * w2))
    b1_cols = bias_columns(0.5 * jnp.transpose(jnp.broadcast_to(b1_ref[...], (128, 128))))
    b2_cols = bias_columns(0.5 * jnp.transpose(jnp.broadcast_to(b2_ref[...], (128, 128))))
    w1t_cat = beside(*split(0.5 * w1t), b1_cols)
    w2t_cat = beside(*split(0.5 * jnp.transpose(w2)), b2_cols)
    wo_t = jnp.transpose(jnp.concatenate([wo_ref[...], jnp.zeros((120, 128), f32)], axis=0))[:, :8]

    def choose(unit, ids):
        onehot = (row == ids).astype(f32)
        wsel_ref[:, unit * 128:(unit + 1) * 128] = lax.dot_general(
            wo_t, onehot, (((1,), (0,)), ((), ())),
            precision=lax.Precision.HIGHEST, preferred_element_type=f32,
        )

    def bias_of(ids):
        b = jnp.zeros((8, 128), f32)
        for k in range(8):
            b = jnp.where(ids == k, bo_ref[0:1, k:k + 1], b)
        return b

    for u in range(OWN):
        choose(u, cid[ROW_OF_UNIT[u]:ROW_OF_UNIT[u] + 1, :])
    bsel = bias_of(cid)

    inner_units = list(range(INNER))
    edge_units = [INNER, INNER + 1, STRIP]

    def pairs(units):
        step = 3 if len(units) == 3 else 2
        return [units[i:i + step] for i in range(0, len(units), step)]

    def first_layer(t, unit, feats, kept):
        n = len(feats)
        at = pl.ds(unit * 128, n * 128)
        ones = jnp.ones((16, n * 128), bf16)
        F = jnp.concatenate(feats, axis=1) if n > 1 else feats[0]
        Fh, Fl = split(F)
        a, h = silu(mm(w1t_cat, jnp.concatenate([Fh, Fl, ones, Fh], axis=0)))
        Hh, Hl = split(h)
        if kept:
            f_ref[t, 0:32, at] = Fh
            f_ref[t, 32:64, at] = Fl
            act1_ref[t, :, at] = slope(a, h)
            h1_ref[t, 0:128, at] = Hh
            h1_ref[t, 128:256, at] = Hl
        return jnp.concatenate([Hh, Hl, ones, Hh], axis=0)

    def second_layer(t, unit, feats, kept, H):
        n = len(feats)
        at = pl.ds(unit * 128, n * 128)
        a, h = silu(mm(w2t_cat, H))
        wsel = wsel_ref[:, at]
        if kept:
            q2_ref[t, :, at] = wsel * slope(a, h)
            h2f_ref[t, :, at] = h
        z = jnp.sum(wsel * h, axis=0, keepdims=True)
        return [z[:, i * 128:(i + 1) * 128] for i in range(n)]

    def staggered(tasks, first, second):
        out, held = [], []
        for task in tasks:
            held.append((task, first(*task)))
            if len(held) > DEPTH:
                done, x = held.pop(0)
                out.append(second(*done, x))
        for done, x in held:
            out.append(second(*done, x))
        return out

    def layers(*tasks):
        return staggered(tasks, first_layer, second_layer)

    def settle(t, units):
        for part in pairs(units):
            at = pl.ds(part[0] * 128, len(part) * 128)
            Hh, Hl = split(h2f_ref[t, :, at])
            h2_ref[t, 0:128, at] = Hh
            h2_ref[t, 128:256, at] = Hl

    def put_features(V, near):
        for f in range(4):
            for part, x in enumerate((V[f],) + tuple(near[f])):
                feat_ref[(4 * part + f) * 8:(4 * part + f + 1) * 8, :] = x

    def feats_of(*rows):
        return [feat_ref[pl.ds(r, 32, stride=8), :] for r in rows]

    def own_layers(t, first, last):
        rows = [ROW_OF_UNIT[u:u + 2] for u in range(first, last, 2)]
        tasks = [(t, u, feats_of(*r), True) for u, r in zip(range(first, last, 2), rows)]
        for pair, out in zip(rows, layers(*tasks)):
            for r, z in zip(pair, out):
                z_ref[r:r + 1, :] = z

    in0_col[0] = column(1, 2)
    in0_col[1] = column(126, 125)
    dfeat_ref[...] = jnp.zeros_like(dfeat_ref)
    feat_ref[160:256, :] = storm_ref[...]
    put_features(V0, [
        (turn(V0[f], 1, 0), turn(V0[f], 7, 0), turn(V0[f], 1, 1), turn(V0[f], 127, 1)) for f in range(4)
    ])
    own_layers(0, 0, INNER)
    settle(0, inner_units)
    for ref, rows in ((f_ref, 64), (h1_ref, 256)):
        ref[:, rows:rows + 16, :] = jnp.ones((2, 16, ref.shape[2]), bf16)
    for ref in (zx_ref, cidx_ref, wetx_ref, dunex_ref):
        ref[...] = jnp.zeros_like(ref)
    spare = acc_ref.shape[0] - ROWS
    if spare:
        acc_ref[ROWS:, :] = jnp.zeros((spare, 128), f32)

    each(has_src, lambda d: copy0_of(d).wait_recv())
    each(diag_src, lambda e: diag_of(e).wait_recv())
    relay(0)

    halo0 = Halo(rcv0_row, rcv0_col)
    near0 = [halo0.around(V0[f], f) for f in range(12)]
    put_features(V0, near0)
    sides = jnp.concatenate(
        [
            rcv0_col[1], rcv0_col[0], snd0_col[0], snd0_col[1], in0_col[0], in0_col[1],
            jnp.zeros((80, 128), f32),
        ], axis=0
    )
    T = jnp.transpose(sides)
    SE, SW, NE, NW = [rcv_diag[e] for e in range(4)]
    RS, RN = rcv0_row[0, 0:16, :], rcv0_row[1, 0:16, :]
    group = lane16 // 8
    V, far = T[0:16], T[NEXT:NEXT + 16]
    plus, minus = turn(V, 16, 1), turn(V, -16, 1)
    N, S = turn(V, 1, 1), turn(V, -1, 1)
    for at, x, c in ((0, NW, 127), (8, NE, 0), (16, RN, 0), (24, RN, 127), (32, RN, 1), (40, RN, 126)):
        N = jnp.where(lane16 == at, turn(x, at - c, 1), N)
    for at, x, c in ((7, SW, 127), (15, SE, 0), (23, RS, 0), (31, RS, 127), (39, RS, 1), (47, RS, 126)):
        S = jnp.where(lane16 == at, turn(x, at - c, 1), S)
    W = jnp.where(group == 1, minus, jnp.where(jnp.logical_or(group == 2, group == 4), plus, far))
    E = jnp.where(group == 0, minus, jnp.where(jnp.logical_or(group == 3, group == 5), plus, far))
    outer = [(V, N, S, W, E)]
    for V, N, S, west, east in (
        (RN, rcv0_row[1, NEXT:NEXT + 16, :], snd0_row[0, 0:16, :], NW, NE),
        (RS, snd0_row[1, 0:16, :], rcv0_row[0, NEXT:NEXT + 16, :], SW, SE),
    ):
        W = jnp.where(lane16 == 0, turn(west, 1, 1), turn(V, 1, 1))
        E = jnp.where(lane16 == 127, turn(east, 127, 1), turn(V, 127, 1))
        outer.append((V, N, S, W, E))
    storms = [T[COL_STORM:COL_STORM + 12], rcv0_row[1, STORM:STORM + 12, :], rcv0_row[0, STORM:STORM + 12, :]]
    mask_rows = [
        [T[COL_MASK + m:COL_MASK + m + 1] for m in range(3)],
        [rcv0_row[1, 12 + m:13 + m, :] for m in range(3)],
        [rcv0_row[0, 12 + m:13 + m, :] for m in range(3)],
    ]
    for w in range(3):
        for part in range(5):
            fx_ref[w, 4 * part:4 * part + 4, :] = outer[w][part][0:4]
        fx_ref[w, 20:32, :] = storms[w]
        wetx_ref[w:w + 1, :] = mask_rows[w][0]
        dunex_ref[w:w + 1, :] = mask_rows[w][1]
        ids = mask_rows[w][2].astype(jnp.int32)
        cidx_ref[w:w + 1, :] = ids
        choose(STRIP + w, ids)
    cidx = cidx_ref[...]
    (z_top, z_low), (z_strip,), (z_north, z_south) = layers(
        (0, INNER, feats_of(0, 7), True), (0, STRIP, [fx_ref[0]], True),
        (0, STRIP + 1, [fx_ref[1], fx_ref[2]], False),
    )
    z_ref[0:1, :] = z_top
    z_ref[7:8, :] = z_low
    zx_ref[0:1, :] = z_strip
    zx_ref[1:2, :] = z_north
    zx_ref[2:3, :] = z_south
    biasx = bias_of(cidx)
    zx = zx_ref[...] + biasx
    pickx = pickup_gain * softplus(zx) * (1.0 - dunex_ref[...])

    def from_strip(x, start):
        return jnp.sum(jnp.where(lane == start + row, x, 0.0), axis=1, keepdims=True)

    inside = jnp.logical_and(row > 0, row < 7)
    at_west = jnp.logical_and(inside, lane == 0)
    at_east = jnp.logical_and(inside, lane == 127)

    def with_strip(z, strip):
        z = jnp.where(at_west, from_strip(strip, 16), z)
        return jnp.where(at_east, from_strip(strip, 24), z)

    def to_strip(x):
        out = jnp.where(lane == 16 + row, x[:, 0:1], jnp.where(lane == 24 + row, x[:, 127:128], 0.0))
        return jnp.sum(jnp.where(inside, out, 0.0), axis=0, keepdims=True)

    z0 = with_strip(z_ref[...] + bsel, zx[0:1, :])

    def advanced(w):
        V, N, S, W, E = outer[w]
        pick, wet = pickx[w:w + 1, :], wetx_ref[w:w + 1, :]
        lap = N + S + W + E - 4.0 * V
        ad, cd = S - N, E - W
        spread = jnp.where(field == 3, bed_diffusion, diffusion) * lap
        sediment = spread - advection * (V[1:2] * ad + V[2:3] * cd) - settling * V
        sediment = sediment + jnp.where(field - 4 == cidx[w:w + 1, :], pick, 0.0)
        total = jnp.sum(
            jnp.where(jnp.logical_and(field >= 4, field < 12), V, 0.0), axis=0, keepdims=True
        )
        first = jnp.where(field == 0, -advection * (ad[1:2] + cd[2:3]), settling * total - pick)
        first = jnp.where(field == 1, -advection * ad[0:1] - friction * V[1:2], first)
        first = jnp.where(field == 2, -advection * cd[0:1] - friction * V[2:3], first)
        return V + wet * jnp.where(field < 4, spread + first, sediment)

    strip1, RN, RS = advanced(0), advanced(1), advanced(2)
    ring_row[1] = RN
    ring_row[0] = RS
    back = jnp.transpose(jnp.concatenate([strip1, jnp.zeros((112, 128), f32)], axis=0))
    ring_col[1] = back[0:8]
    ring_col[0] = back[8:16]

    pickup = softplus(z0) * wash[0]
    lap = []
    for f in range(12):
        n, s, w, e = near0[f]
        lap.append(n + s + w + e - 4.0 * V0[f])
    total = V0[4]
    for k in range(1, 8):
        total = total + V0[4 + k]
    ad = [near0[f][1] - near0[f][0] for f in range(12)]
    cd = [near0[f][3] - near0[f][2] for f in range(12)]
    tend = [
        diffusion * lap[0] - advection * (ad[1] + cd[2]),
        diffusion * lap[1] - advection * ad[0] - friction * V0[1],
        diffusion * lap[2] - advection * cd[0] - friction * V0[2],
        bed_diffusion * lap[3] - pickup_gain * pickup + settling * total,
    ]
    for k in range(8):
        x = diffusion * lap[4 + k] - advection * (V0[1] * ad[4 + k] + V0[2] * cd[4 + k])
        x = x + jnp.where(cid == k, pickup_gain * pickup, 0.0) - settling * V0[4 + k]
        tend.append(x)
    V1 = [V0[f] + wets[0] * tend[f] for f in range(12)]

    halo1 = Halo(ring_row, ring_col)
    near1 = [halo1.around(V1[f], f) for f in range(12)]
    put_features(V1, near1)
    plus, minus = turn(strip1, 16, 1), turn(strip1, -16, 1)
    N, S = turn(strip1, 1, 1), turn(strip1, -1, 1)
    for at, c in ((16, 0), (24, 127)):
        N = jnp.where(lane16 == at, turn(RN, at - c, 1), N)
        S = jnp.where(lane16 == at + 7, turn(RS, at + 7 - c, 1), S)
    W, E = jnp.where(group == 2, plus, minus), jnp.where(group == 2, minus, plus)
    for part, x in enumerate((strip1, N, S, W, E)):
        fx_ref[0, 4 * part:4 * part + 4, :] = x[0:4]
    (z_top, z_low), (z_strip,) = layers(
        (1, INNER, feats_of(0, 7), True), (1, STRIP, [fx_ref[0]], True)
    )
    z_ref[0:1, :] = z_top
    z_ref[7:8, :] = z_low
    z_strip = z_strip + biasx[0:1, :]
    relayed(0)
    relay(1)
    z1 = with_strip(z_ref[...] + bsel, z_strip)
    lam2 = [cot_ref[f * 8:(f + 1) * 8, :] for f in range(12)]

    def closure_cotangent(t, gate, lam):
        G = [None] * 3 + [wets[t] * lam[f] for f in range(3, 12)]
        picked = G[4]
        for k in range(1, 8):
            picked = jnp.where(cid == k, G[4 + k], picked)
        return pickup_gain * (picked - G[3]) * wash[t] * gate

    def sigmoid(z):
        return 1.0 / (1.0 + jnp.exp(-z))

    def adjoint_two(t, units, drows):
        for part in pairs(list(zip(units, drows))):
            at = pl.ds(part[0][0] * 128, len(part) * 128)
            drow = 0.5 * jnp.concatenate([d for _, d in part], axis=1)
            Dh, Dl = split(q2_ref[t, :, at] * drow)
            d2_ref[t, 0:128, at] = Dh
            d2_ref[t, 128:256, at] = Dl

    def adjoint_one(t, units):
        def product(part):
            at = pl.ds(part[0] * 128, len(part) * 128)
            return mm(w2_cat, jnp.concatenate([d2_ref[t, :, at], d2_ref[t, 0:128, at]], axis=0))

        def rest(part, d1):
            at = pl.ds(part[0] * 128, len(part) * 128)
            Dh, Dl = split(d1 * act1_ref[t, :, at])
            d1_ref[t, 0:128, at] = Dh
            d1_ref[t, 128:256, at] = Dl

        staggered([(part,) for part in pairs(units)], product, rest)

    def feature_cotangent(t, units):
        out = []

        def product(part):
            at = pl.ds(part[0] * 128, len(part) * 128)
            return mm(w1_cat, jnp.concatenate([d1_ref[t, :, at], d1_ref[t, 0:128, at]], axis=0))

        def rest(part, dF):
            for i, u in enumerate(part):
                one = dF[:, i * 128:(i + 1) * 128]
                if u < OWN:
                    dfeat_ref[pl.ds(ROW_OF_UNIT[u], 32, stride=8), :] = one
                else:
                    out.append(one)

        staggered([(part,) for part in pairs(units)], product, rest)
        return out

    def adjoint_cells(D, G, near, V, lam):
        lap = [bed_diffusion if f == 3 else diffusion for f in range(12)]
        lg = [lap[f] * G[f] for f in range(12)]
        c = [lam[f] - 4.0 * lg[f] for f in range(12)]
        alongs = jnp.zeros((8, 128), f32)
        crosses = jnp.zeros((8, 128), f32)
        along_part = [advection * G[1], advection * G[0], None, None]
        cross_part = [advection * G[2], None, advection * G[0], None]
        for k in range(8):
            n, s, w, e = near[4 + k]
            alongs = alongs + (s - n) * G[4 + k]
            crosses = crosses + (e - w) * G[4 + k]
            c[4 + k] = c[4 + k] + settling * (G[3] - G[4 + k])
            ag = advection * G[4 + k]
            along_part.append(V[1] * ag)
            cross_part.append(V[2] * ag)
        c[1] = c[1] - friction * G[1] - advection * alongs
        c[2] = c[2] - friction * G[2] - advection * crosses
        to = [[], [], [], []]
        for f in range(12):
            for d, part, sign in ((0, along_part, 1), (1, along_part, -1), (2, cross_part, 1), (3, cross_part, -1)):
                x = lg[f]
                if part[f] is not None:
                    x = x + part[f] if sign > 0 else x - part[f]
                if f < 4:
                    x = x + D[4 + 4 * d + f]
                to[d].append(x)
            if f < 4:
                c[f] = c[f] + D[f]
        return c, to

    def gather(c, to, halo):
        return [
            c[f] + halo.south(to[0][f], f) + halo.north(to[1][f], f)
            + halo.east(to[2][f], f) + halo.west(to[3][f], f)
            for f in range(12)
        ]

    def keep(start, part, first):
        at = pl.ds(start, part.shape[0])
        acc_ref[at, :] = part if first else acc_ref[at, :] + part

    def weights_two(t, units, ids, drows, first):
        at = pl.ds(units[0] * 128, len(units) * 128)
        width = len(units) * 128
        dr = jnp.concatenate(
            [jnp.where(row == k, d, 0.0) for k, d in zip(ids, drows)], axis=1
        )
        dbo = jnp.sum(
            jnp.where(row == lane, jnp.sum(dr, axis=1, keepdims=True), 0.0), axis=0, keepdims=True
        )
        drh, drl = split(jnp.concatenate([dr, jnp.zeros((8, width), f32)], axis=0))
        top = mm_nt(jnp.concatenate([drh, drl], axis=0), h2_ref[t, :, at])
        dwo = top[:8, :128] + top[16:24, :128] + top[:8, 128:]
        top = mm_nt(h1_ref[t, :, at], d2_ref[t, :, at])
        keep(0, top[:128, :128] + top[128:256, :128] + top[:128, 128:], first)
        keep(ROW_WO, dwo, first)
        ones = top[256:264, :128] + top[256:264, 128:]
        keep(ROW_BIAS, jnp.where(row == 1, ones, jnp.where(row == 2, dbo, 0.0)), first)

    def weights_one(t, units, first):
        at = pl.ds(units[0] * 128, len(units) * 128)
        top = mm_nt(f_ref[t, :, at], d1_ref[t, :, at])
        keep(ROW_W1, top[:32, :128] + top[32:64, :128] + top[:32, 128:], first)
        ones = top[64:72, :128] + top[64:72, 128:]
        keep(ROW_BIAS, jnp.where(row == 0, ones, 0.0), False)

    def rows_of(x, units):
        return [x[ROW_OF_UNIT[u]:ROW_OF_UNIT[u] + 1, :] for u in units]

    G1 = [wets[1] * lam2[f] for f in range(12)]
    columns = jnp.logical_and(lane > 0, lane < 127)

    def patched(strip_back):
        turned = jnp.transpose(jnp.concatenate([strip_back, jnp.zeros((96, 128), f32)], axis=0))
        at_w, at_e = turned[16:24], turned[24:32]
        out = []
        for f in range(20):
            x = dfeat_ref[f * 8:(f + 1) * 8, :]
            x = jnp.where(at_west, turn(at_w, -f, 1), x)
            out.append(jnp.where(at_east, turn(at_e, 127 - f, 1), x))
        return out

    dz1 = closure_cotangent(1, sigmoid(z1), lam2)
    edge_rows1 = [dz1[0:1, :], dz1[7:8, :], to_strip(dz1)]
    adjoint_two(1, edge_units, edge_rows1)
    adjoint_one(1, edge_units)
    strip_back = feature_cotangent(1, edge_units)[0]
    _, to1 = adjoint_cells(patched(strip_back), G1, near1, V1, lam2)
    fill(1, *to1)
    each(has_dst, lambda d: copy0_of(d).wait_send())
    each(has_dst, lambda d: copy_of(1, d).start())

    own_layers(1, 0, INNER)
    dz1 = closure_cotangent(1, sigmoid(z_ref[...] + bsel), lam2)
    dz_ref[...] = jnp.where(columns, dz1, 0.0)
    drows1 = rows_of(dz_ref, inner_units)
    adjoint_two(1, inner_units, drows1)
    adjoint_one(1, inner_units)
    feature_cotangent(1, inner_units)
    c1, to1 = adjoint_cells(patched(strip_back), G1, near1, V1, lam2)
    gate0 = sigmoid(z0)
    settle(1, inner_units + edge_units)
    settle(0, edge_units)
    ids_edge = [cid[0:1, :], cid[7:8, :], cidx_ref[0:1, :]]
    weights_two(
        1, inner_units + edge_units, rows_of(cid, inner_units) + ids_edge, drows1 + edge_rows1, True
    )
    weights_one(1, inner_units + edge_units, True)
    lam1 = [
        c1[f] + turn(to1[0][f], 7, 0) + turn(to1[1][f], 1, 0) + turn(to1[2][f], 127, 1) + turn(to1[3][f], 1, 1)
        for f in range(12)
    ]
    dz0 = closure_cotangent(0, gate0, lam1)
    dz_ref[...] = jnp.where(columns, dz0, 0.0)
    drows0 = rows_of(dz_ref, inner_units)
    adjoint_two(0, inner_units, drows0)
    weights_two(0, inner_units, rows_of(cid, inner_units), drows0, False)
    adjoint_one(0, inner_units)
    weights_one(0, inner_units, False)
    feature_cotangent(0, inner_units)

    each(has_src, lambda d: copy_of(1, d).wait_recv())
    relayed(1)
    lam1 = gather(c1, to1, Halo(rcv_row.at[0], rcv_col.at[0]))
    dz0 = closure_cotangent(0, gate0, lam1)
    drows0 = [dz0[0:1, :], dz0[7:8, :], to_strip(dz0)]
    adjoint_two(0, edge_units, drows0)
    weights_two(0, edge_units, ids_edge, drows0, False)
    adjoint_one(0, edge_units)
    weights_one(0, edge_units, False)

    size = src_b.shape[0]
    last_core = nsu - 1
    owner = su == last_core
    piece = al * ncr + cr if direct else cs
    mine = pl.ds(pl.multiple_of(piece * size, 8), size)
    spans = [(dz, dx) for dz in range(nal) for dx in range(ncr)]

    def chip_at(span):
        return lax.rem(al + span[0], nal), lax.rem(cr + span[1], ncr)

    def to_owner(k):
        a, c = chip_at(spans[k])
        slot = 2 * (k - 1) + su if k else 2 * (len(spans) - 1)
        at = pl.ds(pl.multiple_of((a * ncr + c) * size, 8), size)
        return pltpu.make_async_remote_copy(
            src_ref=acc_ref.at[at, :], dst_ref=rcv_a.at[slot], send_sem=sum_send.at[0],
            recv_sem=sa_recv.at[0], device_id=(g, a, c, last_core), device_id_type=MESH,
        )

    def from_owner(k, core):
        a, c = chip_at(spans[k])
        return pltpu.make_async_remote_copy(
            src_ref=full_ref.at[mine, :], dst_ref=full_ref.at[mine, :], send_sem=sum_send.at[1],
            recv_sem=sc_recv.at[0], device_id=(g, a, c, core), device_id_type=MESH,
        )

    def all_of(ref, sem):
        return pltpu.make_async_remote_copy(
            src_ref=ref, dst_ref=ref, send_sem=sem, recv_sem=sem,
            device_id=(g, al, cr, nsu - 1 - su), device_id_type=MESH,
        )

    def copy_a(j):
        peer = lax.rem(cs + j, ncs)
        return pltpu.make_async_remote_copy(
            src_ref=acc_ref.at[pl.ds(pl.multiple_of(peer * size, 8), size), :],
            dst_ref=rcv_a.at[j - 1], send_sem=sum_send.at[j - 1], recv_sem=sa_recv.at[j - 1],
            device_id=dev(al, peer), device_id_type=MESH,
        )

    def copy_b(j):
        return pltpu.make_async_remote_copy(
            src_ref=src_b, dst_ref=rcv_b.at[al], send_sem=sum_send.at[j - 1],
            recv_sem=sb_recv.at[j - 1],
            device_id=dev(lax.rem(al + j, nal), cs), device_id_type=MESH,
        )

    def copy_c(j):
        return pltpu.make_async_remote_copy(
            src_ref=full_ref.at[mine, :], dst_ref=full_ref.at[mine, :],
            send_sem=sum_send.at[j - 1], recv_sem=sc_recv.at[j - 1],
            device_id=dev(al, lax.rem(cs + j, ncs)), device_id_type=MESH,
        )

    others = len(spans) - 1
    if direct:
        for k in range(others, 0, -1):
            to_owner(k).start()

        @pl.when(jnp.logical_not(owner))
        def _():
            to_owner(0).start()
    else:
        for j in range(1, ncs):
            copy_a(j).start()

    D0 = patched(feature_cotangent(0, edge_units)[0])
    G0 = [wets[0] * lam1[f] for f in range(12)]
    c0, to0 = adjoint_cells(D0, G0, near0, V0, lam1)
    fill(2, *to0)
    each(has_dst, lambda d: copy_of(1, d).wait_send())
    each(has_dst, lambda d: copy_of(2, d).start())

    if direct:
        @pl.when(owner)
        def _():
            all_of(rcv_a, sa_recv.at[0]).wait_recv()
            total = acc_ref[mine, :]
            for j in range(rcv_a.shape[0]):
                total = total + rcv_a[j]
            full_ref[mine, :] = total * factor
            for k in range(others, -1, -1):
                for core in range(nsu):
                    if k or core != last_core:
                        from_owner(k, core).start()
    else:
        total = acc_ref[mine, :]
        for j in range(1, ncs):
            copy_a(j).wait_recv()
            total = total + rcv_a[j - 1]
        src_b[...] = total
        rcv_b[al] = total
        for j in range(1, ncs):
            copy_a(j).wait_send()
        for j in range(1, nal):
            copy_b(j).start()
    each(has_src, lambda d: copy_of(2, d).wait_recv())
    last = gather(c0, to0, Halo(rcv_row.at[1], rcv_col.at[1]))
    for f in range(12):
        gstate_ref[f] = last[f]
    each(has_dst, lambda d: copy_of(2, d).wait_send())
    each(diag_dst, lambda e: diag_of(e).wait_send())
    if direct:
        @pl.when(owner)
        def _():
            all_of(acc_ref.at[pl.ds(0, others * size), :], sum_send.at[0]).wait_send()
            all_of(full_ref.at[pl.ds(0, others * size), :], sc_recv.at[0]).wait_recv()
            all_of(rcv_a, sum_send.at[1]).wait_send()

        @pl.when(jnp.logical_not(owner))
        def _():
            all_of(acc_ref, sum_send.at[0]).wait_send()
            all_of(full_ref, sc_recv.at[0]).wait_recv()
    else:
        for j in range(1, nal):
            copy_b(j).wait_recv()
        total = rcv_b[0]
        for j in range(1, nal):
            total = total + rcv_b[j]
        full_ref[mine, :] = total * factor
        for j in range(1, nal):
            copy_b(j).wait_send()
        for j in range(1, ncs):
            copy_c(j).start()
        for j in range(1, ncs):
            copy_c(j).wait_recv()
        for j in range(1, ncs):
            copy_c(j).wait_send()


def unpack(
    state_ref, full_ref,
    gs_hbm, gw1_hbm, gb1_hbm, gw2_hbm, gb2_hbm, gwo_hbm, gbo_hbm, gbo_ref, sem,
):
    gbo_ref[...] = full_ref[ROW_BIAS + 2:ROW_BIAS + 3, 0:8]
    parts = (
        (full_ref.at[0:128], gw2_hbm), (state_ref, gs_hbm), (full_ref.at[ROW_W1:ROW_W1 + 32], gw1_hbm),
        (full_ref.at[ROW_WO:ROW_WO + 8], gwo_hbm), (full_ref.at[ROW_BIAS:ROW_BIAS + 1], gb1_hbm),
        (full_ref.at[ROW_BIAS + 1:ROW_BIAS + 2], gb2_hbm), (gbo_ref, gbo_hbm),
    )
    copies = [pltpu.make_async_copy(src, dst, sem.at[i]) for i, (src, dst) in enumerate(parts)]
    for copy in copies:
        copy.start()
    for copy in copies:
        copy.wait()


def solution(mesh):
    nal, ncr, nsu = mesh.shape["along"], mesh.shape["cross"], mesh.shape["sub"]
    ncs = ncr * nsu
    near_only = nal <= 4 and ncs <= 4
    direct = near_only and nsu == 2
    owners = nal * ncr if direct else ncs
    size = 8 * (-(-ROWS // (8 * owners)))

    def per_device(state, storm, wet, dune, cid, w1, b1, w2, b2, wo, bo, cot):
        rows, cols = state.shape[1], state.shape[2]
        factor = 1.0 / math.sqrt(rows * nal * cols * ncs)
        vmem = pl.BlockSpec(memory_space=pltpu.VMEM)
        hbm = pl.BlockSpec(memory_space=pl.ANY)
        flat = lambda x: x.reshape(-1, 128)
        operands = (
            flat(state), cid, w1, b1.reshape(1, 128), w2, b2.reshape(1, 128), wo.T, bo.reshape(1, 8),
            flat(storm), flat(wet), flat(dune), flat(cot),
        )
        dma = pltpu.SemaphoreType.DMA
        tile = pltpu.VMEM((8, 128), f32)
        big = lambda n, kind: pltpu.VMEM((2, n, (OWN + 1) * 128), kind)
        out = pl.pallas_call(
            functools.partial(kernel, nal, ncr, nsu, near_only, direct, factor),
            out_shape=(pltpu.VMEM((12, 8, 128), f32), pltpu.VMEM((owners * size, 128), f32)),
            in_specs=[hbm] * 12,
            out_specs=(vmem,) * 2,
            scratch_shapes=[
                *[pltpu.VMEM(x.shape, x.dtype) for x in operands],
                dma((12,)),
                pltpu.VMEM((2, 40, 128), f32),
                pltpu.VMEM((2, 8, 128), f32),
                pltpu.VMEM((2, 8, 128), f32),
                pltpu.VMEM((2, 40, 128), f32),
                pltpu.VMEM((2, 8, 128), f32),
                pltpu.VMEM((4, 16, 128), f32),
                pltpu.VMEM((2, 2, 16, 128), f32),
                pltpu.VMEM((2, 2, 8, 128), f32),
                pltpu.VMEM((2, 2, 16, 128), f32),
                pltpu.VMEM((2, 2, 8, 128), f32),
                pltpu.VMEM((2, 16, 128), f32),
                pltpu.VMEM((2, 8, 128), f32),
                dma((4,)), dma((2, 4)), dma((4,)), dma((4,)), pltpu.SemaphoreType.REGULAR((2,)),
                pltpu.VMEM((256, 128), f32),
                pltpu.VMEM((256, 128), f32),
                pltpu.VMEM((3, 32, 128), f32),
                tile, tile, tile, pltpu.VMEM((8, 128), jnp.int32), tile, tile,
                pltpu.VMEM((128, (OWN + 3) * 128), f32), big(128, f32),
                big(80, bf16), big(272, bf16), big(256, bf16), big(128, f32), big(128, f32),
                big(256, bf16), big(256, bf16),
                pltpu.VMEM((owners * size, 128), f32),
                pltpu.VMEM((nsu * owners - 1 if direct else ncs - 1, size, 128), f32),
                pltpu.VMEM((size, 128), f32),
                pltpu.VMEM((1 if direct else nal, size, 128), f32),
                dma((2 if direct else max(ncs, nal) - 1,)), dma((1 if direct else ncs - 1,)),
                dma((1 if direct else nal - 1,)), dma((1 if direct else ncs - 1,)),
            ],
            compiler_params=pltpu.CompilerParams(collective_id=0, has_side_effects=True),
        )(*operands)
        gs, gw1, gb1, gw2, gb2, gwo, gbo = pl.pallas_call(
            unpack,
            out_shape=(
                jax.ShapeDtypeStruct((12, 8, 128), f32),
                jax.ShapeDtypeStruct((32, 128), f32),
                jax.ShapeDtypeStruct((1, 128), f32),
                jax.ShapeDtypeStruct((128, 128), f32),
                jax.ShapeDtypeStruct((1, 128), f32),
                jax.ShapeDtypeStruct((8, 128), f32),
                jax.ShapeDtypeStruct((1, 8), f32),
            ),
            in_specs=[vmem] * 2,
            out_specs=(hbm,) * 7,
            scratch_shapes=[pltpu.VMEM((1, 8), f32), dma((7,))],
        )(*[pltpu.with_memory_space_constraint(x, pltpu.VMEM) for x in out])
        return gs, gw1, gb1.reshape(128), gw2, gb2.reshape(128), gwo.T, gbo.reshape(8)

    tile = P(None, ("groups", "along"), ("cross", "sub"))
    return jax.shard_map(
        per_device,
        mesh=mesh,
        in_specs=(
            tile, tile, tile, tile, P(("groups", "along"), ("cross", "sub")),
            P(), P(), P(), P(), P(), P(), tile,
        ),
        out_specs=(
            tile, P("groups", None), P("groups"), P("groups", None), P("groups"),
            P("groups", None), P("groups"),
        ),
        check_vma=False,
    )
```

```python
import functools
import math

import jax
import jax.numpy as jnp
from jax import lax
from jax.experimental import pallas as pl
from jax.experimental.pallas import tpu as pltpu
from jax.sharding import PartitionSpec as P

MESH = pl.DeviceIdType.MESH
f32 = jnp.float32
bf16 = jnp.bfloat16
diffusion = 0.15
advection = 0.2
friction = 0.05
pickup_gain = 0.5
settling = 0.2
bed_diffusion = 0.1

ROW_W1 = 128
ROW_WO = 160
ROW_BIAS = 168
ROWS = 176
ROW_OF_UNIT = (1, 2, 3, 4, 5, 6, 0, 7)
INNER = 6
DEPTH = 2
OWN = 8
STRIP = 8
NEXT = 16
STORM = 28
COL_STORM = 32
COL_MASK = 44


def split(x):
    high = x.astype(bf16)
    low = (x - high.astype(f32)).astype(bf16)
    return high, low


def mm(a, b):
    return lax.dot_general(a, b, (((1,), (0,)), ((), ())), preferred_element_type=f32)


def mm_nt(a, b):
    return lax.dot_general(a, b, (((1,), (1,)), ((), ())), preferred_element_type=f32)


def beside(high, low, *extra):
    return jnp.concatenate([high, high, *extra, low], axis=1)


def bias_columns(spread):
    high = spread.astype(bf16)
    rest = spread - high.astype(f32)
    middle = rest.astype(bf16)
    low = (rest - middle.astype(f32)).astype(bf16)
    lane = lax.broadcasted_iota(jnp.int32, spread.shape, 1)
    out = jnp.zeros_like(spread)
    for i, part in enumerate((high, middle, low)):
        out = jnp.where(lane == i, part.astype(f32), out)
    return out[:, :16].astype(bf16)


def silu(u):
    a = 1.0 + jnp.tanh(u)
    return a, u * a


def slope(a, h):
    return h * (2.0 - a) + a


def softplus(z):
    return jnp.maximum(z, 0.0) + jnp.log(1.0 + jnp.exp(-jnp.abs(z)))


def kernel(
    nal, ncr, nsu, near_only, direct, factor,
    state_hbm, cid_hbm, w1_hbm, b1_hbm, w2_hbm, b2_hbm, wo_hbm, bo_hbm,
    storm_hbm, wet_hbm, dune_hbm, cot_hbm,
    gstate_ref, full_ref,
    state_ref, cid_ref, w1_ref, b1_ref, w2_ref, b2_ref, wo_ref, bo_ref,
    storm_ref, wet_ref, dune_ref, cot_ref, load_sem,
    snd0_row, snd0_col, in0_col, rcv0_row, rcv0_col, rcv_diag,
    snd_row, snd_col, rcv_row, rcv_col, ring_row, ring_col,
    edge_recv, diag_recv, relay_sem,
    feat_ref, dfeat_ref, fx_ref, z_ref, zx_ref, dz_ref, cidx_ref, wetx_ref, dunex_ref,
    wsel_ref, h2f_ref,
    f_ref, h1_ref, h2_ref, act1_ref, q2_ref, d1_ref, d2_ref,
    acc_ref, rcv_a, src_b, rcv_b,
    sum_sem,
):
    ncs = ncr * nsu
    g = lax.axis_index("groups")
    al = lax.axis_index("along")
    cr = lax.axis_index("cross")
    su = lax.axis_index("sub")
    cs = cr * nsu + su

    def dev(a, c):
        return (g, a, c // nsu, c % nsu)

    has_dst = (al > 0, al < nal - 1, cs > 0, cs < ncs - 1)
    has_src = (al < nal - 1, al > 0, cs < ncs - 1, cs > 0)
    dst_dev = (
        dev(al - 1, cs), dev(al + 1, cs), dev(al, cs - 1), dev(al, cs + 1),
    )
    corners = ((0, 2), (0, 3), (1, 2), (1, 3))
    diag_dst = [jnp.logical_and(has_dst[a], has_dst[c]) for a, c in corners]
    diag_src = [jnp.logical_and(has_src[a], has_src[c]) for a, c in corners]
    diag_dev = [dev(al + (1 if a else -1), cs + (1 if c == 3 else -1)) for a, c in corners]

    loads = [
        pltpu.make_async_copy(src, dst, load_sem.at[i])
        for i, (src, dst) in enumerate((
            (state_hbm, state_ref), (storm_hbm, storm_ref), (wet_hbm, wet_ref), (dune_hbm, dune_ref),
            (cid_hbm, cid_ref), (w1_hbm, w1_ref), (b1_hbm, b1_ref), (w2_hbm, w2_ref),
            (b2_hbm, b2_ref), (wo_hbm, wo_ref), (bo_hbm, bo_ref), (cot_hbm, cot_ref),
        ))
    ]
    for load in loads[:5]:
        load.start()
    for ref in (rcv0_row, rcv0_col, rcv_diag, rcv_row, rcv_col):
        ref[...] = jnp.zeros_like(ref)

    barrier = pltpu.get_barrier_semaphore()
    for e in range(4):
        @pl.when(diag_dst[e])
        def _():
            pl.semaphore_signal(barrier, inc=1, device_id=diag_dev[e], device_id_type=MESH)
    if near_only:
        for d in range(4):
            @pl.when(has_dst[d])
            def _():
                pl.semaphore_signal(barrier, inc=1, device_id=dst_dev[d], device_id_type=MESH)
    else:
        for j in range(1, ncs):
            pl.semaphore_signal(
                barrier, inc=1, device_id=dev(al, lax.rem(cs + j, ncs)), device_id_type=MESH
            )
        for j in range(1, nal):
            pl.semaphore_signal(
                barrier, inc=1, device_id=dev(lax.rem(al + j, nal), cs), device_id_type=MESH
            )
    for load in loads[5:]:
        load.start()
    beside_al = (al + nal - 1) // nal + (2 * nal - 2 - al) // nal
    beside_cs = (cs + ncs - 1) // ncs + (2 * ncs - 2 - cs) // ncs

    row = lax.broadcasted_iota(jnp.int32, (8, 128), 0)
    lane = lax.broadcasted_iota(jnp.int32, (8, 128), 1)
    field = lax.broadcasted_iota(jnp.int32, (16, 128), 0)
    lane16 = lax.broadcasted_iota(jnp.int32, (16, 128), 1)

    def turn(x, shift, axis):
        shift = shift % x.shape[axis]
        return pltpu.roll(x, shift, axis) if shift else x

    def copy0_of(d):
        src, dst = (snd0_row, rcv0_row) if d < 2 else (snd0_col, rcv0_col)
        return pltpu.make_async_remote_copy(
            src_ref=src.at[d % 2], dst_ref=dst.at[d % 2], send_sem=load_sem.at[d],
            recv_sem=edge_recv.at[0, d], device_id=dst_dev[d], device_id_type=MESH,
        )

    def diag_of(e):
        return pltpu.make_async_remote_copy(
            src_ref=snd0_row.at[e // 2, pl.ds(0, 16)], dst_ref=rcv_diag.at[e],
            send_sem=load_sem.at[4 + e], recv_sem=diag_recv.at[e],
            device_id=diag_dev[e], device_id_type=MESH,
        )

    def copy_of(k, d):
        src, dst = (snd_row, rcv_row) if d < 2 else (snd_col, rcv_col)
        return pltpu.make_async_remote_copy(
            src_ref=src.at[k - 1, d % 2], dst_ref=dst.at[k - 1, d % 2], send_sem=load_sem.at[d],
            recv_sem=edge_recv.at[k % 2, d], device_id=dst_dev[d], device_id_type=MESH,
        )

    around = beside_al + beside_cs + beside_al * beside_cs

    def relay(k):
        if near_only:
            for flags, devices in ((has_dst, dst_dev), (diag_dst, diag_dev)):
                each(flags, lambda i: pl.semaphore_signal(
                    relay_sem.at[k], inc=1, device_id=devices[i], device_id_type=MESH))

    def relayed(k):
        if near_only:
            pl.semaphore_wait(relay_sem.at[k], around)

    def each(flags, action):
        for i in range(4):
            @pl.when(flags[i])
            def _():
                action(i)

    def fill(k, xn, xs, xw, xe):
        west = jnp.zeros((8, 128), f32)
        east = jnp.zeros((8, 128), f32)
        for f in range(12):
            snd_row[k - 1, 0, f:f + 1, :] = xn[f][0:1, :]
            snd_row[k - 1, 1, f:f + 1, :] = xs[f][7:8, :]
            west = jnp.where(lane == f, turn(xw[f], f, 1), west)
            east = jnp.where(lane == f, turn(xe[f], f + 1, 1), east)
        snd_col[k - 1, 0] = west
        snd_col[k - 1, 1] = east

    class Halo:
        def __init__(self, rows, cols):
            self.rows, self.cols = rows, cols

        def south(self, x, f):
            return jnp.where(row == 7, self.rows[0, f:f + 1, :], turn(x, 7, 0))

        def north(self, x, f):
            return jnp.where(row == 0, self.rows[1, f:f + 1, :], turn(x, 1, 0))

        def east(self, x, f):
            return jnp.where(lane == 127, turn(self.cols[0], 127 - f, 1), turn(x, 127, 1))

        def west(self, x, f):
            return jnp.where(lane == 0, turn(self.cols[1], -f, 1), turn(x, 1, 1))

        def around(self, x, f):
            return self.north(x, f), self.south(x, f), self.west(x, f), self.east(x, f)

    for load in loads[:5]:
        load.wait()
    V0 = [state_ref[f * 8:(f + 1) * 8, :] for f in range(12)]
    storm = [storm_ref[f * 8:(f + 1) * 8, :] for f in range(12)]
    wets = [wet_ref[t * 8:(t + 1) * 8, :].astype(f32) for t in range(2)]
    dunes = [dune_ref[t * 8:(t + 1) * 8, :].astype(f32) for t in range(2)]
    wash = [1.0 - dunes[t] for t in range(2)]
    cid = cid_ref[...]
    masks = [wets[0], dunes[0], cid.astype(f32)]
    for d, edge, inner in ((0, 0, 1), (1, 7, 6)):
        for f in range(12):
            snd0_row[d, f:f + 1, :] = V0[f][edge:edge + 1, :]
            snd0_row[d, NEXT + f:NEXT + f + 1, :] = V0[f][inner:inner + 1, :]
            snd0_row[d, STORM + f:STORM + f + 1, :] = storm[f][edge:edge + 1, :]
        for m in range(3):
            snd0_row[d, 12 + m:13 + m, :] = masks[m][edge:edge + 1, :]
        snd0_row[d, 15:16, :] = jnp.zeros((1, 128), f32)

    def column(edge, inner):
        out = jnp.zeros((8, 128), f32)
        for x, at, c in (
            [(V0[f], f, edge) for f in range(12)] + [(V0[f], NEXT + f, inner) for f in range(12)]
            + [(storm[f], COL_STORM + f, edge) for f in range(12)]
            + [(masks[m], COL_MASK + m, edge) for m in range(3)]
        ):
            out = jnp.where(lane == at, turn(x, at - c, 1), out)
        return out

    snd0_col[0] = column(0, 1)
    snd0_col[1] = column(127, 126)
    if near_only:
        pl.semaphore_wait(barrier, around)
    else:
        pl.semaphore_wait(barrier, ncs - 1 + nal - 1 + beside_al * beside_cs)
    for load in loads[5:]:
        load.wait()
    each(diag_dst, lambda e: diag_of(e).start())
    each(has_dst, lambda d: copy0_of(d).start())

    w1 = w1_ref[...]
    w1t = jnp.transpose(jnp.concatenate([w1, jnp.zeros((96, 128), f32)], axis=0))[:, :32]
    w2 = w2_ref[...]
    w1_cat = beside(*split(w1))
    w2_cat = beside(*split(0.5 * w2))
    b1_cols = bias_columns(0.5 * jnp.transpose(jnp.broadcast_to(b1_ref[...], (128, 128))))
    b2_cols = bias_columns(0.5 * jnp.transpose(jnp.broadcast_to(b2_ref[...], (128, 128))))
    w1t_cat = beside(*split(0.5 * w1t), b1_cols)
    w2t_cat = beside(*split(0.5 * jnp.transpose(w2)), b2_cols)
    wo_t = jnp.transpose(jnp.concatenate([wo_ref[...], jnp.zeros((120, 128), f32)], axis=0))[:, :8]

    def choose(unit, ids):
        onehot = (row == ids).astype(f32)
        wsel_ref[:, unit * 128:(unit + 1) * 128] = lax.dot_general(
            wo_t, onehot, (((1,), (0,)), ((), ())),
            precision=lax.Precision.HIGHEST, preferred_element_type=f32,
        )

    def bias_of(ids):
        b = jnp.zeros((8, 128), f32)
        for k in range(8):
            b = jnp.where(ids == k, bo_ref[0:1, k:k + 1], b)
        return b

    for u in range(OWN):
        choose(u, cid[ROW_OF_UNIT[u]:ROW_OF_UNIT[u] + 1, :])
    bsel = bias_of(cid)

    inner_units = list(range(INNER))
    edge_units = [INNER, INNER + 1, STRIP]

    def pairs(units):
        step = 3 if len(units) == 3 else 2
        return [units[i:i + step] for i in range(0, len(units), step)]

    def first_layer(t, unit, feats, kept):
        n = len(feats)
        at = pl.ds(unit * 128, n * 128)
        ones = jnp.ones((16, n * 128), bf16)
        F = jnp.concatenate(feats, axis=1) if n > 1 else feats[0]
        Fh, Fl = split(F)
        a, h = silu(mm(w1t_cat, jnp.concatenate([Fh, Fl, ones, Fh], axis=0)))
        Hh, Hl = split(h)
        if kept:
            f_ref[t, 0:32, at] = Fh
            f_ref[t, 32:64, at] = Fl
            act1_ref[t, :, at] = slope(a, h)
            h1_ref[t, 0:128, at] = Hh
            h1_ref[t, 128:256, at] = Hl
        return jnp.concatenate([Hh, Hl, ones, Hh], axis=0)

    def second_layer(t, unit, feats, kept, H):
        n = len(feats)
        at = pl.ds(unit * 128, n * 128)
        a, h = silu(mm(w2t_cat, H))
        wsel = wsel_ref[:, at]
        if kept:
            q2_ref[t, :, at] = wsel * slope(a, h)
            h2f_ref[t, :, at] = h
        z = jnp.sum(wsel * h, axis=0, keepdims=True)
        return [z[:, i * 128:(i + 1) * 128] for i in range(n)]

    def staggered(tasks, first, second):
        out, held = [], []
        for task in tasks:
            held.append((task, first(*task)))
            if len(held) > DEPTH:
                done, x = held.pop(0)
                out.append(second(*done, x))
        for done, x in held:
            out.append(second(*done, x))
        return out

    def layers(*tasks):
        return staggered(tasks, first_layer, second_layer)

    def settle(t, units):
        for part in pairs(units):
            at = pl.ds(part[0] * 128, len(part) * 128)
            Hh, Hl = split(h2f_ref[t, :, at])
            h2_ref[t, 0:128, at] = Hh
            h2_ref[t, 128:256, at] = Hl

    def put_features(V, near):
        for f in range(4):
            for part, x in enumerate((V[f],) + tuple(near[f])):
                feat_ref[(4 * part + f) * 8:(4 * part + f + 1) * 8, :] = x

    def feats_of(*rows):
        return [feat_ref[pl.ds(r, 32, stride=8), :] for r in rows]

    def own_layers(t, first, last):
        rows = [ROW_OF_UNIT[u:u + 2] for u in range(first, last, 2)]
        tasks = [(t, u, feats_of(*r), True) for u, r in zip(range(first, last, 2), rows)]
        for pair, out in zip(rows, layers(*tasks)):
            for r, z in zip(pair, out):
                z_ref[r:r + 1, :] = z

    in0_col[0] = column(1, 2)
    in0_col[1] = column(126, 125)
    dfeat_ref[...] = jnp.zeros_like(dfeat_ref)
    feat_ref[160:256, :] = storm_ref[...]
    put_features(V0, [
        (turn(V0[f], 1, 0), turn(V0[f], 7, 0), turn(V0[f], 1, 1), turn(V0[f], 127, 1)) for f in range(4)
    ])
    own_layers(0, 0, INNER)
    settle(0, inner_units)
    for ref, rows in ((f_ref, 64), (h1_ref, 256)):
        ref[:, rows:rows + 16, :] = jnp.ones((2, 16, ref.shape[2]), bf16)
    for ref in (zx_ref, cidx_ref, wetx_ref, dunex_ref):
        ref[...] = jnp.zeros_like(ref)
    spare = acc_ref.shape[0] - ROWS
    if spare:
        acc_ref[ROWS:, :] = jnp.zeros((spare, 128), f32)

    each(has_src, lambda d: copy0_of(d).wait_recv())
    each(diag_src, lambda e: diag_of(e).wait_recv())
    relay(0)

    halo0 = Halo(rcv0_row, rcv0_col)
    near0 = [halo0.around(V0[f], f) for f in range(12)]
    put_features(V0, near0)
    sides = jnp.concatenate(
        [
            rcv0_col[1], rcv0_col[0], snd0_col[0], snd0_col[1], in0_col[0], in0_col[1],
            jnp.zeros((80, 128), f32),
        ], axis=0
    )
    T = jnp.transpose(sides)
    SE, SW, NE, NW = [rcv_diag[e] for e in range(4)]
    RS, RN = rcv0_row[0, 0:16, :], rcv0_row[1, 0:16, :]
    group = lane16 // 8
    V, far = T[0:16], T[NEXT:NEXT + 16]
    plus, minus = turn(V, 16, 1), turn(V, -16, 1)
    N, S = turn(V, 1, 1), turn(V, -1, 1)
    for at, x, c in ((0, NW, 127), (8, NE, 0), (16, RN, 0), (24, RN, 127), (32, RN, 1), (40, RN, 126)):
        N = jnp.where(lane16 == at, turn(x, at - c, 1), N)
    for at, x, c in ((7, SW, 127), (15, SE, 0), (23, RS, 0), (31, RS, 127), (39, RS, 1), (47, RS, 126)):
        S = jnp.where(lane16 == at, turn(x, at - c, 1), S)
    W = jnp.where(group == 1, minus, jnp.where(jnp.logical_or(group == 2, group == 4), plus, far))
    E = jnp.where(group == 0, minus, jnp.where(jnp.logical_or(group == 3, group == 5), plus, far))
    outer = [(V, N, S, W, E)]
    for V, N, S, west, east in (
        (RN, rcv0_row[1, NEXT:NEXT + 16, :], snd0_row[0, 0:16, :], NW, NE),
        (RS, snd0_row[1, 0:16, :], rcv0_row[0, NEXT:NEXT + 16, :], SW, SE),
    ):
        W = jnp.where(lane16 == 0, turn(west, 1, 1), turn(V, 1, 1))
        E = jnp.where(lane16 == 127, turn(east, 127, 1), turn(V, 127, 1))
        outer.append((V, N, S, W, E))
    storms = [T[COL_STORM:COL_STORM + 12], rcv0_row[1, STORM:STORM + 12, :], rcv0_row[0, STORM:STORM + 12, :]]
    mask_rows = [
        [T[COL_MASK + m:COL_MASK + m + 1] for m in range(3)],
        [rcv0_row[1, 12 + m:13 + m, :] for m in range(3)],
        [rcv0_row[0, 12 + m:13 + m, :] for m in range(3)],
    ]
    for w in range(3):
        for part in range(5):
            fx_ref[w, 4 * part:4 * part + 4, :] = outer[w][part][0:4]
        fx_ref[w, 20:32, :] = storms[w]
        wetx_ref[w:w + 1, :] = mask_rows[w][0]
        dunex_ref[w:w + 1, :] = mask_rows[w][1]
        ids = mask_rows[w][2].astype(jnp.int32)
        cidx_ref[w:w + 1, :] = ids
        choose(STRIP + w, ids)
    cidx = cidx_ref[...]
    (z_top, z_low), (z_strip,), (z_north, z_south) = layers(
        (0, INNER, feats_of(0, 7), True), (0, STRIP, [fx_ref[0]], True),
        (0, STRIP + 1, [fx_ref[1], fx_ref[2]], False),
    )
    z_ref[0:1, :] = z_top
    z_ref[7:8, :] = z_low
    zx_ref[0:1, :] = z_strip
    zx_ref[1:2, :] = z_north
    zx_ref[2:3, :] = z_south
    biasx = bias_of(cidx)
    zx = zx_ref[...] + biasx
    pickx = pickup_gain * softplus(zx) * (1.0 - dunex_ref[...])

    def from_strip(x, start):
        return jnp.sum(jnp.where(lane == start + row, x, 0.0), axis=1, keepdims=True)

    inside = jnp.logical_and(row > 0, row < 7)
    at_west = jnp.logical_and(inside, lane == 0)
    at_east = jnp.logical_and(inside, lane == 127)

    def with_strip(z, strip):
        z = jnp.where(at_west, from_strip(strip, 16), z)
        return jnp.where(at_east, from_strip(strip, 24), z)

    def to_strip(x):
        out = jnp.where(lane == 16 + row, x[:, 0:1], jnp.where(lane == 24 + row, x[:, 127:128], 0.0))
        return jnp.sum(jnp.where(inside, out, 0.0), axis=0, keepdims=True)

    z0 = with_strip(z_ref[...] + bsel, zx[0:1, :])

    def advanced(w):
        V, N, S, W, E = outer[w]
        pick, wet = pickx[w:w + 1, :], wetx_ref[w:w + 1, :]
        lap = N + S + W + E - 4.0 * V
        ad, cd = S - N, E - W
        spread = jnp.where(field == 3, bed_diffusion, diffusion) * lap
        sediment = spread - advection * (V[1:2] * ad + V[2:3] * cd) - settling * V
        sediment = sediment + jnp.where(field - 4 == cidx[w:w + 1, :], pick, 0.0)
        total = jnp.sum(
            jnp.where(jnp.logical_and(field >= 4, field < 12), V, 0.0), axis=0, keepdims=True
        )
        first = jnp.where(field == 0, -advection * (ad[1:2] + cd[2:3]), settling * total - pick)
        first = jnp.where(field == 1, -advection * ad[0:1] - friction * V[1:2], first)
        first = jnp.where(field == 2, -advection * cd[0:1] - friction * V[2:3], first)
        return V + wet * jnp.where(field < 4, spread + first, sediment)

    strip1, RN, RS = advanced(0), advanced(1), advanced(2)
    ring_row[1] = RN
    ring_row[0] = RS
    back = jnp.transpose(jnp.concatenate([strip1, jnp.zeros((112, 128), f32)], axis=0))
    ring_col[1] = back[0:8]
    ring_col[0] = back[8:16]

    pickup = softplus(z0) * wash[0]
    lap = []
    for f in range(12):
        n, s, w, e = near0[f]
        lap.append(n + s + w + e - 4.0 * V0[f])
    total = V0[4]
    for k in range(1, 8):
        total = total + V0[4 + k]
    ad = [near0[f][1] - near0[f][0] for f in range(12)]
    cd = [near0[f][3] - near0[f][2] for f in range(12)]
    tend = [
        diffusion * lap[0] - advection * (ad[1] + cd[2]),
        diffusion * lap[1] - advection * ad[0] - friction * V0[1],
        diffusion * lap[2] - advection * cd[0] - friction * V0[2],
        bed_diffusion * lap[3] - pickup_gain * pickup + settling * total,
    ]
    for k in range(8):
        x = diffusion * lap[4 + k] - advection * (V0[1] * ad[4 + k] + V0[2] * cd[4 + k])
        x = x + jnp.where(cid == k, pickup_gain * pickup, 0.0) - settling * V0[4 + k]
        tend.append(x)
    V1 = [V0[f] + wets[0] * tend[f] for f in range(12)]

    halo1 = Halo(ring_row, ring_col)
    near1 = [halo1.around(V1[f], f) for f in range(12)]
    put_features(V1, near1)
    plus, minus = turn(strip1, 16, 1), turn(strip1, -16, 1)
    N, S = turn(strip1, 1, 1), turn(strip1, -1, 1)
    for at, c in ((16, 0), (24, 127)):
        N = jnp.where(lane16 == at, turn(RN, at - c, 1), N)
        S = jnp.where(lane16 == at + 7, turn(RS, at + 7 - c, 1), S)
    W, E = jnp.where(group == 2, plus, minus), jnp.where(group == 2, minus, plus)
    for part, x in enumerate((strip1, N, S, W, E)):
        fx_ref[0, 4 * part:4 * part + 4, :] = x[0:4]
    (z_top, z_low), (z_strip,) = layers(
        (1, INNER, feats_of(0, 7), True), (1, STRIP, [fx_ref[0]], True)
    )
    z_ref[0:1, :] = z_top
    z_ref[7:8, :] = z_low
    z_strip = z_strip + biasx[0:1, :]
    relayed(0)
    relay(1)
    z1 = with_strip(z_ref[...] + bsel, z_strip)
    lam2 = [cot_ref[f * 8:(f + 1) * 8, :] for f in range(12)]

    def closure_cotangent(t, gate, lam):
        G = [None] * 3 + [wets[t] * lam[f] for f in range(3, 12)]
        picked = G[4]
        for k in range(1, 8):
            picked = jnp.where(cid == k, G[4 + k], picked)
        return pickup_gain * (picked - G[3]) * wash[t] * gate

    def sigmoid(z):
        return 1.0 / (1.0 + jnp.exp(-z))

    def adjoint_two(t, units, drows):
        for part in pairs(list(zip(units, drows))):
            at = pl.ds(part[0][0] * 128, len(part) * 128)
            drow = 0.5 * jnp.concatenate([d for _, d in part], axis=1)
            Dh, Dl = split(q2_ref[t, :, at] * drow)
            d2_ref[t, 0:128, at] = Dh
            d2_ref[t, 128:256, at] = Dl

    def adjoint_one(t, units):
        def product(part):
            at = pl.ds(part[0] * 128, len(part) * 128)
            return mm(w2_cat, jnp.concatenate([d2_ref[t, :, at], d2_ref[t, 0:128, at]], axis=0))

        def rest(part, d1):
            at = pl.ds(part[0] * 128, len(part) * 128)
            Dh, Dl = split(d1 * act1_ref[t, :, at])
            d1_ref[t, 0:128, at] = Dh
            d1_ref[t, 128:256, at] = Dl

        staggered([(part,) for part in pairs(units)], product, rest)

    def feature_cotangent(t, units):
        out = []

        def product(part):
            at = pl.ds(part[0] * 128, len(part) * 128)
            return mm(w1_cat, jnp.concatenate([d1_ref[t, :, at], d1_ref[t, 0:128, at]], axis=0))

        def rest(part, dF):
            for i, u in enumerate(part):
                one = dF[:, i * 128:(i + 1) * 128]
                if u < OWN:
                    dfeat_ref[pl.ds(ROW_OF_UNIT[u], 32, stride=8), :] = one
                else:
                    out.append(one)

        staggered([(part,) for part in pairs(units)], product, rest)
        return out

    def adjoint_cells(D, G, near, V, lam):
        lap = [bed_diffusion if f == 3 else diffusion for f in range(12)]
        lg = [lap[f] * G[f] for f in range(12)]
        c = [lam[f] - 4.0 * lg[f] for f in range(12)]
        alongs = jnp.zeros((8, 128), f32)
        crosses = jnp.zeros((8, 128), f32)
        along_part = [advection * G[1], advection * G[0], None, None]
        cross_part = [advection * G[2], None, advection * G[0], None]
        for k in range(8):
            n, s, w, e = near[4 + k]
            alongs = alongs + (s - n) * G[4 + k]
            crosses = crosses + (e - w) * G[4 + k]
            c[4 + k] = c[4 + k] + settling * (G[3] - G[4 + k])
            ag = advection * G[4 + k]
            along_part.append(V[1] * ag)
            cross_part.append(V[2] * ag)
        c[1] = c[1] - friction * G[1] - advection * alongs
        c[2] = c[2] - friction * G[2] - advection * crosses
        to = [[], [], [], []]
        for f in range(12):
            for d, part, sign in ((0, along_part, 1), (1, along_part, -1), (2, cross_part, 1), (3, cross_part, -1)):
                x = lg[f]
                if part[f] is not None:
                    x = x + part[f] if sign > 0 else x - part[f]
                if f < 4:
                    x = x + D[4 + 4 * d + f]
                to[d].append(x)
            if f < 4:
                c[f] = c[f] + D[f]
        return c, to

    def gather(c, to, halo):
        return [
            c[f] + halo.south(to[0][f], f) + halo.north(to[1][f], f)
            + halo.east(to[2][f], f) + halo.west(to[3][f], f)
            for f in range(12)
        ]

    def keep(start, part, first):
        at = pl.ds(start, part.shape[0])
        acc_ref[at, :] = part if first else acc_ref[at, :] + part

    def weights_two(t, units, ids, drows, first):
        at = pl.ds(units[0] * 128, len(units) * 128)
        width = len(units) * 128
        dr = jnp.concatenate(
            [jnp.where(row == k, d, 0.0) for k, d in zip(ids, drows)], axis=1
        )
        dbo = jnp.sum(
            jnp.where(row == lane, jnp.sum(dr, axis=1, keepdims=True), 0.0), axis=0, keepdims=True
        )
        drh, drl = split(jnp.concatenate([dr, jnp.zeros((8, width), f32)], axis=0))
        top = mm_nt(jnp.concatenate([drh, drl], axis=0), h2_ref[t, :, at])
        dwo = top[:8, :128] + top[16:24, :128] + top[:8, 128:]
        top = mm_nt(h1_ref[t, :, at], d2_ref[t, :, at])
        keep(0, top[:128, :128] + top[128:256, :128] + top[:128, 128:], first)
        keep(ROW_WO, dwo, first)
        ones = top[256:264, :128] + top[256:264, 128:]
        keep(ROW_BIAS, jnp.where(row == 1, ones, jnp.where(row == 2, dbo, 0.0)), first)

    def weights_one(t, units, first):
        at = pl.ds(units[0] * 128, len(units) * 128)
        top = mm_nt(f_ref[t, :, at], d1_ref[t, :, at])
        keep(ROW_W1, top[:32, :128] + top[32:64, :128] + top[:32, 128:], first)
        ones = top[64:72, :128] + top[64:72, 128:]
        keep(ROW_BIAS, jnp.where(row == 0, ones, 0.0), False)

    def rows_of(x, units):
        return [x[ROW_OF_UNIT[u]:ROW_OF_UNIT[u] + 1, :] for u in units]

    G1 = [wets[1] * lam2[f] for f in range(12)]
    columns = jnp.logical_and(lane > 0, lane < 127)

    def patched(strip_back):
        turned = jnp.transpose(jnp.concatenate([strip_back, jnp.zeros((96, 128), f32)], axis=0))
        at_w, at_e = turned[16:24], turned[24:32]
        out = []
        for f in range(20):
            x = dfeat_ref[f * 8:(f + 1) * 8, :]
            x = jnp.where(at_west, turn(at_w, -f, 1), x)
            out.append(jnp.where(at_east, turn(at_e, 127 - f, 1), x))
        return out

    dz1 = closure_cotangent(1, sigmoid(z1), lam2)
    edge_rows1 = [dz1[0:1, :], dz1[7:8, :], to_strip(dz1)]
    adjoint_two(1, edge_units, edge_rows1)
    adjoint_one(1, edge_units)
    strip_back = feature_cotangent(1, edge_units)[0]
    _, to1 = adjoint_cells(patched(strip_back), G1, near1, V1, lam2)
    fill(1, *to1)
    each(has_dst, lambda d: copy0_of(d).wait_send())
    each(has_dst, lambda d: copy_of(1, d).start())

    own_layers(1, 0, INNER)
    dz1 = closure_cotangent(1, sigmoid(z_ref[...] + bsel), lam2)
    dz_ref[...] = jnp.where(columns, dz1, 0.0)
    drows1 = rows_of(dz_ref, inner_units)
    adjoint_two(1, inner_units, drows1)
    adjoint_one(1, inner_units)
    feature_cotangent(1, inner_units)
    c1, to1 = adjoint_cells(patched(strip_back), G1, near1, V1, lam2)
    gate0 = sigmoid(z0)
    settle(1, inner_units + edge_units)
    settle(0, edge_units)
    ids_edge = [cid[0:1, :], cid[7:8, :], cidx_ref[0:1, :]]
    weights_two(
        1, inner_units + edge_units, rows_of(cid, inner_units) + ids_edge, drows1 + edge_rows1, True
    )
    weights_one(1, inner_units + edge_units, True)
    lam1 = [
        c1[f] + turn(to1[0][f], 7, 0) + turn(to1[1][f], 1, 0) + turn(to1[2][f], 127, 1) + turn(to1[3][f], 1, 1)
        for f in range(12)
    ]
    dz0 = closure_cotangent(0, gate0, lam1)
    dz_ref[...] = jnp.where(columns, dz0, 0.0)
    drows0 = rows_of(dz_ref, inner_units)
    adjoint_two(0, inner_units, drows0)
    weights_two(0, inner_units, rows_of(cid, inner_units), drows0, False)
    adjoint_one(0, inner_units)
    weights_one(0, inner_units, False)
    feature_cotangent(0, inner_units)

    each(has_src, lambda d: copy_of(1, d).wait_recv())
    relayed(1)
    lam1 = gather(c1, to1, Halo(rcv_row.at[0], rcv_col.at[0]))
    dz0 = closure_cotangent(0, gate0, lam1)
    drows0 = [dz0[0:1, :], dz0[7:8, :], to_strip(dz0)]
    adjoint_two(0, edge_units, drows0)
    weights_two(0, edge_units, ids_edge, drows0, False)
    adjoint_one(0, edge_units)
    weights_one(0, edge_units, False)

    size = src_b.shape[0]
    last_core = nsu - 1
    owner = su == last_core
    piece = al * ncr + cr if direct else cs
    mine = pl.ds(pl.multiple_of(piece * size, 8), size)
    spans = [(dz, dx) for dz in range(nal) for dx in range(ncr)]

    sense = 1 - 2 * ((2 * al) // nal)

    def chip_at(span):
        return lax.rem(al + nal + sense * span[0], nal), lax.rem(cr + span[1], ncr)

    after = max(ncs, nal) - 1

    def to_owner(k):
        a, c = chip_at(spans[k])
        source = lax.rem(al - a + nal, nal) * ncr + lax.rem(cr - c + ncr, ncr)
        slot = 2 * (source - 1) + su if k else 2 * (len(spans) - 1)
        at = pl.ds(pl.multiple_of((a * ncr + c) * size, 8), size)
        return pltpu.make_async_remote_copy(
            src_ref=acc_ref.at[at, :], dst_ref=rcv_a.at[slot], send_sem=load_sem.at[8],
            recv_sem=load_sem.at[10], device_id=(g, a, c, last_core), device_id_type=MESH,
        )

    def from_owner(k, core):
        a, c = chip_at(spans[k])
        return pltpu.make_async_remote_copy(
            src_ref=full_ref.at[mine, :], dst_ref=full_ref.at[mine, :], send_sem=load_sem.at[9],
            recv_sem=load_sem.at[11], device_id=(g, a, c, core), device_id_type=MESH,
        )

    def all_of(ref, sem):
        return pltpu.make_async_remote_copy(
            src_ref=ref, dst_ref=ref, send_sem=sem, recv_sem=sem,
            device_id=(g, al, cr, nsu - 1 - su), device_id_type=MESH,
        )

    def copy_a(j):
        peer = lax.rem(cs + j, ncs)
        return pltpu.make_async_remote_copy(
            src_ref=acc_ref.at[pl.ds(pl.multiple_of(peer * size, 8), size), :],
            dst_ref=rcv_a.at[j - 1], send_sem=sum_sem.at[j - 1], recv_sem=sum_sem.at[after + j - 1],
            device_id=dev(al, peer), device_id_type=MESH,
        )

    def copy_b(j):
        return pltpu.make_async_remote_copy(
            src_ref=src_b, dst_ref=rcv_b.at[al], send_sem=sum_sem.at[j - 1],
            recv_sem=sum_sem.at[after + 2 * ncs + j - 3],
            device_id=dev(lax.rem(al + j, nal), cs), device_id_type=MESH,
        )

    def copy_c(j):
        return pltpu.make_async_remote_copy(
            src_ref=full_ref.at[mine, :], dst_ref=full_ref.at[mine, :],
            send_sem=sum_sem.at[j - 1], recv_sem=sum_sem.at[after + ncs + j - 2],
            device_id=dev(al, lax.rem(cs + j, ncs)), device_id_type=MESH,
        )

    others = len(spans) - 1
    if direct:
        for k in range(others, 0, -1):
            to_owner(k).start()

        @pl.when(jnp.logical_not(owner))
        def _():
            to_owner(0).start()
    else:
        for j in range(1, ncs):
            copy_a(j).start()

    D0 = patched(feature_cotangent(0, edge_units)[0])
    G0 = [wets[0] * lam1[f] for f in range(12)]
    c0, to0 = adjoint_cells(D0, G0, near0, V0, lam1)
    fill(2, *to0)
    each(has_dst, lambda d: copy_of(1, d).wait_send())
    each(has_dst, lambda d: copy_of(2, d).start())

    if direct:
        @pl.when(owner)
        def _():
            all_of(rcv_a, load_sem.at[10]).wait_recv()
            total = acc_ref[mine, :]
            for j in range(rcv_a.shape[0]):
                total = total + rcv_a[j]
            full_ref[mine, :] = total * factor
            for k in range(others, -1, -1):
                for core in range(nsu):
                    if k or core != last_core:
                        from_owner(k, core).start()
    else:
        total = acc_ref[mine, :]
        for j in range(1, ncs):
            copy_a(j).wait_recv()
            total = total + rcv_a[j - 1]
        src_b[...] = total
        rcv_b[al] = total
        for j in range(1, ncs):
            copy_a(j).wait_send()
        for j in range(1, nal):
            copy_b(j).start()
    each(has_src, lambda d: copy_of(2, d).wait_recv())
    last = gather(c0, to0, Halo(rcv_row.at[1], rcv_col.at[1]))
    for f in range(12):
        gstate_ref[f] = last[f]
    each(has_dst, lambda d: copy_of(2, d).wait_send())
    each(diag_dst, lambda e: diag_of(e).wait_send())
    if direct:
        @pl.when(owner)
        def _():
            all_of(acc_ref.at[pl.ds(0, others * size), :], load_sem.at[8]).wait_send()
            all_of(full_ref.at[pl.ds(0, others * size), :], load_sem.at[11]).wait_recv()
            all_of(rcv_a, load_sem.at[9]).wait_send()

        @pl.when(jnp.logical_not(owner))
        def _():
            all_of(acc_ref, load_sem.at[8]).wait_send()
            all_of(full_ref, load_sem.at[11]).wait_recv()
    else:
        for j in range(1, nal):
            copy_b(j).wait_recv()
        total = rcv_b[0]
        for j in range(1, nal):
            total = total + rcv_b[j]
        full_ref[mine, :] = total * factor
        for j in range(1, nal):
            copy_b(j).wait_send()
        for j in range(1, ncs):
            copy_c(j).start()
        for j in range(1, ncs):
            copy_c(j).wait_recv()
        for j in range(1, ncs):
            copy_c(j).wait_send()


def unpack(
    state_ref, full_ref,
    gs_hbm, gw1_hbm, gb1_hbm, gw2_hbm, gb2_hbm, gwo_hbm, gbo_hbm, gbo_ref, sem,
):
    gbo_ref[...] = full_ref[ROW_BIAS + 2:ROW_BIAS + 3, 0:8]
    parts = (
        (full_ref.at[0:128], gw2_hbm), (state_ref, gs_hbm), (full_ref.at[ROW_W1:ROW_W1 + 32], gw1_hbm),
        (full_ref.at[ROW_WO:ROW_WO + 8], gwo_hbm), (full_ref.at[ROW_BIAS:ROW_BIAS + 1], gb1_hbm),
        (full_ref.at[ROW_BIAS + 1:ROW_BIAS + 2], gb2_hbm), (gbo_ref, gbo_hbm),
    )
    copies = [pltpu.make_async_copy(src, dst, sem.at[i]) for i, (src, dst) in enumerate(parts)]
    for copy in copies:
        copy.start()
    for copy in copies:
        copy.wait()


def solution(mesh):
    nal, ncr, nsu = mesh.shape["along"], mesh.shape["cross"], mesh.shape["sub"]
    ncs = ncr * nsu
    near_only = nal <= 4 and ncs <= 4
    direct = near_only and nsu == 2
    owners = nal * ncr if direct else ncs
    size = 8 * (-(-ROWS // (8 * owners)))

    def per_device(state, storm, wet, dune, cid, w1, b1, w2, b2, wo, bo, cot):
        rows, cols = state.shape[1], state.shape[2]
        factor = 1.0 / math.sqrt(rows * nal * cols * ncs)
        vmem = pl.BlockSpec(memory_space=pltpu.VMEM)
        hbm = pl.BlockSpec(memory_space=pl.ANY)
        flat = lambda x: x.reshape(-1, 128)
        operands = (
            flat(state), cid, w1, b1.reshape(1, 128), w2, b2.reshape(1, 128), wo.T, bo.reshape(1, 8),
            flat(storm), flat(wet), flat(dune), flat(cot),
        )
        dma = pltpu.SemaphoreType.DMA
        tile = pltpu.VMEM((8, 128), f32)
        big = lambda n, kind: pltpu.VMEM((2, n, (OWN + 1) * 128), kind)
        out = pl.pallas_call(
            functools.partial(kernel, nal, ncr, nsu, near_only, direct, factor),
            out_shape=(pltpu.VMEM((12, 8, 128), f32), pltpu.VMEM((owners * size, 128), f32)),
            in_specs=[hbm] * 12,
            out_specs=(vmem,) * 2,
            scratch_shapes=[
                *[pltpu.VMEM(x.shape, x.dtype) for x in operands],
                dma((12,)),
                pltpu.VMEM((2, 40, 128), f32),
                pltpu.VMEM((2, 8, 128), f32),
                pltpu.VMEM((2, 8, 128), f32),
                pltpu.VMEM((2, 40, 128), f32),
                pltpu.VMEM((2, 8, 128), f32),
                pltpu.VMEM((4, 16, 128), f32),
                pltpu.VMEM((2, 2, 16, 128), f32),
                pltpu.VMEM((2, 2, 8, 128), f32),
                pltpu.VMEM((2, 2, 16, 128), f32),
                pltpu.VMEM((2, 2, 8, 128), f32),
                pltpu.VMEM((2, 16, 128), f32),
                pltpu.VMEM((2, 8, 128), f32),
                dma((2, 4)), dma((4,)), pltpu.SemaphoreType.REGULAR((2,)),
                pltpu.VMEM((256, 128), f32),
                pltpu.VMEM((256, 128), f32),
                pltpu.VMEM((3, 32, 128), f32),
                tile, tile, tile, pltpu.VMEM((8, 128), jnp.int32), tile, tile,
                pltpu.VMEM((128, (OWN + 3) * 128), f32), big(128, f32),
                big(80, bf16), big(272, bf16), big(256, bf16), big(128, f32), big(128, f32),
                big(256, bf16), big(256, bf16),
                pltpu.VMEM((owners * size, 128), f32),
                pltpu.VMEM((nsu * owners - 1 if direct else ncs - 1, size, 128), f32),
                pltpu.VMEM((size, 128), f32),
                pltpu.VMEM((1 if direct else nal, size, 128), f32),
                dma((1 if direct else max(ncs, nal) + 2 * ncs + nal - 4,)),
            ],
            compiler_params=pltpu.CompilerParams(collective_id=0, has_side_effects=True),
        )(*operands)
        gs, gw1, gb1, gw2, gb2, gwo, gbo = pl.pallas_call(
            unpack,
            out_shape=(
                jax.ShapeDtypeStruct((12, 8, 128), f32),
                jax.ShapeDtypeStruct((32, 128), f32),
                jax.ShapeDtypeStruct((1, 128), f32),
                jax.ShapeDtypeStruct((128, 128), f32),
                jax.ShapeDtypeStruct((1, 128), f32),
                jax.ShapeDtypeStruct((8, 128), f32),
                jax.ShapeDtypeStruct((1, 8), f32),
            ),
            in_specs=[vmem] * 2,
            out_specs=(hbm,) * 7,
            scratch_shapes=[pltpu.VMEM((1, 8), f32), dma((7,))],
        )(*[pltpu.with_memory_space_constraint(x, pltpu.VMEM) for x in out])
        return gs, gw1, gb1.reshape(128), gw2, gb2.reshape(128), gwo.T, gbo.reshape(8)

    tile = P(None, ("groups", "along"), ("cross", "sub"))
    return jax.shard_map(
        per_device,
        mesh=mesh,
        in_specs=(
            tile, tile, tile, tile, P(("groups", "along"), ("cross", "sub")),
            P(), P(), P(), P(), P(), P(), tile,
        ),
        out_specs=(
            tile, P("groups", None), P("groups"), P("groups", None), P("groups"),
            P("groups", None), P("groups"),
        ),
        check_vma=False,
    )
```

```python
import functools
import math

import jax
import jax.numpy as jnp
from jax import lax
from jax.experimental import pallas as pl
from jax.experimental.pallas import tpu as pltpu
from jax.sharding import PartitionSpec as P

MESH = pl.DeviceIdType.MESH
f32 = jnp.float32
bf16 = jnp.bfloat16
diffusion = 0.15
advection = 0.2
friction = 0.05
pickup_gain = 0.5
settling = 0.2
bed_diffusion = 0.1

ROW_W1 = 128
ROW_WO = 160
ROW_BIAS = 168
ROWS = 176
ROW_OF_UNIT = (1, 2, 3, 4, 5, 6, 0, 7)
INNER = 6
DEPTH = 2
OWN = 8
STRIP = 8
NEXT = 16
STORM = 28
COL_STORM = 32
COL_MASK = 44


def split(x):
    high = x.astype(bf16)
    low = (x - high.astype(f32)).astype(bf16)
    return high, low


def mm(a, b):
    return lax.dot_general(a, b, (((1,), (0,)), ((), ())), preferred_element_type=f32)


def mm_nt(a, b):
    return lax.dot_general(a, b, (((1,), (1,)), ((), ())), preferred_element_type=f32)


def beside(high, low, *extra):
    return jnp.concatenate([high, high, *extra, low], axis=1)


def bias_columns(spread):
    high = spread.astype(bf16)
    rest = spread - high.astype(f32)
    middle = rest.astype(bf16)
    low = (rest - middle.astype(f32)).astype(bf16)
    lane = lax.broadcasted_iota(jnp.int32, spread.shape, 1)
    out = jnp.zeros_like(spread)
    for i, part in enumerate((high, middle, low)):
        out = jnp.where(lane == i, part.astype(f32), out)
    return out[:, :16].astype(bf16)


def silu(u):
    a = 1.0 + jnp.tanh(u)
    return a, u * a


def slope(a, h):
    return h * (2.0 - a) + a


def softplus(z):
    return jnp.maximum(z, 0.0) + jnp.log(1.0 + jnp.exp(-jnp.abs(z)))


def kernel(
    nal, ncr, nsu, near_only, direct, factor,
    state_hbm, cid_hbm, w1_hbm, b1_hbm, w2_hbm, b2_hbm, wo_hbm, bo_hbm,
    storm_hbm, wet_hbm, dune_hbm, cot_hbm,
    gstate_ref, full_ref,
    state_ref, cid_ref, w1_ref, b1_ref, w2_ref, b2_ref, wo_ref, bo_ref,
    storm_ref, wet_ref, dune_ref, cot_ref, load_sem,
    snd0_row, snd0_col, in0_col, rcv0_row, rcv0_col, rcv_diag,
    snd_row, snd_col, rcv_row, rcv_col, ring_row, ring_col,
    edge_recv, diag_recv, relay_sem,
    feat_ref, dfeat_ref, fx_ref, z_ref, zx_ref, dz_ref, cidx_ref, wetx_ref, dunex_ref,
    wsel_ref, h2f_ref,
    f_ref, h1_ref, h2_ref, act1_ref, q2_ref, d1_ref, d2_ref,
    acc_ref, rcv_a, rcv_e, src_b, rcv_b,
    sum_sem,
):
    ncs = ncr * nsu
    g = lax.axis_index("groups")
    al = lax.axis_index("along")
    cr = lax.axis_index("cross")
    su = lax.axis_index("sub")
    cs = cr * nsu + su

    def dev(a, c):
        return (g, a, c // nsu, c % nsu)

    has_dst = (al > 0, al < nal - 1, cs > 0, cs < ncs - 1)
    has_src = (al < nal - 1, al > 0, cs < ncs - 1, cs > 0)
    dst_dev = (
        dev(al - 1, cs), dev(al + 1, cs), dev(al, cs - 1), dev(al, cs + 1),
    )
    corners = ((0, 2), (0, 3), (1, 2), (1, 3))
    diag_dst = [jnp.logical_and(has_dst[a], has_dst[c]) for a, c in corners]
    diag_src = [jnp.logical_and(has_src[a], has_src[c]) for a, c in corners]
    diag_dev = [dev(al + (1 if a else -1), cs + (1 if c == 3 else -1)) for a, c in corners]

    loads = [
        pltpu.make_async_copy(src, dst, load_sem.at[i])
        for i, (src, dst) in enumerate((
            (state_hbm, state_ref), (storm_hbm, storm_ref), (wet_hbm, wet_ref), (dune_hbm, dune_ref),
            (cid_hbm, cid_ref), (w1_hbm, w1_ref), (b1_hbm, b1_ref), (w2_hbm, w2_ref),
            (b2_hbm, b2_ref), (wo_hbm, wo_ref), (bo_hbm, bo_ref), (cot_hbm, cot_ref),
        ))
    ]
    for load in loads[:5]:
        load.start()
    for ref in (rcv0_row, rcv0_col, rcv_diag, rcv_row, rcv_col):
        ref[...] = jnp.zeros_like(ref)

    barrier = pltpu.get_barrier_semaphore()
    for e in range(4):
        @pl.when(diag_dst[e])
        def _():
            pl.semaphore_signal(barrier, inc=1, device_id=diag_dev[e], device_id_type=MESH)
    if near_only:
        for d in range(4):
            @pl.when(has_dst[d])
            def _():
                pl.semaphore_signal(barrier, inc=1, device_id=dst_dev[d], device_id_type=MESH)
    else:
        for j in range(1, ncs):
            pl.semaphore_signal(
                barrier, inc=1, device_id=dev(al, lax.rem(cs + j, ncs)), device_id_type=MESH
            )
        for j in range(1, nal):
            pl.semaphore_signal(
                barrier, inc=1, device_id=dev(lax.rem(al + j, nal), cs), device_id_type=MESH
            )
    for load in loads[5:]:
        load.start()
    beside_al = (al + nal - 1) // nal + (2 * nal - 2 - al) // nal
    beside_cs = (cs + ncs - 1) // ncs + (2 * ncs - 2 - cs) // ncs

    row = lax.broadcasted_iota(jnp.int32, (8, 128), 0)
    lane = lax.broadcasted_iota(jnp.int32, (8, 128), 1)
    field = lax.broadcasted_iota(jnp.int32, (16, 128), 0)
    lane16 = lax.broadcasted_iota(jnp.int32, (16, 128), 1)

    def turn(x, shift, axis):
        shift = shift % x.shape[axis]
        return pltpu.roll(x, shift, axis) if shift else x

    def copy0_of(d):
        src, dst = (snd0_row, rcv0_row) if d < 2 else (snd0_col, rcv0_col)
        return pltpu.make_async_remote_copy(
            src_ref=src.at[d % 2], dst_ref=dst.at[d % 2], send_sem=load_sem.at[d],
            recv_sem=edge_recv.at[0, d], device_id=dst_dev[d], device_id_type=MESH,
        )

    def diag_of(e):
        return pltpu.make_async_remote_copy(
            src_ref=snd0_row.at[e // 2, pl.ds(0, 16)], dst_ref=rcv_diag.at[e],
            send_sem=load_sem.at[4 + e], recv_sem=diag_recv.at[e],
            device_id=diag_dev[e], device_id_type=MESH,
        )

    def copy_of(k, d):
        src, dst = (snd_row, rcv_row) if d < 2 else (snd_col, rcv_col)
        return pltpu.make_async_remote_copy(
            src_ref=src.at[k - 1, d % 2], dst_ref=dst.at[k - 1, d % 2], send_sem=load_sem.at[d],
            recv_sem=edge_recv.at[k % 2, d], device_id=dst_dev[d], device_id_type=MESH,
        )

    around = beside_al + beside_cs + beside_al * beside_cs

    def relay(k):
        if near_only:
            for flags, devices in ((has_dst, dst_dev), (diag_dst, diag_dev)):
                each(flags, lambda i: pl.semaphore_signal(
                    relay_sem.at[k], inc=1, device_id=devices[i], device_id_type=MESH))

    def relayed(k):
        if near_only:
            pl.semaphore_wait(relay_sem.at[k], around)

    def each(flags, action):
        for i in range(4):
            @pl.when(flags[i])
            def _():
                action(i)

    def fill(k, xn, xs, xw, xe):
        west = jnp.zeros((8, 128), f32)
        east = jnp.zeros((8, 128), f32)
        for f in range(12):
            snd_row[k - 1, 0, f:f + 1, :] = xn[f][0:1, :]
            snd_row[k - 1, 1, f:f + 1, :] = xs[f][7:8, :]
            west = jnp.where(lane == f, turn(xw[f], f, 1), west)
            east = jnp.where(lane == f, turn(xe[f], f + 1, 1), east)
        snd_col[k - 1, 0] = west
        snd_col[k - 1, 1] = east

    class Halo:
        def __init__(self, rows, cols):
            self.rows, self.cols = rows, cols

        def south(self, x, f):
            return jnp.where(row == 7, self.rows[0, f:f + 1, :], turn(x, 7, 0))

        def north(self, x, f):
            return jnp.where(row == 0, self.rows[1, f:f + 1, :], turn(x, 1, 0))

        def east(self, x, f):
            return jnp.where(lane == 127, turn(self.cols[0], 127 - f, 1), turn(x, 127, 1))

        def west(self, x, f):
            return jnp.where(lane == 0, turn(self.cols[1], -f, 1), turn(x, 1, 1))

        def around(self, x, f):
            return self.north(x, f), self.south(x, f), self.west(x, f), self.east(x, f)

    for load in loads[:5]:
        load.wait()
    V0 = [state_ref[f * 8:(f + 1) * 8, :] for f in range(12)]
    storm = [storm_ref[f * 8:(f + 1) * 8, :] for f in range(12)]
    wets = [wet_ref[t * 8:(t + 1) * 8, :].astype(f32) for t in range(2)]
    dunes = [dune_ref[t * 8:(t + 1) * 8, :].astype(f32) for t in range(2)]
    wash = [1.0 - dunes[t] for t in range(2)]
    cid = cid_ref[...]
    masks = [wets[0], dunes[0], cid.astype(f32)]
    for d, edge, inner in ((0, 0, 1), (1, 7, 6)):
        for f in range(12):
            snd0_row[d, f:f + 1, :] = V0[f][edge:edge + 1, :]
            snd0_row[d, NEXT + f:NEXT + f + 1, :] = V0[f][inner:inner + 1, :]
            snd0_row[d, STORM + f:STORM + f + 1, :] = storm[f][edge:edge + 1, :]
        for m in range(3):
            snd0_row[d, 12 + m:13 + m, :] = masks[m][edge:edge + 1, :]
        snd0_row[d, 15:16, :] = jnp.zeros((1, 128), f32)

    def column(edge, inner):
        out = jnp.zeros((8, 128), f32)
        for x, at, c in (
            [(V0[f], f, edge) for f in range(12)] + [(V0[f], NEXT + f, inner) for f in range(12)]
            + [(storm[f], COL_STORM + f, edge) for f in range(12)]
            + [(masks[m], COL_MASK + m, edge) for m in range(3)]
        ):
            out = jnp.where(lane == at, turn(x, at - c, 1), out)
        return out

    snd0_col[0] = column(0, 1)
    snd0_col[1] = column(127, 126)
    if near_only:
        pl.semaphore_wait(barrier, around)
    else:
        pl.semaphore_wait(barrier, ncs - 1 + nal - 1 + beside_al * beside_cs)
    for load in loads[5:]:
        load.wait()
    each(diag_dst, lambda e: diag_of(e).start())
    each(has_dst, lambda d: copy0_of(d).start())

    w1 = w1_ref[...]
    w1t = jnp.transpose(jnp.concatenate([w1, jnp.zeros((96, 128), f32)], axis=0))[:, :32]
    w2 = w2_ref[...]
    w1_cat = beside(*split(w1))
    w2_cat = beside(*split(0.5 * w2))
    b1_cols = bias_columns(0.5 * jnp.transpose(jnp.broadcast_to(b1_ref[...], (128, 128))))
    b2_cols = bias_columns(0.5 * jnp.transpose(jnp.broadcast_to(b2_ref[...], (128, 128))))
    w1t_cat = beside(*split(0.5 * w1t), b1_cols)
    w2t_cat = beside(*split(0.5 * jnp.transpose(w2)), b2_cols)
    wo_t = jnp.transpose(jnp.concatenate([wo_ref[...], jnp.zeros((120, 128), f32)], axis=0))[:, :8]

    def choose(unit, ids):
        onehot = (row == ids).astype(f32)
        wsel_ref[:, unit * 128:(unit + 1) * 128] = lax.dot_general(
            wo_t, onehot, (((1,), (0,)), ((), ())),
            precision=lax.Precision.HIGHEST, preferred_element_type=f32,
        )

    def bias_of(ids):
        b = jnp.zeros((8, 128), f32)
        for k in range(8):
            b = jnp.where(ids == k, bo_ref[0:1, k:k + 1], b)
        return b

    for u in range(OWN):
        choose(u, cid[ROW_OF_UNIT[u]:ROW_OF_UNIT[u] + 1, :])
    bsel = bias_of(cid)

    inner_units = list(range(INNER))
    edge_units = [INNER, INNER + 1, STRIP]

    def pairs(units):
        step = 3 if len(units) == 3 else 2
        return [units[i:i + step] for i in range(0, len(units), step)]

    def first_layer(t, unit, feats, kept):
        n = len(feats)
        at = pl.ds(unit * 128, n * 128)
        ones = jnp.ones((16, n * 128), bf16)
        F = jnp.concatenate(feats, axis=1) if n > 1 else feats[0]
        Fh, Fl = split(F)
        a, h = silu(mm(w1t_cat, jnp.concatenate([Fh, Fl, ones, Fh], axis=0)))
        Hh, Hl = split(h)
        if kept:
            f_ref[t, 0:32, at] = Fh
            f_ref[t, 32:64, at] = Fl
            act1_ref[t, :, at] = slope(a, h)
            h1_ref[t, 0:128, at] = Hh
            h1_ref[t, 128:256, at] = Hl
        return jnp.concatenate([Hh, Hl, ones, Hh], axis=0)

    def second_layer(t, unit, feats, kept, H):
        n = len(feats)
        at = pl.ds(unit * 128, n * 128)
        a, h = silu(mm(w2t_cat, H))
        wsel = wsel_ref[:, at]
        if kept:
            q2_ref[t, :, at] = wsel * slope(a, h)
            h2f_ref[t, :, at] = h
        z = jnp.sum(wsel * h, axis=0, keepdims=True)
        return [z[:, i * 128:(i + 1) * 128] for i in range(n)]

    def staggered(tasks, first, second):
        out, held = [], []
        for task in tasks:
            held.append((task, first(*task)))
            if len(held) > DEPTH:
                done, x = held.pop(0)
                out.append(second(*done, x))
        for done, x in held:
            out.append(second(*done, x))
        return out

    def layers(*tasks):
        return staggered(tasks, first_layer, second_layer)

    def settle(t, units):
        for part in pairs(units):
            at = pl.ds(part[0] * 128, len(part) * 128)
            Hh, Hl = split(h2f_ref[t, :, at])
            h2_ref[t, 0:128, at] = Hh
            h2_ref[t, 128:256, at] = Hl

    def put_features(V, near):
        for f in range(4):
            for part, x in enumerate((V[f],) + tuple(near[f])):
                feat_ref[(4 * part + f) * 8:(4 * part + f + 1) * 8, :] = x

    def feats_of(*rows):
        return [feat_ref[pl.ds(r, 32, stride=8), :] for r in rows]

    def own_layers(t, first, last):
        rows = [ROW_OF_UNIT[u:u + 2] for u in range(first, last, 2)]
        tasks = [(t, u, feats_of(*r), True) for u, r in zip(range(first, last, 2), rows)]
        for pair, out in zip(rows, layers(*tasks)):
            for r, z in zip(pair, out):
                z_ref[r:r + 1, :] = z

    in0_col[0] = column(1, 2)
    in0_col[1] = column(126, 125)
    dfeat_ref[...] = jnp.zeros_like(dfeat_ref)
    feat_ref[160:256, :] = storm_ref[...]
    put_features(V0, [
        (turn(V0[f], 1, 0), turn(V0[f], 7, 0), turn(V0[f], 1, 1), turn(V0[f], 127, 1)) for f in range(4)
    ])
    own_layers(0, 0, INNER)
    settle(0, inner_units)
    for ref, rows in ((f_ref, 64), (h1_ref, 256)):
        ref[:, rows:rows + 16, :] = jnp.ones((2, 16, ref.shape[2]), bf16)
    for ref in (zx_ref, cidx_ref, wetx_ref, dunex_ref):
        ref[...] = jnp.zeros_like(ref)
    spare = acc_ref.shape[0] - ROWS
    if spare:
        acc_ref[ROWS:, :] = jnp.zeros((spare, 128), f32)

    each(has_src, lambda d: copy0_of(d).wait_recv())
    each(diag_src, lambda e: diag_of(e).wait_recv())
    relay(0)

    halo0 = Halo(rcv0_row, rcv0_col)
    near0 = [halo0.around(V0[f], f) for f in range(12)]
    put_features(V0, near0)
    sides = jnp.concatenate(
        [
            rcv0_col[1], rcv0_col[0], snd0_col[0], snd0_col[1], in0_col[0], in0_col[1],
            jnp.zeros((80, 128), f32),
        ], axis=0
    )
    T = jnp.transpose(sides)
    SE, SW, NE, NW = [rcv_diag[e] for e in range(4)]
    RS, RN = rcv0_row[0, 0:16, :], rcv0_row[1, 0:16, :]
    group = lane16 // 8
    V, far = T[0:16], T[NEXT:NEXT + 16]
    plus, minus = turn(V, 16, 1), turn(V, -16, 1)
    N, S = turn(V, 1, 1), turn(V, -1, 1)
    for at, x, c in ((0, NW, 127), (8, NE, 0), (16, RN, 0), (24, RN, 127), (32, RN, 1), (40, RN, 126)):
        N = jnp.where(lane16 == at, turn(x, at - c, 1), N)
    for at, x, c in ((7, SW, 127), (15, SE, 0), (23, RS, 0), (31, RS, 127), (39, RS, 1), (47, RS, 126)):
        S = jnp.where(lane16 == at, turn(x, at - c, 1), S)
    W = jnp.where(group == 1, minus, jnp.where(jnp.logical_or(group == 2, group == 4), plus, far))
    E = jnp.where(group == 0, minus, jnp.where(jnp.logical_or(group == 3, group == 5), plus, far))
    outer = [(V, N, S, W, E)]
    for V, N, S, west, east in (
        (RN, rcv0_row[1, NEXT:NEXT + 16, :], snd0_row[0, 0:16, :], NW, NE),
        (RS, snd0_row[1, 0:16, :], rcv0_row[0, NEXT:NEXT + 16, :], SW, SE),
    ):
        W = jnp.where(lane16 == 0, turn(west, 1, 1), turn(V, 1, 1))
        E = jnp.where(lane16 == 127, turn(east, 127, 1), turn(V, 127, 1))
        outer.append((V, N, S, W, E))
    storms = [T[COL_STORM:COL_STORM + 12], rcv0_row[1, STORM:STORM + 12, :], rcv0_row[0, STORM:STORM + 12, :]]
    mask_rows = [
        [T[COL_MASK + m:COL_MASK + m + 1] for m in range(3)],
        [rcv0_row[1, 12 + m:13 + m, :] for m in range(3)],
        [rcv0_row[0, 12 + m:13 + m, :] for m in range(3)],
    ]
    for w in range(3):
        for part in range(5):
            fx_ref[w, 4 * part:4 * part + 4, :] = outer[w][part][0:4]
        fx_ref[w, 20:32, :] = storms[w]
        wetx_ref[w:w + 1, :] = mask_rows[w][0]
        dunex_ref[w:w + 1, :] = mask_rows[w][1]
        ids = mask_rows[w][2].astype(jnp.int32)
        cidx_ref[w:w + 1, :] = ids
        choose(STRIP + w, ids)
    cidx = cidx_ref[...]
    (z_top, z_low), (z_strip,), (z_north, z_south) = layers(
        (0, INNER, feats_of(0, 7), True), (0, STRIP, [fx_ref[0]], True),
        (0, STRIP + 1, [fx_ref[1], fx_ref[2]], False),
    )
    z_ref[0:1, :] = z_top
    z_ref[7:8, :] = z_low
    zx_ref[0:1, :] = z_strip
    zx_ref[1:2, :] = z_north
    zx_ref[2:3, :] = z_south
    biasx = bias_of(cidx)
    zx = zx_ref[...] + biasx
    pickx = pickup_gain * softplus(zx) * (1.0 - dunex_ref[...])

    def from_strip(x, start):
        return jnp.sum(jnp.where(lane == start + row, x, 0.0), axis=1, keepdims=True)

    inside = jnp.logical_and(row > 0, row < 7)
    at_west = jnp.logical_and(inside, lane == 0)
    at_east = jnp.logical_and(inside, lane == 127)

    def with_strip(z, strip):
        z = jnp.where(at_west, from_strip(strip, 16), z)
        return jnp.where(at_east, from_strip(strip, 24), z)

    def to_strip(x):
        out = jnp.where(lane == 16 + row, x[:, 0:1], jnp.where(lane == 24 + row, x[:, 127:128], 0.0))
        return jnp.sum(jnp.where(inside, out, 0.0), axis=0, keepdims=True)

    z0 = with_strip(z_ref[...] + bsel, zx[0:1, :])

    def advanced(w):
        V, N, S, W, E = outer[w]
        pick, wet = pickx[w:w + 1, :], wetx_ref[w:w + 1, :]
        lap = N + S + W + E - 4.0 * V
        ad, cd = S - N, E - W
        spread = jnp.where(field == 3, bed_diffusion, diffusion) * lap
        sediment = spread - advection * (V[1:2] * ad + V[2:3] * cd) - settling * V
        sediment = sediment + jnp.where(field - 4 == cidx[w:w + 1, :], pick, 0.0)
        total = jnp.sum(
            jnp.where(jnp.logical_and(field >= 4, field < 12), V, 0.0), axis=0, keepdims=True
        )
        first = jnp.where(field == 0, -advection * (ad[1:2] + cd[2:3]), settling * total - pick)
        first = jnp.where(field == 1, -advection * ad[0:1] - friction * V[1:2], first)
        first = jnp.where(field == 2, -advection * cd[0:1] - friction * V[2:3], first)
        return V + wet * jnp.where(field < 4, spread + first, sediment)

    strip1, RN, RS = advanced(0), advanced(1), advanced(2)
    ring_row[1] = RN
    ring_row[0] = RS
    back = jnp.transpose(jnp.concatenate([strip1, jnp.zeros((112, 128), f32)], axis=0))
    ring_col[1] = back[0:8]
    ring_col[0] = back[8:16]

    pickup = softplus(z0) * wash[0]
    lap = []
    for f in range(12):
        n, s, w, e = near0[f]
        lap.append(n + s + w + e - 4.0 * V0[f])
    total = V0[4]
    for k in range(1, 8):
        total = total + V0[4 + k]
    ad = [near0[f][1] - near0[f][0] for f in range(12)]
    cd = [near0[f][3] - near0[f][2] for f in range(12)]
    tend = [
        diffusion * lap[0] - advection * (ad[1] + cd[2]),
        diffusion * lap[1] - advection * ad[0] - friction * V0[1],
        diffusion * lap[2] - advection * cd[0] - friction * V0[2],
        bed_diffusion * lap[3] - pickup_gain * pickup + settling * total,
    ]
    for k in range(8):
        x = diffusion * lap[4 + k] - advection * (V0[1] * ad[4 + k] + V0[2] * cd[4 + k])
        x = x + jnp.where(cid == k, pickup_gain * pickup, 0.0) - settling * V0[4 + k]
        tend.append(x)
    V1 = [V0[f] + wets[0] * tend[f] for f in range(12)]

    halo1 = Halo(ring_row, ring_col)
    near1 = [halo1.around(V1[f], f) for f in range(12)]
    put_features(V1, near1)
    plus, minus = turn(strip1, 16, 1), turn(strip1, -16, 1)
    N, S = turn(strip1, 1, 1), turn(strip1, -1, 1)
    for at, c in ((16, 0), (24, 127)):
        N = jnp.where(lane16 == at, turn(RN, at - c, 1), N)
        S = jnp.where(lane16 == at + 7, turn(RS, at + 7 - c, 1), S)
    W, E = jnp.where(group == 2, plus, minus), jnp.where(group == 2, minus, plus)
    for part, x in enumerate((strip1, N, S, W, E)):
        fx_ref[0, 4 * part:4 * part + 4, :] = x[0:4]
    (z_top, z_low), (z_strip,) = layers(
        (1, INNER, feats_of(0, 7), True), (1, STRIP, [fx_ref[0]], True)
    )
    z_ref[0:1, :] = z_top
    z_ref[7:8, :] = z_low
    z_strip = z_strip + biasx[0:1, :]
    relayed(0)
    relay(1)
    z1 = with_strip(z_ref[...] + bsel, z_strip)
    lam2 = [cot_ref[f * 8:(f + 1) * 8, :] for f in range(12)]

    def closure_cotangent(t, gate, lam):
        G = [None] * 3 + [wets[t] * lam[f] for f in range(3, 12)]
        picked = G[4]
        for k in range(1, 8):
            picked = jnp.where(cid == k, G[4 + k], picked)
        return pickup_gain * (picked - G[3]) * wash[t] * gate

    def sigmoid(z):
        return 1.0 / (1.0 + jnp.exp(-z))

    def adjoint_two(t, units, drows):
        for part in pairs(list(zip(units, drows))):
            at = pl.ds(part[0][0] * 128, len(part) * 128)
            drow = 0.5 * jnp.concatenate([d for _, d in part], axis=1)
            Dh, Dl = split(q2_ref[t, :, at] * drow)
            d2_ref[t, 0:128, at] = Dh
            d2_ref[t, 128:256, at] = Dl

    def adjoint_one(t, units):
        def product(part):
            at = pl.ds(part[0] * 128, len(part) * 128)
            return mm(w2_cat, jnp.concatenate([d2_ref[t, :, at], d2_ref[t, 0:128, at]], axis=0))

        def rest(part, d1):
            at = pl.ds(part[0] * 128, len(part) * 128)
            Dh, Dl = split(d1 * act1_ref[t, :, at])
            d1_ref[t, 0:128, at] = Dh
            d1_ref[t, 128:256, at] = Dl

        staggered([(part,) for part in pairs(units)], product, rest)

    def feature_cotangent(t, units):
        out = []

        def product(part):
            at = pl.ds(part[0] * 128, len(part) * 128)
            return mm(w1_cat, jnp.concatenate([d1_ref[t, :, at], d1_ref[t, 0:128, at]], axis=0))

        def rest(part, dF):
            for i, u in enumerate(part):
                one = dF[:, i * 128:(i + 1) * 128]
                if u < OWN:
                    dfeat_ref[pl.ds(ROW_OF_UNIT[u], 32, stride=8), :] = one
                else:
                    out.append(one)

        staggered([(part,) for part in pairs(units)], product, rest)
        return out

    def adjoint_cells(D, G, near, V, lam):
        lap = [bed_diffusion if f == 3 else diffusion for f in range(12)]
        lg = [lap[f] * G[f] for f in range(12)]
        c = [lam[f] - 4.0 * lg[f] for f in range(12)]
        alongs = jnp.zeros((8, 128), f32)
        crosses = jnp.zeros((8, 128), f32)
        along_part = [advection * G[1], advection * G[0], None, None]
        cross_part = [advection * G[2], None, advection * G[0], None]
        for k in range(8):
            n, s, w, e = near[4 + k]
            alongs = alongs + (s - n) * G[4 + k]
            crosses = crosses + (e - w) * G[4 + k]
            c[4 + k] = c[4 + k] + settling * (G[3] - G[4 + k])
            ag = advection * G[4 + k]
            along_part.append(V[1] * ag)
            cross_part.append(V[2] * ag)
        c[1] = c[1] - friction * G[1] - advection * alongs
        c[2] = c[2] - friction * G[2] - advection * crosses
        to = [[], [], [], []]
        for f in range(12):
            for d, part, sign in ((0, along_part, 1), (1, along_part, -1), (2, cross_part, 1), (3, cross_part, -1)):
                x = lg[f]
                if part[f] is not None:
                    x = x + part[f] if sign > 0 else x - part[f]
                if f < 4:
                    x = x + D[4 + 4 * d + f]
                to[d].append(x)
            if f < 4:
                c[f] = c[f] + D[f]
        return c, to

    def gather(c, to, halo):
        return [
            c[f] + halo.south(to[0][f], f) + halo.north(to[1][f], f)
            + halo.east(to[2][f], f) + halo.west(to[3][f], f)
            for f in range(12)
        ]

    def keep(start, part, first):
        at = pl.ds(start, part.shape[0])
        acc_ref[at, :] = part if first else acc_ref[at, :] + part

    def weights_two(t, units, ids, drows, first):
        at = pl.ds(units[0] * 128, len(units) * 128)
        width = len(units) * 128
        dr = jnp.concatenate(
            [jnp.where(row == k, d, 0.0) for k, d in zip(ids, drows)], axis=1
        )
        dbo = jnp.sum(
            jnp.where(row == lane, jnp.sum(dr, axis=1, keepdims=True), 0.0), axis=0, keepdims=True
        )
        drh, drl = split(jnp.concatenate([dr, jnp.zeros((8, width), f32)], axis=0))
        top = mm_nt(jnp.concatenate([drh, drl], axis=0), h2_ref[t, :, at])
        dwo = top[:8, :128] + top[16:24, :128] + top[:8, 128:]
        top = mm_nt(h1_ref[t, :, at], d2_ref[t, :, at])
        keep(0, top[:128, :128] + top[128:256, :128] + top[:128, 128:], first)
        keep(ROW_WO, dwo, first)
        ones = top[256:264, :128] + top[256:264, 128:]
        keep(ROW_BIAS, jnp.where(row == 1, ones, jnp.where(row == 2, dbo, 0.0)), first)

    def weights_one(t, units, first):
        at = pl.ds(units[0] * 128, len(units) * 128)
        top = mm_nt(f_ref[t, :, at], d1_ref[t, :, at])
        keep(ROW_W1, top[:32, :128] + top[32:64, :128] + top[:32, 128:], first)
        ones = top[64:72, :128] + top[64:72, 128:]
        keep(ROW_BIAS, jnp.where(row == 0, ones, 0.0), False)

    def rows_of(x, units):
        return [x[ROW_OF_UNIT[u]:ROW_OF_UNIT[u] + 1, :] for u in units]

    G1 = [wets[1] * lam2[f] for f in range(12)]
    columns = jnp.logical_and(lane > 0, lane < 127)

    def patched(strip_back):
        turned = jnp.transpose(jnp.concatenate([strip_back, jnp.zeros((96, 128), f32)], axis=0))
        at_w, at_e = turned[16:24], turned[24:32]
        out = []
        for f in range(20):
            x = dfeat_ref[f * 8:(f + 1) * 8, :]
            x = jnp.where(at_west, turn(at_w, -f, 1), x)
            out.append(jnp.where(at_east, turn(at_e, 127 - f, 1), x))
        return out

    dz1 = closure_cotangent(1, sigmoid(z1), lam2)
    edge_rows1 = [dz1[0:1, :], dz1[7:8, :], to_strip(dz1)]
    adjoint_two(1, edge_units, edge_rows1)
    adjoint_one(1, edge_units)
    strip_back = feature_cotangent(1, edge_units)[0]
    _, to1 = adjoint_cells(patched(strip_back), G1, near1, V1, lam2)
    fill(1, *to1)
    each(has_dst, lambda d: copy0_of(d).wait_send())
    each(has_dst, lambda d: copy_of(1, d).start())

    own_layers(1, 0, INNER)
    dz1 = closure_cotangent(1, sigmoid(z_ref[...] + bsel), lam2)
    dz_ref[...] = jnp.where(columns, dz1, 0.0)
    drows1 = rows_of(dz_ref, inner_units)
    adjoint_two(1, inner_units, drows1)
    adjoint_one(1, inner_units)
    feature_cotangent(1, inner_units)
    c1, to1 = adjoint_cells(patched(strip_back), G1, near1, V1, lam2)
    gate0 = sigmoid(z0)
    settle(1, inner_units + edge_units)
    settle(0, edge_units)
    ids_edge = [cid[0:1, :], cid[7:8, :], cidx_ref[0:1, :]]
    weights_two(
        1, inner_units + edge_units, rows_of(cid, inner_units) + ids_edge, drows1 + edge_rows1, True
    )
    weights_one(1, inner_units + edge_units, True)
    lam1 = [
        c1[f] + turn(to1[0][f], 7, 0) + turn(to1[1][f], 1, 0) + turn(to1[2][f], 127, 1) + turn(to1[3][f], 1, 1)
        for f in range(12)
    ]
    dz0 = closure_cotangent(0, gate0, lam1)
    dz_ref[...] = jnp.where(columns, dz0, 0.0)
    drows0 = rows_of(dz_ref, inner_units)
    adjoint_two(0, inner_units, drows0)
    weights_two(0, inner_units, rows_of(cid, inner_units), drows0, False)
    adjoint_one(0, inner_units)
    weights_one(0, inner_units, False)
    feature_cotangent(0, inner_units)

    each(has_src, lambda d: copy_of(1, d).wait_recv())
    relayed(1)
    lam1 = gather(c1, to1, Halo(rcv_row.at[0], rcv_col.at[0]))
    dz0 = closure_cotangent(0, gate0, lam1)
    drows0 = [dz0[0:1, :], dz0[7:8, :], to_strip(dz0)]
    adjoint_two(0, edge_units, drows0)
    weights_two(0, edge_units, ids_edge, drows0, False)
    adjoint_one(0, edge_units)
    weights_one(0, edge_units, False)

    size = src_b.shape[0]
    last_core = nsu - 1
    owner = su == last_core
    mine = pl.ds(pl.multiple_of(cs * size, 8), size)
    spans = [(dz, dx) for dz in range(nal) for dx in range(ncr)]
    pieces = (rcv_a, rcv_e)
    low_rows = 2 * ncr * rcv_e.shape[1]

    sense = 1 - 2 * ((2 * al) // nal)

    def chip_at(span):
        return lax.rem(al + nal + sense * span[0], nal), lax.rem(cr + span[1], ncr)

    after = max(ncs, nal) - 1

    def is_end(a):
        return jnp.logical_or(a == 0, a == nal - 1)

    def piece_of(a, c, end):
        n = pieces[end].shape[1]
        start = ((a // (nal - 1)) * ncr + c) * n if end else low_rows + ((a - 1) * ncr + c) * n
        return pl.ds(pl.multiple_of(start, 8), n)

    def to_owner(k, end):
        a, c = chip_at(spans[k])
        source = lax.rem(al - a + nal, nal) * ncr + lax.rem(cr - c + ncr, ncr)
        slot = 2 * (source - 1) + su if k else 2 * (len(spans) - 1)
        return pltpu.make_async_remote_copy(
            src_ref=acc_ref.at[piece_of(a, c, end), :], dst_ref=pieces[end].at[slot],
            send_sem=load_sem.at[8], recv_sem=load_sem.at[10],
            device_id=(g, a, c, last_core), device_id_type=MESH,
        )

    def from_owner(k, core, end):
        a, c = chip_at(spans[k])
        own = full_ref.at[piece_of(al, cr, end), :]
        return pltpu.make_async_remote_copy(
            src_ref=own, dst_ref=own, send_sem=load_sem.at[9], recv_sem=load_sem.at[11],
            device_id=(g, a, c, core), device_id_type=MESH,
        )

    def share(k):
        ends = is_end(chip_at(spans[k])[0])

        @pl.when(ends)
        def _():
            to_owner(k, 1).start()

        @pl.when(jnp.logical_not(ends))
        def _():
            to_owner(k, 0).start()

    def each_owner(action):
        ends = is_end(al)

        @pl.when(jnp.logical_and(owner, ends))
        def _():
            action(1)

        @pl.when(jnp.logical_and(owner, jnp.logical_not(ends)))
        def _():
            action(0)

    def spread(end):
        ref = pieces[end]
        own = piece_of(al, cr, end)
        all_of(ref, load_sem.at[10]).wait_recv()
        total = acc_ref[own, :]
        for j in range(ref.shape[0]):
            total = total + ref[j]
        full_ref[own, :] = total * factor
        for k in range(others, -1, -1):
            for core in range(nsu):
                if k or core != last_core:
                    from_owner(k, core, end).start()

    def close(end):
        ref = pieces[end]
        rest = pl.ds(0, acc_ref.shape[0] - ref.shape[1])
        all_of(acc_ref.at[rest, :], load_sem.at[8]).wait_send()
        all_of(full_ref.at[rest, :], load_sem.at[11]).wait_recv()
        all_of(ref, load_sem.at[9]).wait_send()

    def all_of(ref, sem):
        return pltpu.make_async_remote_copy(
            src_ref=ref, dst_ref=ref, send_sem=sem, recv_sem=sem,
            device_id=(g, al, cr, nsu - 1 - su), device_id_type=MESH,
        )

    def copy_a(j):
        peer = lax.rem(cs + j, ncs)
        return pltpu.make_async_remote_copy(
            src_ref=acc_ref.at[pl.ds(pl.multiple_of(peer * size, 8), size), :],
            dst_ref=rcv_a.at[j - 1], send_sem=sum_sem.at[j - 1], recv_sem=sum_sem.at[after + j - 1],
            device_id=dev(al, peer), device_id_type=MESH,
        )

    def copy_b(j):
        return pltpu.make_async_remote_copy(
            src_ref=src_b, dst_ref=rcv_b.at[al], send_sem=sum_sem.at[j - 1],
            recv_sem=sum_sem.at[after + 2 * ncs + j - 3],
            device_id=dev(lax.rem(al + j, nal), cs), device_id_type=MESH,
        )

    def copy_c(j):
        return pltpu.make_async_remote_copy(
            src_ref=full_ref.at[mine, :], dst_ref=full_ref.at[mine, :],
            send_sem=sum_sem.at[j - 1], recv_sem=sum_sem.at[after + ncs + j - 2],
            device_id=dev(al, lax.rem(cs + j, ncs)), device_id_type=MESH,
        )

    others = len(spans) - 1
    if direct:
        for k in range(others, 0, -1):
            share(k)

        @pl.when(jnp.logical_not(owner))
        def _():
            share(0)
    else:
        for j in range(1, ncs):
            copy_a(j).start()

    D0 = patched(feature_cotangent(0, edge_units)[0])
    G0 = [wets[0] * lam1[f] for f in range(12)]
    c0, to0 = adjoint_cells(D0, G0, near0, V0, lam1)
    fill(2, *to0)
    each(has_dst, lambda d: copy_of(1, d).wait_send())
    each(has_dst, lambda d: copy_of(2, d).start())

    if direct:
        each_owner(spread)
    else:
        total = acc_ref[mine, :]
        for j in range(1, ncs):
            copy_a(j).wait_recv()
            total = total + rcv_a[j - 1]
        src_b[...] = total
        rcv_b[al] = total
        for j in range(1, ncs):
            copy_a(j).wait_send()
        for j in range(1, nal):
            copy_b(j).start()
    each(has_src, lambda d: copy_of(2, d).wait_recv())
    last = gather(c0, to0, Halo(rcv_row.at[1], rcv_col.at[1]))
    for f in range(12):
        gstate_ref[f] = last[f]
    each(has_dst, lambda d: copy_of(2, d).wait_send())
    each(diag_dst, lambda e: diag_of(e).wait_send())
    if direct:
        each_owner(close)

        @pl.when(jnp.logical_not(owner))
        def _():
            all_of(acc_ref, load_sem.at[8]).wait_send()
            all_of(full_ref, load_sem.at[11]).wait_recv()
    else:
        for j in range(1, nal):
            copy_b(j).wait_recv()
        total = rcv_b[0]
        for j in range(1, nal):
            total = total + rcv_b[j]
        full_ref[mine, :] = total * factor
        for j in range(1, nal):
            copy_b(j).wait_send()
        for j in range(1, ncs):
            copy_c(j).start()
        for j in range(1, ncs):
            copy_c(j).wait_recv()
        for j in range(1, ncs):
            copy_c(j).wait_send()


def unpack(
    state_ref, full_ref,
    gs_hbm, gw1_hbm, gb1_hbm, gw2_hbm, gb2_hbm, gwo_hbm, gbo_hbm, gbo_ref, sem,
):
    gbo_ref[...] = full_ref[ROW_BIAS + 2:ROW_BIAS + 3, 0:8]
    parts = (
        (full_ref.at[0:128], gw2_hbm), (state_ref, gs_hbm), (full_ref.at[ROW_W1:ROW_W1 + 32], gw1_hbm),
        (full_ref.at[ROW_WO:ROW_WO + 8], gwo_hbm), (full_ref.at[ROW_BIAS:ROW_BIAS + 1], gb1_hbm),
        (full_ref.at[ROW_BIAS + 1:ROW_BIAS + 2], gb2_hbm), (gbo_ref, gbo_hbm),
    )
    copies = [pltpu.make_async_copy(src, dst, sem.at[i]) for i, (src, dst) in enumerate(parts)]
    for copy in copies:
        copy.start()
    for copy in copies:
        copy.wait()


def solution(mesh):
    nal, ncr, nsu = mesh.shape["along"], mesh.shape["cross"], mesh.shape["sub"]
    ncs = ncr * nsu
    near_only = nal <= 4 and ncs <= 4
    direct = near_only and nsu == 2 and nal == 4
    size = 8 * (-(-ROWS // (8 * ncs)))
    at_end = 8
    left = ROWS - 2 * ncr * at_end
    middle = 8 * (-(-left // (8 * 2 * ncr)))
    rows_sum = 2 * ncr * (at_end + middle) if direct else ncs * size
    sources = 2 * nal * ncr - 1

    def per_device(state, storm, wet, dune, cid, w1, b1, w2, b2, wo, bo, cot):
        rows, cols = state.shape[1], state.shape[2]
        factor = 1.0 / math.sqrt(rows * nal * cols * ncs)
        vmem = pl.BlockSpec(memory_space=pltpu.VMEM)
        hbm = pl.BlockSpec(memory_space=pl.ANY)
        flat = lambda x: x.reshape(-1, 128)
        operands = (
            flat(state), cid, w1, b1.reshape(1, 128), w2, b2.reshape(1, 128), wo.T, bo.reshape(1, 8),
            flat(storm), flat(wet), flat(dune), flat(cot),
        )
        dma = pltpu.SemaphoreType.DMA
        tile = pltpu.VMEM((8, 128), f32)
        big = lambda n, kind: pltpu.VMEM((2, n, (OWN + 1) * 128), kind)
        out = pl.pallas_call(
            functools.partial(kernel, nal, ncr, nsu, near_only, direct, factor),
            out_shape=(pltpu.VMEM((12, 8, 128), f32), pltpu.VMEM((rows_sum, 128), f32)),
            in_specs=[hbm] * 12,
            out_specs=(vmem,) * 2,
            scratch_shapes=[
                *[pltpu.VMEM(x.shape, x.dtype) for x in operands],
                dma((12,)),
                pltpu.VMEM((2, 40, 128), f32),
                pltpu.VMEM((2, 8, 128), f32),
                pltpu.VMEM((2, 8, 128), f32),
                pltpu.VMEM((2, 40, 128), f32),
                pltpu.VMEM((2, 8, 128), f32),
                pltpu.VMEM((4, 16, 128), f32),
                pltpu.VMEM((2, 2, 16, 128), f32),
                pltpu.VMEM((2, 2, 8, 128), f32),
                pltpu.VMEM((2, 2, 16, 128), f32),
                pltpu.VMEM((2, 2, 8, 128), f32),
                pltpu.VMEM((2, 16, 128), f32),
                pltpu.VMEM((2, 8, 128), f32),
                dma((2, 4)), dma((4,)), pltpu.SemaphoreType.REGULAR((2,)),
                pltpu.VMEM((256, 128), f32),
                pltpu.VMEM((256, 128), f32),
                pltpu.VMEM((3, 32, 128), f32),
                tile, tile, tile, pltpu.VMEM((8, 128), jnp.int32), tile, tile,
                pltpu.VMEM((128, (OWN + 3) * 128), f32), big(128, f32),
                big(80, bf16), big(272, bf16), big(256, bf16), big(128, f32), big(128, f32),
                big(256, bf16), big(256, bf16),
                pltpu.VMEM((rows_sum, 128), f32),
                pltpu.VMEM((sources, middle, 128) if direct else (ncs - 1, size, 128), f32),
                pltpu.VMEM((sources if direct else 1, at_end, 128), f32),
                pltpu.VMEM((size, 128), f32),
                pltpu.VMEM((1 if direct else nal, size, 128), f32),
                dma((1 if direct else max(ncs, nal) + 2 * ncs + nal - 4,)),
            ],
            compiler_params=pltpu.CompilerParams(collective_id=0, has_side_effects=True),
        )(*operands)
        gs, gw1, gb1, gw2, gb2, gwo, gbo = pl.pallas_call(
            unpack,
            out_shape=(
                jax.ShapeDtypeStruct((12, 8, 128), f32),
                jax.ShapeDtypeStruct((32, 128), f32),
                jax.ShapeDtypeStruct((1, 128), f32),
                jax.ShapeDtypeStruct((128, 128), f32),
                jax.ShapeDtypeStruct((1, 128), f32),
                jax.ShapeDtypeStruct((8, 128), f32),
                jax.ShapeDtypeStruct((1, 8), f32),
            ),
            in_specs=[vmem] * 2,
            out_specs=(hbm,) * 7,
            scratch_shapes=[pltpu.VMEM((1, 8), f32), dma((7,))],
        )(*[pltpu.with_memory_space_constraint(x, pltpu.VMEM) for x in out])
        return gs, gw1, gb1.reshape(128), gw2, gb2.reshape(128), gwo.T, gbo.reshape(8)

    tile = P(None, ("groups", "along"), ("cross", "sub"))
    return jax.shard_map(
        per_device,
        mesh=mesh,
        in_specs=(
            tile, tile, tile, tile, P(("groups", "along"), ("cross", "sub")),
            P(), P(), P(), P(), P(), P(), tile,
        ),
        out_specs=(
            tile, P("groups", None), P("groups"), P("groups", None), P("groups"),
            P("groups", None), P("groups"),
        ),
        check_vma=False,
    )
```

```python
import functools
import math

import jax
import jax.numpy as jnp
from jax import lax
from jax.experimental import pallas as pl
from jax.experimental.pallas import tpu as pltpu
from jax.sharding import PartitionSpec as P

MESH = pl.DeviceIdType.MESH
f32 = jnp.float32
bf16 = jnp.bfloat16
diffusion = 0.15
advection = 0.2
friction = 0.05
pickup_gain = 0.5
settling = 0.2
bed_diffusion = 0.1

ROW_W1 = 128
ROW_WO = 160
ROW_BIAS = 168
ROWS = 176
ROW_OF_UNIT = (1, 2, 3, 4, 5, 6, 0, 7)
INNER = 6
DEPTH = 2
OWN = 8
STRIP = 8
NEXT = 16
STORM = 28
COL_STORM = 32
COL_MASK = 44


def split(x):
    high = x.astype(bf16)
    low = (x - high.astype(f32)).astype(bf16)
    return high, low


def mm(a, b):
    return lax.dot_general(a, b, (((1,), (0,)), ((), ())), preferred_element_type=f32)


def mm_nt(a, b):
    return lax.dot_general(a, b, (((1,), (1,)), ((), ())), preferred_element_type=f32)


def beside(high, low, *extra):
    return jnp.concatenate([high, high, *extra, low], axis=1)


def bias_columns(spread):
    high = spread.astype(bf16)
    rest = spread - high.astype(f32)
    middle = rest.astype(bf16)
    low = (rest - middle.astype(f32)).astype(bf16)
    lane = lax.broadcasted_iota(jnp.int32, spread.shape, 1)
    out = jnp.zeros_like(spread)
    for i, part in enumerate((high, middle, low)):
        out = jnp.where(lane == i, part.astype(f32), out)
    return out[:, :16].astype(bf16)


def silu(u):
    a = 1.0 + jnp.tanh(u)
    return a, u * a


def slope(a, h):
    return h * (2.0 - a) + a


def softplus(z):
    return jnp.maximum(z, 0.0) + jnp.log(1.0 + jnp.exp(-jnp.abs(z)))


def kernel(
    nal, ncr, nsu, near_only, direct, factor,
    state_hbm, cid_hbm, w1_hbm, b1_hbm, w2_hbm, b2_hbm, wo_hbm, bo_hbm,
    storm_hbm, wet_hbm, dune_hbm, cot_hbm,
    gstate_ref, full_ref,
    state_ref, cid_ref, w1_ref, b1_ref, w2_ref, b2_ref, wo_ref, bo_ref,
    storm_ref, wet_ref, dune_ref, cot_ref, load_sem,
    snd0_row, snd0_col, in0_col, rcv0_row, rcv0_col, rcv_diag,
    snd_row, snd_col, rcv_row, rcv_col, ring_row, ring_col,
    edge_recv, diag_recv, relay_sem,
    feat_ref, dfeat_ref, fx_ref, z_ref, zx_ref, dz_ref, cidx_ref, wetx_ref, dunex_ref,
    wsel_ref, h2f_ref,
    f_ref, h1_ref, h2_ref, act1_ref, q2_ref, d1_ref, d2_ref,
    acc_ref, rcv_a, rcv_e, src_b, rcv_b,
    sum_sem,
):
    ncs = ncr * nsu
    g = lax.axis_index("groups")
    al = lax.axis_index("along")
    cr = lax.axis_index("cross")
    su = lax.axis_index("sub")
    cs = cr * nsu + su

    def dev(a, c):
        return (g, a, c // nsu, c % nsu)

    has_dst = (al > 0, al < nal - 1, cs > 0, cs < ncs - 1)
    has_src = (al < nal - 1, al > 0, cs < ncs - 1, cs > 0)
    dst_dev = (
        dev(al - 1, cs), dev(al + 1, cs), dev(al, cs - 1), dev(al, cs + 1),
    )
    corners = ((0, 2), (0, 3), (1, 2), (1, 3))
    diag_dst = [jnp.logical_and(has_dst[a], has_dst[c]) for a, c in corners]
    diag_src = [jnp.logical_and(has_src[a], has_src[c]) for a, c in corners]
    diag_dev = [dev(al + (1 if a else -1), cs + (1 if c == 3 else -1)) for a, c in corners]

    loads = [
        pltpu.make_async_copy(src, dst, load_sem.at[i])
        for i, (src, dst) in enumerate((
            (state_hbm, state_ref), (storm_hbm, storm_ref), (wet_hbm, wet_ref), (dune_hbm, dune_ref),
            (cid_hbm, cid_ref), (w1_hbm, w1_ref), (b1_hbm, b1_ref), (w2_hbm, w2_ref),
            (b2_hbm, b2_ref), (wo_hbm, wo_ref), (bo_hbm, bo_ref), (cot_hbm, cot_ref),
        ))
    ]
    for load in loads[:5]:
        load.start()
    for ref in (rcv0_row, rcv0_col, rcv_diag, rcv_row, rcv_col):
        ref[...] = jnp.zeros_like(ref)

    barrier = pltpu.get_barrier_semaphore()
    for e in range(4):
        @pl.when(diag_dst[e])
        def _():
            pl.semaphore_signal(barrier, inc=1, device_id=diag_dev[e], device_id_type=MESH)
    if near_only:
        for d in range(4):
            @pl.when(has_dst[d])
            def _():
                pl.semaphore_signal(barrier, inc=1, device_id=dst_dev[d], device_id_type=MESH)
    else:
        for j in range(1, ncs):
            pl.semaphore_signal(
                barrier, inc=1, device_id=dev(al, lax.rem(cs + j, ncs)), device_id_type=MESH
            )
        for j in range(1, nal):
            pl.semaphore_signal(
                barrier, inc=1, device_id=dev(lax.rem(al + j, nal), cs), device_id_type=MESH
            )
    for load in loads[5:]:
        load.start()
    beside_al = (al + nal - 1) // nal + (2 * nal - 2 - al) // nal
    beside_cs = (cs + ncs - 1) // ncs + (2 * ncs - 2 - cs) // ncs

    row = lax.broadcasted_iota(jnp.int32, (8, 128), 0)
    lane = lax.broadcasted_iota(jnp.int32, (8, 128), 1)
    field = lax.broadcasted_iota(jnp.int32, (16, 128), 0)
    lane16 = lax.broadcasted_iota(jnp.int32, (16, 128), 1)

    def turn(x, shift, axis):
        shift = shift % x.shape[axis]
        return pltpu.roll(x, shift, axis) if shift else x

    def copy0_of(d):
        src, dst = (snd0_row, rcv0_row) if d < 2 else (snd0_col, rcv0_col)
        return pltpu.make_async_remote_copy(
            src_ref=src.at[d % 2], dst_ref=dst.at[d % 2], send_sem=load_sem.at[d],
            recv_sem=edge_recv.at[0, d], device_id=dst_dev[d], device_id_type=MESH,
        )

    def diag_of(e):
        return pltpu.make_async_remote_copy(
            src_ref=snd0_row.at[e // 2, pl.ds(0, 16)], dst_ref=rcv_diag.at[e],
            send_sem=load_sem.at[4 + e], recv_sem=diag_recv.at[e],
            device_id=diag_dev[e], device_id_type=MESH,
        )

    def copy_of(k, d):
        src, dst = (snd_row, rcv_row) if d < 2 else (snd_col, rcv_col)
        return pltpu.make_async_remote_copy(
            src_ref=src.at[k - 1, d % 2], dst_ref=dst.at[k - 1, d % 2], send_sem=load_sem.at[d],
            recv_sem=edge_recv.at[k % 2, d], device_id=dst_dev[d], device_id_type=MESH,
        )

    around = beside_al + beside_cs + beside_al * beside_cs

    def relay(k):
        if near_only:
            for flags, devices in ((has_dst, dst_dev), (diag_dst, diag_dev)):
                each(flags, lambda i: pl.semaphore_signal(
                    relay_sem.at[k], inc=1, device_id=devices[i], device_id_type=MESH))

    def relayed(k):
        if near_only:
            pl.semaphore_wait(relay_sem.at[k], around)

    def each(flags, action):
        for i in range(4):
            @pl.when(flags[i])
            def _():
                action(i)

    def fill(k, xn, xs, xw, xe):
        west = jnp.zeros((8, 128), f32)
        east = jnp.zeros((8, 128), f32)
        for f in range(12):
            snd_row[k - 1, 0, f:f + 1, :] = xn[f][0:1, :]
            snd_row[k - 1, 1, f:f + 1, :] = xs[f][7:8, :]
            west = jnp.where(lane == f, turn(xw[f], f, 1), west)
            east = jnp.where(lane == f, turn(xe[f], f + 1, 1), east)
        snd_col[k - 1, 0] = west
        snd_col[k - 1, 1] = east

    class Halo:
        def __init__(self, rows, cols):
            self.rows, self.cols = rows, cols

        def south(self, x, f):
            return jnp.where(row == 7, self.rows[0, f:f + 1, :], turn(x, 7, 0))

        def north(self, x, f):
            return jnp.where(row == 0, self.rows[1, f:f + 1, :], turn(x, 1, 0))

        def east(self, x, f):
            return jnp.where(lane == 127, turn(self.cols[0], 127 - f, 1), turn(x, 127, 1))

        def west(self, x, f):
            return jnp.where(lane == 0, turn(self.cols[1], -f, 1), turn(x, 1, 1))

        def around(self, x, f):
            return self.north(x, f), self.south(x, f), self.west(x, f), self.east(x, f)

    for load in loads[:5]:
        load.wait()
    V0 = [state_ref[f * 8:(f + 1) * 8, :] for f in range(12)]
    storm = [storm_ref[f * 8:(f + 1) * 8, :] for f in range(12)]
    wets = [wet_ref[t * 8:(t + 1) * 8, :].astype(f32) for t in range(2)]
    dunes = [dune_ref[t * 8:(t + 1) * 8, :].astype(f32) for t in range(2)]
    wash = [1.0 - dunes[t] for t in range(2)]
    cid = cid_ref[...]
    masks = [wets[0], dunes[0], cid.astype(f32)]
    for d, edge, inner in ((0, 0, 1), (1, 7, 6)):
        for f in range(12):
            snd0_row[d, f:f + 1, :] = V0[f][edge:edge + 1, :]
            snd0_row[d, NEXT + f:NEXT + f + 1, :] = V0[f][inner:inner + 1, :]
            snd0_row[d, STORM + f:STORM + f + 1, :] = storm[f][edge:edge + 1, :]
        for m in range(3):
            snd0_row[d, 12 + m:13 + m, :] = masks[m][edge:edge + 1, :]
        snd0_row[d, 15:16, :] = jnp.zeros((1, 128), f32)

    def column(edge, inner):
        out = jnp.zeros((8, 128), f32)
        for x, at, c in (
            [(V0[f], f, edge) for f in range(12)] + [(V0[f], NEXT + f, inner) for f in range(12)]
            + [(storm[f], COL_STORM + f, edge) for f in range(12)]
            + [(masks[m], COL_MASK + m, edge) for m in range(3)]
        ):
            out = jnp.where(lane == at, turn(x, at - c, 1), out)
        return out

    snd0_col[0] = column(0, 1)
    snd0_col[1] = column(127, 126)
    if near_only:
        pl.semaphore_wait(barrier, around)
    else:
        pl.semaphore_wait(barrier, ncs - 1 + nal - 1 + beside_al * beside_cs)
    for load in loads[5:]:
        load.wait()
    each(diag_dst, lambda e: diag_of(e).start())
    each(has_dst, lambda d: copy0_of(d).start())

    w1 = w1_ref[...]
    w1t = jnp.transpose(jnp.concatenate([w1, jnp.zeros((96, 128), f32)], axis=0))[:, :32]
    w2 = w2_ref[...]
    w1_cat = beside(*split(w1))
    w2_cat = beside(*split(0.5 * w2))
    b1_cols = bias_columns(0.5 * jnp.transpose(jnp.broadcast_to(b1_ref[...], (128, 128))))
    b2_cols = bias_columns(0.5 * jnp.transpose(jnp.broadcast_to(b2_ref[...], (128, 128))))
    w1t_cat = beside(*split(0.5 * w1t), b1_cols)
    w2t_cat = beside(*split(0.5 * jnp.transpose(w2)), b2_cols)
    wo_t = jnp.transpose(jnp.concatenate([wo_ref[...], jnp.zeros((120, 128), f32)], axis=0))[:, :8]

    def choose(unit, ids):
        onehot = (row == ids).astype(f32)
        wsel_ref[:, unit * 128:(unit + 1) * 128] = lax.dot_general(
            wo_t, onehot, (((1,), (0,)), ((), ())),
            precision=lax.Precision.HIGHEST, preferred_element_type=f32,
        )

    def bias_of(ids):
        b = jnp.zeros((8, 128), f32)
        for k in range(8):
            b = jnp.where(ids == k, bo_ref[0:1, k:k + 1], b)
        return b

    for u in range(OWN):
        choose(u, cid[ROW_OF_UNIT[u]:ROW_OF_UNIT[u] + 1, :])
    bsel = bias_of(cid)

    inner_units = list(range(INNER))
    edge_units = [INNER, INNER + 1, STRIP]

    def pairs(units):
        step = 3 if len(units) == 3 else 2
        return [units[i:i + step] for i in range(0, len(units), step)]

    def first_layer(t, unit, feats, kept):
        n = len(feats)
        at = pl.ds(unit * 128, n * 128)
        ones = jnp.ones((16, n * 128), bf16)
        F = jnp.concatenate(feats, axis=1) if n > 1 else feats[0]
        Fh, Fl = split(F)
        a, h = silu(mm(w1t_cat, jnp.concatenate([Fh, Fl, ones, Fh], axis=0)))
        Hh, Hl = split(h)
        if kept:
            f_ref[t, 0:32, at] = Fh
            f_ref[t, 32:64, at] = Fl
            act1_ref[t, :, at] = slope(a, h)
            h1_ref[t, 0:128, at] = Hh
            h1_ref[t, 128:256, at] = Hl
        return jnp.concatenate([Hh, Hl, ones, Hh], axis=0)

    def second_layer(t, unit, feats, kept, H):
        n = len(feats)
        at = pl.ds(unit * 128, n * 128)
        a, h = silu(mm(w2t_cat, H))
        wsel = wsel_ref[:, at]
        if kept:
            q2_ref[t, :, at] = wsel * slope(a, h)
            h2f_ref[t, :, at] = h
        z = jnp.sum(wsel * h, axis=0, keepdims=True)
        return [z[:, i * 128:(i + 1) * 128] for i in range(n)]

    def staggered(tasks, first, second):
        out, held = [], []
        for task in tasks:
            held.append((task, first(*task)))
            if len(held) > DEPTH:
                done, x = held.pop(0)
                out.append(second(*done, x))
        for done, x in held:
            out.append(second(*done, x))
        return out

    def layers(*tasks):
        return staggered(tasks, first_layer, second_layer)

    def settle(t, units):
        for part in pairs(units):
            at = pl.ds(part[0] * 128, len(part) * 128)
            Hh, Hl = split(h2f_ref[t, :, at])
            h2_ref[t, 0:128, at] = Hh
            h2_ref[t, 128:256, at] = Hl

    def put_features(V, near):
        for f in range(4):
            for part, x in enumerate((V[f],) + tuple(near[f])):
                feat_ref[(4 * part + f) * 8:(4 * part + f + 1) * 8, :] = x

    def feats_of(*rows):
        return [feat_ref[pl.ds(r, 32, stride=8), :] for r in rows]

    def own_layers(t, first, last):
        rows = [ROW_OF_UNIT[u:u + 2] for u in range(first, last, 2)]
        tasks = [(t, u, feats_of(*r), True) for u, r in zip(range(first, last, 2), rows)]
        for pair, out in zip(rows, layers(*tasks)):
            for r, z in zip(pair, out):
                z_ref[r:r + 1, :] = z

    in0_col[0] = column(1, 2)
    in0_col[1] = column(126, 125)
    dfeat_ref[...] = jnp.zeros_like(dfeat_ref)
    feat_ref[160:256, :] = storm_ref[...]
    put_features(V0, [
        (turn(V0[f], 1, 0), turn(V0[f], 7, 0), turn(V0[f], 1, 1), turn(V0[f], 127, 1)) for f in range(4)
    ])
    own_layers(0, 0, INNER)
    settle(0, inner_units)
    for ref, rows in ((f_ref, 64), (h1_ref, 256)):
        ref[:, rows:rows + 16, :] = jnp.ones((2, 16, ref.shape[2]), bf16)
    for ref in (zx_ref, cidx_ref, wetx_ref, dunex_ref):
        ref[...] = jnp.zeros_like(ref)
    spare = acc_ref.shape[0] - ROWS
    if spare:
        acc_ref[ROWS:, :] = jnp.zeros((spare, 128), f32)

    each(has_src, lambda d: copy0_of(d).wait_recv())
    each(diag_src, lambda e: diag_of(e).wait_recv())
    relay(0)

    halo0 = Halo(rcv0_row, rcv0_col)
    near0 = [halo0.around(V0[f], f) for f in range(12)]
    put_features(V0, near0)
    sides = jnp.concatenate(
        [
            rcv0_col[1], rcv0_col[0], snd0_col[0], snd0_col[1], in0_col[0], in0_col[1],
            jnp.zeros((80, 128), f32),
        ], axis=0
    )
    T = jnp.transpose(sides)
    SE, SW, NE, NW = [rcv_diag[e] for e in range(4)]
    RS, RN = rcv0_row[0, 0:16, :], rcv0_row[1, 0:16, :]
    group = lane16 // 8
    V, far = T[0:16], T[NEXT:NEXT + 16]
    plus, minus = turn(V, 16, 1), turn(V, -16, 1)
    N, S = turn(V, 1, 1), turn(V, -1, 1)
    for at, x, c in ((0, NW, 127), (8, NE, 0), (16, RN, 0), (24, RN, 127), (32, RN, 1), (40, RN, 126)):
        N = jnp.where(lane16 == at, turn(x, at - c, 1), N)
    for at, x, c in ((7, SW, 127), (15, SE, 0), (23, RS, 0), (31, RS, 127), (39, RS, 1), (47, RS, 126)):
        S = jnp.where(lane16 == at, turn(x, at - c, 1), S)
    W = jnp.where(group == 1, minus, jnp.where(jnp.logical_or(group == 2, group == 4), plus, far))
    E = jnp.where(group == 0, minus, jnp.where(jnp.logical_or(group == 3, group == 5), plus, far))
    outer = [(V, N, S, W, E)]
    for V, N, S, west, east in (
        (RN, rcv0_row[1, NEXT:NEXT + 16, :], snd0_row[0, 0:16, :], NW, NE),
        (RS, snd0_row[1, 0:16, :], rcv0_row[0, NEXT:NEXT + 16, :], SW, SE),
    ):
        W = jnp.where(lane16 == 0, turn(west, 1, 1), turn(V, 1, 1))
        E = jnp.where(lane16 == 127, turn(east, 127, 1), turn(V, 127, 1))
        outer.append((V, N, S, W, E))
    storms = [T[COL_STORM:COL_STORM + 12], rcv0_row[1, STORM:STORM + 12, :], rcv0_row[0, STORM:STORM + 12, :]]
    mask_rows = [
        [T[COL_MASK + m:COL_MASK + m + 1] for m in range(3)],
        [rcv0_row[1, 12 + m:13 + m, :] for m in range(3)],
        [rcv0_row[0, 12 + m:13 + m, :] for m in range(3)],
    ]
    for w in range(3):
        for part in range(5):
            fx_ref[w, 4 * part:4 * part + 4, :] = outer[w][part][0:4]
        fx_ref[w, 20:32, :] = storms[w]
        wetx_ref[w:w + 1, :] = mask_rows[w][0]
        dunex_ref[w:w + 1, :] = mask_rows[w][1]
        ids = mask_rows[w][2].astype(jnp.int32)
        cidx_ref[w:w + 1, :] = ids
        choose(STRIP + w, ids)
    cidx = cidx_ref[...]
    (z_top, z_low), (z_strip,), (z_north, z_south) = layers(
        (0, INNER, feats_of(0, 7), True), (0, STRIP, [fx_ref[0]], True),
        (0, STRIP + 1, [fx_ref[1], fx_ref[2]], False),
    )
    z_ref[0:1, :] = z_top
    z_ref[7:8, :] = z_low
    zx_ref[0:1, :] = z_strip
    zx_ref[1:2, :] = z_north
    zx_ref[2:3, :] = z_south
    biasx = bias_of(cidx)
    zx = zx_ref[...] + biasx
    pickx = pickup_gain * softplus(zx) * (1.0 - dunex_ref[...])

    def from_strip(x, start):
        return jnp.sum(jnp.where(lane == start + row, x, 0.0), axis=1, keepdims=True)

    inside = jnp.logical_and(row > 0, row < 7)
    at_west = jnp.logical_and(inside, lane == 0)
    at_east = jnp.logical_and(inside, lane == 127)

    def with_strip(z, strip):
        z = jnp.where(at_west, from_strip(strip, 16), z)
        return jnp.where(at_east, from_strip(strip, 24), z)

    def to_strip(x):
        out = jnp.where(lane == 16 + row, x[:, 0:1], jnp.where(lane == 24 + row, x[:, 127:128], 0.0))
        return jnp.sum(jnp.where(inside, out, 0.0), axis=0, keepdims=True)

    z0 = with_strip(z_ref[...] + bsel, zx[0:1, :])

    def advanced(w):
        V, N, S, W, E = outer[w]
        pick, wet = pickx[w:w + 1, :], wetx_ref[w:w + 1, :]
        lap = N + S + W + E - 4.0 * V
        ad, cd = S - N, E - W
        spread = jnp.where(field == 3, bed_diffusion, diffusion) * lap
        sediment = spread - advection * (V[1:2] * ad + V[2:3] * cd) - settling * V
        sediment = sediment + jnp.where(field - 4 == cidx[w:w + 1, :], pick, 0.0)
        total = jnp.sum(
            jnp.where(jnp.logical_and(field >= 4, field < 12), V, 0.0), axis=0, keepdims=True
        )
        first = jnp.where(field == 0, -advection * (ad[1:2] + cd[2:3]), settling * total - pick)
        first = jnp.where(field == 1, -advection * ad[0:1] - friction * V[1:2], first)
        first = jnp.where(field == 2, -advection * cd[0:1] - friction * V[2:3], first)
        return V + wet * jnp.where(field < 4, spread + first, sediment)

    strip1, RN, RS = advanced(0), advanced(1), advanced(2)
    ring_row[1] = RN
    ring_row[0] = RS
    back = jnp.transpose(jnp.concatenate([strip1, jnp.zeros((112, 128), f32)], axis=0))
    ring_col[1] = back[0:8]
    ring_col[0] = back[8:16]

    pickup = softplus(z0) * wash[0]
    lap = []
    for f in range(12):
        n, s, w, e = near0[f]
        lap.append(n + s + w + e - 4.0 * V0[f])
    total = V0[4]
    for k in range(1, 8):
        total = total + V0[4 + k]
    ad = [near0[f][1] - near0[f][0] for f in range(12)]
    cd = [near0[f][3] - near0[f][2] for f in range(12)]
    tend = [
        diffusion * lap[0] - advection * (ad[1] + cd[2]),
        diffusion * lap[1] - advection * ad[0] - friction * V0[1],
        diffusion * lap[2] - advection * cd[0] - friction * V0[2],
        bed_diffusion * lap[3] - pickup_gain * pickup + settling * total,
    ]
    for k in range(8):
        x = diffusion * lap[4 + k] - advection * (V0[1] * ad[4 + k] + V0[2] * cd[4 + k])
        x = x + jnp.where(cid == k, pickup_gain * pickup, 0.0) - settling * V0[4 + k]
        tend.append(x)
    V1 = [V0[f] + wets[0] * tend[f] for f in range(12)]

    halo1 = Halo(ring_row, ring_col)
    near1 = [halo1.around(V1[f], f) for f in range(12)]
    put_features(V1, near1)
    plus, minus = turn(strip1, 16, 1), turn(strip1, -16, 1)
    N, S = turn(strip1, 1, 1), turn(strip1, -1, 1)
    for at, c in ((16, 0), (24, 127)):
        N = jnp.where(lane16 == at, turn(RN, at - c, 1), N)
        S = jnp.where(lane16 == at + 7, turn(RS, at + 7 - c, 1), S)
    W, E = jnp.where(group == 2, plus, minus), jnp.where(group == 2, minus, plus)
    for part, x in enumerate((strip1, N, S, W, E)):
        fx_ref[0, 4 * part:4 * part + 4, :] = x[0:4]
    (z_top, z_low), (z_strip,) = layers(
        (1, INNER, feats_of(0, 7), True), (1, STRIP, [fx_ref[0]], True)
    )
    z_ref[0:1, :] = z_top
    z_ref[7:8, :] = z_low
    z_strip = z_strip + biasx[0:1, :]
    z1 = with_strip(z_ref[...] + bsel, z_strip)
    lam2 = [cot_ref[f * 8:(f + 1) * 8, :] for f in range(12)]

    def closure_cotangent(t, gate, lam):
        G = [None] * 3 + [wets[t] * lam[f] for f in range(3, 12)]
        picked = G[4]
        for k in range(1, 8):
            picked = jnp.where(cid == k, G[4 + k], picked)
        return pickup_gain * (picked - G[3]) * wash[t] * gate

    def sigmoid(z):
        return 1.0 / (1.0 + jnp.exp(-z))

    def adjoint_two(t, units, drows):
        for part in pairs(list(zip(units, drows))):
            at = pl.ds(part[0][0] * 128, len(part) * 128)
            drow = 0.5 * jnp.concatenate([d for _, d in part], axis=1)
            Dh, Dl = split(q2_ref[t, :, at] * drow)
            d2_ref[t, 0:128, at] = Dh
            d2_ref[t, 128:256, at] = Dl

    def adjoint_one(t, units):
        def product(part):
            at = pl.ds(part[0] * 128, len(part) * 128)
            return mm(w2_cat, jnp.concatenate([d2_ref[t, :, at], d2_ref[t, 0:128, at]], axis=0))

        def rest(part, d1):
            at = pl.ds(part[0] * 128, len(part) * 128)
            Dh, Dl = split(d1 * act1_ref[t, :, at])
            d1_ref[t, 0:128, at] = Dh
            d1_ref[t, 128:256, at] = Dl

        staggered([(part,) for part in pairs(units)], product, rest)

    def feature_cotangent(t, units):
        out = []

        def product(part):
            at = pl.ds(part[0] * 128, len(part) * 128)
            return mm(w1_cat, jnp.concatenate([d1_ref[t, :, at], d1_ref[t, 0:128, at]], axis=0))

        def rest(part, dF):
            for i, u in enumerate(part):
                one = dF[:, i * 128:(i + 1) * 128]
                if u < OWN:
                    dfeat_ref[pl.ds(ROW_OF_UNIT[u], 32, stride=8), :] = one
                else:
                    out.append(one)

        staggered([(part,) for part in pairs(units)], product, rest)
        return out

    def adjoint_cells(D, G, near, V, lam):
        lap = [bed_diffusion if f == 3 else diffusion for f in range(12)]
        lg = [lap[f] * G[f] for f in range(12)]
        c = [lam[f] - 4.0 * lg[f] for f in range(12)]
        alongs = jnp.zeros((8, 128), f32)
        crosses = jnp.zeros((8, 128), f32)
        along_part = [advection * G[1], advection * G[0], None, None]
        cross_part = [advection * G[2], None, advection * G[0], None]
        for k in range(8):
            n, s, w, e = near[4 + k]
            alongs = alongs + (s - n) * G[4 + k]
            crosses = crosses + (e - w) * G[4 + k]
            c[4 + k] = c[4 + k] + settling * (G[3] - G[4 + k])
            ag = advection * G[4 + k]
            along_part.append(V[1] * ag)
            cross_part.append(V[2] * ag)
        c[1] = c[1] - friction * G[1] - advection * alongs
        c[2] = c[2] - friction * G[2] - advection * crosses
        to = [[], [], [], []]
        for f in range(12):
            for d, part, sign in ((0, along_part, 1), (1, along_part, -1), (2, cross_part, 1), (3, cross_part, -1)):
                x = lg[f]
                if part[f] is not None:
                    x = x + part[f] if sign > 0 else x - part[f]
                if f < 4:
                    x = x + D[4 + 4 * d + f]
                to[d].append(x)
            if f < 4:
                c[f] = c[f] + D[f]
        return c, to

    def gather(c, to, halo):
        return [
            c[f] + halo.south(to[0][f], f) + halo.north(to[1][f], f)
            + halo.east(to[2][f], f) + halo.west(to[3][f], f)
            for f in range(12)
        ]

    def keep(start, part, first):
        at = pl.ds(start, part.shape[0])
        acc_ref[at, :] = part if first else acc_ref[at, :] + part

    def weights_two(t, units, ids, drows, first):
        at = pl.ds(units[0] * 128, len(units) * 128)
        width = len(units) * 128
        dr = jnp.concatenate(
            [jnp.where(row == k, d, 0.0) for k, d in zip(ids, drows)], axis=1
        )
        dbo = jnp.sum(
            jnp.where(row == lane, jnp.sum(dr, axis=1, keepdims=True), 0.0), axis=0, keepdims=True
        )
        drh, drl = split(jnp.concatenate([dr, jnp.zeros((8, width), f32)], axis=0))
        top = mm_nt(jnp.concatenate([drh, drl], axis=0), h2_ref[t, :, at])
        dwo = top[:8, :128] + top[16:24, :128] + top[:8, 128:]
        top = mm_nt(h1_ref[t, :, at], d2_ref[t, :, at])
        keep(0, top[:128, :128] + top[128:256, :128] + top[:128, 128:], first)
        keep(ROW_WO, dwo, first)
        ones = top[256:264, :128] + top[256:264, 128:]
        keep(ROW_BIAS, jnp.where(row == 1, ones, jnp.where(row == 2, dbo, 0.0)), first)

    def weights_one(t, units, first):
        at = pl.ds(units[0] * 128, len(units) * 128)
        top = mm_nt(f_ref[t, :, at], d1_ref[t, :, at])
        keep(ROW_W1, top[:32, :128] + top[32:64, :128] + top[:32, 128:], first)
        ones = top[64:72, :128] + top[64:72, 128:]
        keep(ROW_BIAS, jnp.where(row == 0, ones, 0.0), False)

    def rows_of(x, units):
        return [x[ROW_OF_UNIT[u]:ROW_OF_UNIT[u] + 1, :] for u in units]

    G1 = [wets[1] * lam2[f] for f in range(12)]
    columns = jnp.logical_and(lane > 0, lane < 127)

    def patched(strip_back):
        turned = jnp.transpose(jnp.concatenate([strip_back, jnp.zeros((96, 128), f32)], axis=0))
        at_w, at_e = turned[16:24], turned[24:32]
        out = []
        for f in range(20):
            x = dfeat_ref[f * 8:(f + 1) * 8, :]
            x = jnp.where(at_west, turn(at_w, -f, 1), x)
            out.append(jnp.where(at_east, turn(at_e, 127 - f, 1), x))
        return out

    dz1 = closure_cotangent(1, sigmoid(z1), lam2)
    edge_rows1 = [dz1[0:1, :], dz1[7:8, :], to_strip(dz1)]
    adjoint_two(1, edge_units, edge_rows1)
    adjoint_one(1, edge_units)
    strip_back = feature_cotangent(1, edge_units)[0]
    _, to1 = adjoint_cells(patched(strip_back), G1, near1, V1, lam2)
    fill(1, *to1)
    each(has_dst, lambda d: copy0_of(d).wait_send())
    each(has_dst, lambda d: copy_of(1, d).start())
    relayed(0)
    relay(1)

    own_layers(1, 0, INNER)
    dz1 = closure_cotangent(1, sigmoid(z_ref[...] + bsel), lam2)
    dz_ref[...] = jnp.where(columns, dz1, 0.0)
    drows1 = rows_of(dz_ref, inner_units)
    adjoint_two(1, inner_units, drows1)
    adjoint_one(1, inner_units)
    feature_cotangent(1, inner_units)
    c1, to1 = adjoint_cells(patched(strip_back), G1, near1, V1, lam2)
    gate0 = sigmoid(z0)
    settle(1, inner_units + edge_units)
    settle(0, edge_units)
    ids_edge = [cid[0:1, :], cid[7:8, :], cidx_ref[0:1, :]]
    weights_two(
        1, inner_units + edge_units, rows_of(cid, inner_units) + ids_edge, drows1 + edge_rows1, True
    )
    weights_one(1, inner_units + edge_units, True)
    lam1 = [
        c1[f] + turn(to1[0][f], 7, 0) + turn(to1[1][f], 1, 0) + turn(to1[2][f], 127, 1) + turn(to1[3][f], 1, 1)
        for f in range(12)
    ]
    dz0 = closure_cotangent(0, gate0, lam1)
    dz_ref[...] = jnp.where(columns, dz0, 0.0)
    drows0 = rows_of(dz_ref, inner_units)
    adjoint_two(0, inner_units, drows0)
    weights_two(0, inner_units, rows_of(cid, inner_units), drows0, False)
    adjoint_one(0, inner_units)
    weights_one(0, inner_units, False)
    feature_cotangent(0, inner_units)

    each(has_src, lambda d: copy_of(1, d).wait_recv())
    relayed(1)
    lam1 = gather(c1, to1, Halo(rcv_row.at[0], rcv_col.at[0]))
    dz0 = closure_cotangent(0, gate0, lam1)
    drows0 = [dz0[0:1, :], dz0[7:8, :], to_strip(dz0)]
    adjoint_two(0, edge_units, drows0)
    weights_two(0, edge_units, ids_edge, drows0, False)
    adjoint_one(0, edge_units)
    weights_one(0, edge_units, False)

    size = src_b.shape[0]
    last_core = nsu - 1
    owner = su == last_core
    mine = pl.ds(pl.multiple_of(cs * size, 8), size)
    spans = [(dz, dx) for dz in range(nal) for dx in range(ncr)]
    pieces = (rcv_a, rcv_e)
    low_rows = 2 * ncr * rcv_e.shape[1]

    sense = 1 - 2 * ((2 * al) // nal)

    def chip_at(span):
        return lax.rem(al + nal + sense * span[0], nal), lax.rem(cr + span[1], ncr)

    after = max(ncs, nal) - 1

    def is_end(a):
        return jnp.logical_or(a == 0, a == nal - 1)

    def piece_of(a, c, end):
        n = pieces[end].shape[1]
        start = ((a // (nal - 1)) * ncr + c) * n if end else low_rows + ((a - 1) * ncr + c) * n
        return pl.ds(pl.multiple_of(start, 8), n)

    def to_owner(k, end):
        a, c = chip_at(spans[k])
        source = lax.rem(al - a + nal, nal) * ncr + lax.rem(cr - c + ncr, ncr)
        slot = 2 * (source - 1) + su if k else 2 * (len(spans) - 1)
        return pltpu.make_async_remote_copy(
            src_ref=acc_ref.at[piece_of(a, c, end), :], dst_ref=pieces[end].at[slot],
            send_sem=load_sem.at[8], recv_sem=load_sem.at[10],
            device_id=(g, a, c, last_core), device_id_type=MESH,
        )

    def from_owner(k, core, end):
        a, c = chip_at(spans[k])
        own = full_ref.at[piece_of(al, cr, end), :]
        return pltpu.make_async_remote_copy(
            src_ref=own, dst_ref=own, send_sem=load_sem.at[9], recv_sem=load_sem.at[11],
            device_id=(g, a, c, core), device_id_type=MESH,
        )

    def share(k):
        ends = is_end(chip_at(spans[k])[0])

        @pl.when(ends)
        def _():
            to_owner(k, 1).start()

        @pl.when(jnp.logical_not(ends))
        def _():
            to_owner(k, 0).start()

    def each_owner(action):
        ends = is_end(al)

        @pl.when(jnp.logical_and(owner, ends))
        def _():
            action(1)

        @pl.when(jnp.logical_and(owner, jnp.logical_not(ends)))
        def _():
            action(0)

    def spread(end):
        ref = pieces[end]
        own = piece_of(al, cr, end)
        all_of(ref, load_sem.at[10]).wait_recv()
        total = acc_ref[own, :]
        for j in range(ref.shape[0]):
            total = total + ref[j]
        full_ref[own, :] = total * factor
        for k in range(others, -1, -1):
            for core in range(nsu):
                if k or core != last_core:
                    from_owner(k, core, end).start()

    def close(end):
        ref = pieces[end]
        rest = pl.ds(0, acc_ref.shape[0] - ref.shape[1])
        all_of(acc_ref.at[rest, :], load_sem.at[8]).wait_send()
        all_of(full_ref.at[rest, :], load_sem.at[11]).wait_recv()
        all_of(ref, load_sem.at[9]).wait_send()

    def all_of(ref, sem):
        return pltpu.make_async_remote_copy(
            src_ref=ref, dst_ref=ref, send_sem=sem, recv_sem=sem,
            device_id=(g, al, cr, nsu - 1 - su), device_id_type=MESH,
        )

    def copy_a(j):
        peer = lax.rem(cs + j, ncs)
        return pltpu.make_async_remote_copy(
            src_ref=acc_ref.at[pl.ds(pl.multiple_of(peer * size, 8), size), :],
            dst_ref=rcv_a.at[j - 1], send_sem=sum_sem.at[j - 1], recv_sem=sum_sem.at[after + j - 1],
            device_id=dev(al, peer), device_id_type=MESH,
        )

    def copy_b(j):
        return pltpu.make_async_remote_copy(
            src_ref=src_b, dst_ref=rcv_b.at[al], send_sem=sum_sem.at[j - 1],
            recv_sem=sum_sem.at[after + 2 * ncs + j - 3],
            device_id=dev(lax.rem(al + j, nal), cs), device_id_type=MESH,
        )

    def copy_c(j):
        return pltpu.make_async_remote_copy(
            src_ref=full_ref.at[mine, :], dst_ref=full_ref.at[mine, :],
            send_sem=sum_sem.at[j - 1], recv_sem=sum_sem.at[after + ncs + j - 2],
            device_id=dev(al, lax.rem(cs + j, ncs)), device_id_type=MESH,
        )

    others = len(spans) - 1
    if direct:
        for k in range(others, 0, -1):
            share(k)

        @pl.when(jnp.logical_not(owner))
        def _():
            share(0)
    else:
        for j in range(1, ncs):
            copy_a(j).start()

    D0 = patched(feature_cotangent(0, edge_units)[0])
    G0 = [wets[0] * lam1[f] for f in range(12)]
    c0, to0 = adjoint_cells(D0, G0, near0, V0, lam1)
    fill(2, *to0)
    each(has_dst, lambda d: copy_of(1, d).wait_send())
    each(has_dst, lambda d: copy_of(2, d).start())

    if direct:
        each_owner(spread)
    else:
        total = acc_ref[mine, :]
        for j in range(1, ncs):
            copy_a(j).wait_recv()
            total = total + rcv_a[j - 1]
        src_b[...] = total
        rcv_b[al] = total
        for j in range(1, ncs):
            copy_a(j).wait_send()
        for j in range(1, nal):
            copy_b(j).start()
    each(has_src, lambda d: copy_of(2, d).wait_recv())
    last = gather(c0, to0, Halo(rcv_row.at[1], rcv_col.at[1]))
    for f in range(12):
        gstate_ref[f] = last[f]
    each(has_dst, lambda d: copy_of(2, d).wait_send())
    each(diag_dst, lambda e: diag_of(e).wait_send())
    if direct:
        each_owner(close)

        @pl.when(jnp.logical_not(owner))
        def _():
            all_of(acc_ref, load_sem.at[8]).wait_send()
            all_of(full_ref, load_sem.at[11]).wait_recv()
    else:
        for j in range(1, nal):
            copy_b(j).wait_recv()
        total = rcv_b[0]
        for j in range(1, nal):
            total = total + rcv_b[j]
        full_ref[mine, :] = total * factor
        for j in range(1, nal):
            copy_b(j).wait_send()
        for j in range(1, ncs):
            copy_c(j).start()
        for j in range(1, ncs):
            copy_c(j).wait_recv()
        for j in range(1, ncs):
            copy_c(j).wait_send()


def unpack(
    state_ref, full_ref,
    gs_hbm, gw1_hbm, gb1_hbm, gw2_hbm, gb2_hbm, gwo_hbm, gbo_hbm, gbo_ref, sem,
):
    gbo_ref[...] = full_ref[ROW_BIAS + 2:ROW_BIAS + 3, 0:8]
    parts = (
        (full_ref.at[0:128], gw2_hbm), (state_ref, gs_hbm), (full_ref.at[ROW_W1:ROW_W1 + 32], gw1_hbm),
        (full_ref.at[ROW_WO:ROW_WO + 8], gwo_hbm), (full_ref.at[ROW_BIAS:ROW_BIAS + 1], gb1_hbm),
        (full_ref.at[ROW_BIAS + 1:ROW_BIAS + 2], gb2_hbm), (gbo_ref, gbo_hbm),
    )
    copies = [pltpu.make_async_copy(src, dst, sem.at[i]) for i, (src, dst) in enumerate(parts)]
    for copy in copies:
        copy.start()
    for copy in copies:
        copy.wait()


def solution(mesh):
    nal, ncr, nsu = mesh.shape["along"], mesh.shape["cross"], mesh.shape["sub"]
    ncs = ncr * nsu
    near_only = nal <= 4 and ncs <= 4
    direct = near_only and nsu == 2 and nal == 4
    size = 8 * (-(-ROWS // (8 * ncs)))
    at_end = 8
    left = ROWS - 2 * ncr * at_end
    middle = 8 * (-(-left // (8 * 2 * ncr)))
    rows_sum = 2 * ncr * (at_end + middle) if direct else ncs * size
    sources = 2 * nal * ncr - 1

    def per_device(state, storm, wet, dune, cid, w1, b1, w2, b2, wo, bo, cot):
        rows, cols = state.shape[1], state.shape[2]
        factor = 1.0 / math.sqrt(rows * nal * cols * ncs)
        vmem = pl.BlockSpec(memory_space=pltpu.VMEM)
        hbm = pl.BlockSpec(memory_space=pl.ANY)
        flat = lambda x: x.reshape(-1, 128)
        operands = (
            flat(state), cid, w1, b1.reshape(1, 128), w2, b2.reshape(1, 128), wo.T, bo.reshape(1, 8),
            flat(storm), flat(wet), flat(dune), flat(cot),
        )
        dma = pltpu.SemaphoreType.DMA
        tile = pltpu.VMEM((8, 128), f32)
        big = lambda n, kind: pltpu.VMEM((2, n, (OWN + 1) * 128), kind)
        out = pl.pallas_call(
            functools.partial(kernel, nal, ncr, nsu, near_only, direct, factor),
            out_shape=(pltpu.VMEM((12, 8, 128), f32), pltpu.VMEM((rows_sum, 128), f32)),
            in_specs=[hbm] * 12,
            out_specs=(vmem,) * 2,
            scratch_shapes=[
                *[pltpu.VMEM(x.shape, x.dtype) for x in operands],
                dma((12,)),
                pltpu.VMEM((2, 40, 128), f32),
                pltpu.VMEM((2, 8, 128), f32),
                pltpu.VMEM((2, 8, 128), f32),
                pltpu.VMEM((2, 40, 128), f32),
                pltpu.VMEM((2, 8, 128), f32),
                pltpu.VMEM((4, 16, 128), f32),
                pltpu.VMEM((2, 2, 16, 128), f32),
                pltpu.VMEM((2, 2, 8, 128), f32),
                pltpu.VMEM((2, 2, 16, 128), f32),
                pltpu.VMEM((2, 2, 8, 128), f32),
                pltpu.VMEM((2, 16, 128), f32),
                pltpu.VMEM((2, 8, 128), f32),
                dma((2, 4)), dma((4,)), pltpu.SemaphoreType.REGULAR((2,)),
                pltpu.VMEM((256, 128), f32),
                pltpu.VMEM((256, 128), f32),
                pltpu.VMEM((3, 32, 128), f32),
                tile, tile, tile, pltpu.VMEM((8, 128), jnp.int32), tile, tile,
                pltpu.VMEM((128, (OWN + 3) * 128), f32), big(128, f32),
                big(80, bf16), big(272, bf16), big(256, bf16), big(128, f32), big(128, f32),
                big(256, bf16), big(256, bf16),
                pltpu.VMEM((rows_sum, 128), f32),
                pltpu.VMEM((sources, middle, 128) if direct else (ncs - 1, size, 128), f32),
                pltpu.VMEM((sources if direct else 1, at_end, 128), f32),
                pltpu.VMEM((size, 128), f32),
                pltpu.VMEM((1 if direct else nal, size, 128), f32),
                dma((1 if direct else max(ncs, nal) + 2 * ncs + nal - 4,)),
            ],
            compiler_params=pltpu.CompilerParams(collective_id=0, has_side_effects=True),
        )(*operands)
        gs, gw1, gb1, gw2, gb2, gwo, gbo = pl.pallas_call(
            unpack,
            out_shape=(
                jax.ShapeDtypeStruct((12, 8, 128), f32),
                jax.ShapeDtypeStruct((32, 128), f32),
                jax.ShapeDtypeStruct((1, 128), f32),
                jax.ShapeDtypeStruct((128, 128), f32),
                jax.ShapeDtypeStruct((1, 128), f32),
                jax.ShapeDtypeStruct((8, 128), f32),
                jax.ShapeDtypeStruct((1, 8), f32),
            ),
            in_specs=[vmem] * 2,
            out_specs=(hbm,) * 7,
            scratch_shapes=[pltpu.VMEM((1, 8), f32), dma((7,))],
        )(*[pltpu.with_memory_space_constraint(x, pltpu.VMEM) for x in out])
        return gs, gw1, gb1.reshape(128), gw2, gb2.reshape(128), gwo.T, gbo.reshape(8)

    tile = P(None, ("groups", "along"), ("cross", "sub"))
    return jax.shard_map(
        per_device,
        mesh=mesh,
        in_specs=(
            tile, tile, tile, tile, P(("groups", "along"), ("cross", "sub")),
            P(), P(), P(), P(), P(), P(), tile,
        ),
        out_specs=(
            tile, P("groups", None), P("groups"), P("groups", None), P("groups"),
            P("groups", None), P("groups"),
        ),
        check_vma=False,
    )
```

```python
import functools
import math

import jax
import jax.numpy as jnp
from jax import lax
from jax.experimental import pallas as pl
from jax.experimental.pallas import tpu as pltpu
from jax.sharding import PartitionSpec as P

MESH = pl.DeviceIdType.MESH
f32 = jnp.float32
bf16 = jnp.bfloat16
diffusion = 0.15
advection = 0.2
friction = 0.05
pickup_gain = 0.5
settling = 0.2
bed_diffusion = 0.1

ROW_W1 = 128
ROW_WO = 160
ROW_BIAS = 168
ROWS = 176
ROW_OF_UNIT = (1, 2, 3, 4, 5, 6, 0, 7)
INNER = 6
DEPTH = 2
OWN = 8
STRIP = 8
NEXT = 16
STORM = 28
COL_STORM = 32
COL_MASK = 44


def split(x):
    high = x.astype(bf16)
    low = (x - high.astype(f32)).astype(bf16)
    return high, low


def mm(a, b):
    return lax.dot_general(a, b, (((1,), (0,)), ((), ())), preferred_element_type=f32)


def mm_nt(a, b):
    return lax.dot_general(a, b, (((1,), (1,)), ((), ())), preferred_element_type=f32)


def beside(high, low, *extra):
    return jnp.concatenate([high, high, *extra, low], axis=1)


def bias_columns(spread):
    high = spread.astype(bf16)
    rest = spread - high.astype(f32)
    middle = rest.astype(bf16)
    low = (rest - middle.astype(f32)).astype(bf16)
    lane = lax.broadcasted_iota(jnp.int32, spread.shape, 1)
    out = jnp.zeros_like(spread)
    for i, part in enumerate((high, middle, low)):
        out = jnp.where(lane == i, part.astype(f32), out)
    return out[:, :16].astype(bf16)


def silu(u):
    a = 1.0 + jnp.tanh(u)
    return a, u * a


def slope(a, h):
    return h * (2.0 - a) + a


def softplus(z):
    return jnp.maximum(z, 0.0) + jnp.log(1.0 + jnp.exp(-jnp.abs(z)))


def kernel(
    nal, ncr, nsu, near_only, direct, factor,
    state_hbm, cid_hbm, w1_hbm, b1_hbm, w2_hbm, b2_hbm, wo_hbm, bo_hbm,
    storm_hbm, wet_hbm, dune_hbm, cot_hbm,
    gstate_ref, full_ref,
    state_ref, cid_ref, w1_ref, b1_ref, w2_ref, b2_ref, wo_ref, bo_ref,
    storm_ref, wet_ref, dune_ref, cot_ref, load_sem,
    snd0_row, snd0_col, in0_col, rcv0_row, rcv0_col, rcv_diag,
    snd_row, snd_col, rcv_row, rcv_col, ring_row, ring_col,
    edge_recv, diag_recv, relay_sem,
    feat_ref, dfeat_ref, fx_ref, z_ref, zx_ref, dz_ref, cidx_ref, wetx_ref, dunex_ref,
    wsel_ref, h2f_ref,
    f_ref, h1_ref, h2_ref, act1_ref, q2_ref, d1_ref, d2_ref,
    acc_ref, rcv_a, rcv_e, src_b, rcv_b,
    sum_sem,
):
    ncs = ncr * nsu
    g = lax.axis_index("groups")
    al = lax.axis_index("along")
    cr = lax.axis_index("cross")
    su = lax.axis_index("sub")
    cs = cr * nsu + su

    def dev(a, c):
        return (g, a, c // nsu, c % nsu)

    has_dst = (al > 0, al < nal - 1, cs > 0, cs < ncs - 1)
    has_src = (al < nal - 1, al > 0, cs < ncs - 1, cs > 0)
    dst_dev = (
        dev(al - 1, cs), dev(al + 1, cs), dev(al, cs - 1), dev(al, cs + 1),
    )
    corners = ((0, 2), (0, 3), (1, 2), (1, 3))
    diag_dst = [jnp.logical_and(has_dst[a], has_dst[c]) for a, c in corners]
    diag_src = [jnp.logical_and(has_src[a], has_src[c]) for a, c in corners]
    diag_dev = [dev(al + (1 if a else -1), cs + (1 if c == 3 else -1)) for a, c in corners]

    loads = [
        pltpu.make_async_copy(src, dst, load_sem.at[i])
        for i, (src, dst) in enumerate((
            (state_hbm, state_ref), (storm_hbm, storm_ref), (wet_hbm, wet_ref), (dune_hbm, dune_ref),
            (cid_hbm, cid_ref), (w1_hbm, w1_ref), (b1_hbm, b1_ref), (w2_hbm, w2_ref),
            (b2_hbm, b2_ref), (wo_hbm, wo_ref), (bo_hbm, bo_ref), (cot_hbm, cot_ref),
        ))
    ]
    for load in loads[:5]:
        load.start()
    for ref in (rcv0_row, rcv0_col, rcv_diag, rcv_row, rcv_col):
        ref[...] = jnp.zeros_like(ref)

    barrier = pltpu.get_barrier_semaphore()
    for e in range(4):
        @pl.when(diag_dst[e])
        def _():
            pl.semaphore_signal(barrier, inc=1, device_id=diag_dev[e], device_id_type=MESH)
    if near_only:
        for d in range(4):
            @pl.when(has_dst[d])
            def _():
                pl.semaphore_signal(barrier, inc=1, device_id=dst_dev[d], device_id_type=MESH)
    else:
        for j in range(1, ncs):
            pl.semaphore_signal(
                barrier, inc=1, device_id=dev(al, lax.rem(cs + j, ncs)), device_id_type=MESH
            )
        for j in range(1, nal):
            pl.semaphore_signal(
                barrier, inc=1, device_id=dev(lax.rem(al + j, nal), cs), device_id_type=MESH
            )
    for load in loads[5:]:
        load.start()
    beside_al = (al + nal - 1) // nal + (2 * nal - 2 - al) // nal
    beside_cs = (cs + ncs - 1) // ncs + (2 * ncs - 2 - cs) // ncs

    row = lax.broadcasted_iota(jnp.int32, (8, 128), 0)
    lane = lax.broadcasted_iota(jnp.int32, (8, 128), 1)
    field = lax.broadcasted_iota(jnp.int32, (16, 128), 0)
    lane16 = lax.broadcasted_iota(jnp.int32, (16, 128), 1)

    def turn(x, shift, axis):
        shift = shift % x.shape[axis]
        return pltpu.roll(x, shift, axis) if shift else x

    def copy0_of(d):
        src, dst = (snd0_row, rcv0_row) if d < 2 else (snd0_col, rcv0_col)
        return pltpu.make_async_remote_copy(
            src_ref=src.at[d % 2], dst_ref=dst.at[d % 2], send_sem=load_sem.at[d],
            recv_sem=edge_recv.at[0, d], device_id=dst_dev[d], device_id_type=MESH,
        )

    def diag_of(e):
        return pltpu.make_async_remote_copy(
            src_ref=snd0_row.at[e // 2, pl.ds(0, 16)], dst_ref=rcv_diag.at[e],
            send_sem=load_sem.at[4 + e], recv_sem=diag_recv.at[e],
            device_id=diag_dev[e], device_id_type=MESH,
        )

    def copy_of(k, d):
        src, dst = (snd_row, rcv_row) if d < 2 else (snd_col, rcv_col)
        return pltpu.make_async_remote_copy(
            src_ref=src.at[k - 1, d % 2], dst_ref=dst.at[k - 1, d % 2], send_sem=load_sem.at[d],
            recv_sem=edge_recv.at[k % 2, d], device_id=dst_dev[d], device_id_type=MESH,
        )

    around = beside_al + beside_cs + beside_al * beside_cs

    def relay(k):
        if near_only:
            for flags, devices in ((has_dst, dst_dev), (diag_dst, diag_dev)):
                each(flags, lambda i: pl.semaphore_signal(
                    relay_sem.at[k], inc=1, device_id=devices[i], device_id_type=MESH))

    def relayed(k):
        if near_only:
            pl.semaphore_wait(relay_sem.at[k], around)

    def each(flags, action):
        for i in range(4):
            @pl.when(flags[i])
            def _():
                action(i)

    def fill(k, xn, xs, xw, xe):
        west = jnp.zeros((8, 128), f32)
        east = jnp.zeros((8, 128), f32)
        for f in range(12):
            snd_row[k - 1, 0, f:f + 1, :] = xn[f][0:1, :]
            snd_row[k - 1, 1, f:f + 1, :] = xs[f][7:8, :]
            west = jnp.where(lane == f, turn(xw[f], f, 1), west)
            east = jnp.where(lane == f, turn(xe[f], f + 1, 1), east)
        snd_col[k - 1, 0] = west
        snd_col[k - 1, 1] = east

    class Halo:
        def __init__(self, rows, cols):
            self.rows, self.cols = rows, cols

        def south(self, x, f):
            return jnp.where(row == 7, self.rows[0, f:f + 1, :], turn(x, 7, 0))

        def north(self, x, f):
            return jnp.where(row == 0, self.rows[1, f:f + 1, :], turn(x, 1, 0))

        def east(self, x, f):
            return jnp.where(lane == 127, turn(self.cols[0], 127 - f, 1), turn(x, 127, 1))

        def west(self, x, f):
            return jnp.where(lane == 0, turn(self.cols[1], -f, 1), turn(x, 1, 1))

        def around(self, x, f):
            return self.north(x, f), self.south(x, f), self.west(x, f), self.east(x, f)

    for load in loads[:5]:
        load.wait()
    V0 = [state_ref[f * 8:(f + 1) * 8, :] for f in range(12)]
    storm = [storm_ref[f * 8:(f + 1) * 8, :] for f in range(12)]
    wets = [wet_ref[t * 8:(t + 1) * 8, :].astype(f32) for t in range(2)]
    dunes = [dune_ref[t * 8:(t + 1) * 8, :].astype(f32) for t in range(2)]
    wash = [1.0 - dunes[t] for t in range(2)]
    cid = cid_ref[...]
    masks = [wets[0], dunes[0], cid.astype(f32)]
    for d, edge, inner in ((0, 0, 1), (1, 7, 6)):
        for f in range(12):
            snd0_row[d, f:f + 1, :] = V0[f][edge:edge + 1, :]
            snd0_row[d, NEXT + f:NEXT + f + 1, :] = V0[f][inner:inner + 1, :]
            snd0_row[d, STORM + f:STORM + f + 1, :] = storm[f][edge:edge + 1, :]
        for m in range(3):
            snd0_row[d, 12 + m:13 + m, :] = masks[m][edge:edge + 1, :]
        snd0_row[d, 15:16, :] = jnp.zeros((1, 128), f32)

    def column(edge, inner):
        out = jnp.zeros((8, 128), f32)
        for x, at, c in (
            [(V0[f], f, edge) for f in range(12)] + [(V0[f], NEXT + f, inner) for f in range(12)]
            + [(storm[f], COL_STORM + f, edge) for f in range(12)]
            + [(masks[m], COL_MASK + m, edge) for m in range(3)]
        ):
            out = jnp.where(lane == at, turn(x, at - c, 1), out)
        return out

    snd0_col[0] = column(0, 1)
    snd0_col[1] = column(127, 126)
    if near_only:
        pl.semaphore_wait(barrier, around)
    else:
        pl.semaphore_wait(barrier, ncs - 1 + nal - 1 + beside_al * beside_cs)
    for load in loads[5:]:
        load.wait()
    each(diag_dst, lambda e: diag_of(e).start())
    each(has_dst, lambda d: copy0_of(d).start())

    w1 = w1_ref[...]
    w1t = jnp.transpose(jnp.concatenate([w1, jnp.zeros((96, 128), f32)], axis=0))[:, :32]
    w2 = w2_ref[...]
    w1_cat = beside(*split(w1))
    w2_cat = beside(*split(0.5 * w2))
    b1_cols = bias_columns(0.5 * jnp.transpose(jnp.broadcast_to(b1_ref[...], (128, 128))))
    b2_cols = bias_columns(0.5 * jnp.transpose(jnp.broadcast_to(b2_ref[...], (128, 128))))
    w1t_cat = beside(*split(0.5 * w1t), b1_cols)
    w2t_cat = beside(*split(0.5 * jnp.transpose(w2)), b2_cols)
    wo_t = jnp.transpose(jnp.concatenate([wo_ref[...], jnp.zeros((120, 128), f32)], axis=0))[:, :8]

    def choose(unit, ids):
        onehot = (row == ids).astype(f32)
        wsel_ref[:, unit * 128:(unit + 1) * 128] = lax.dot_general(
            wo_t, onehot, (((1,), (0,)), ((), ())),
            precision=lax.Precision.HIGHEST, preferred_element_type=f32,
        )

    def bias_of(ids):
        b = jnp.zeros((8, 128), f32)
        for k in range(8):
            b = jnp.where(ids == k, bo_ref[0:1, k:k + 1], b)
        return b

    for u in range(OWN):
        choose(u, cid[ROW_OF_UNIT[u]:ROW_OF_UNIT[u] + 1, :])
    bsel = bias_of(cid)

    inner_units = list(range(INNER))
    edge_units = [INNER, INNER + 1, STRIP]

    def pairs(units):
        step = 3 if len(units) == 3 else 2
        return [units[i:i + step] for i in range(0, len(units), step)]

    def first_layer(t, unit, feats, kept):
        n = len(feats)
        at = pl.ds(unit * 128, n * 128)
        ones = jnp.ones((16, n * 128), bf16)
        F = jnp.concatenate(feats, axis=1) if n > 1 else feats[0]
        Fh, Fl = split(F)
        a, h = silu(mm(w1t_cat, jnp.concatenate([Fh, Fl, ones, Fh], axis=0)))
        Hh, Hl = split(h)
        if kept:
            f_ref[t, 0:32, at] = Fh
            f_ref[t, 32:64, at] = Fl
            act1_ref[t, :, at] = slope(a, h)
            h1_ref[t, 0:128, at] = Hh
            h1_ref[t, 128:256, at] = Hl
        return jnp.concatenate([Hh, Hl, ones, Hh], axis=0)

    def second_layer(t, unit, feats, kept, H):
        n = len(feats)
        at = pl.ds(unit * 128, n * 128)
        a, h = silu(mm(w2t_cat, H))
        wsel = wsel_ref[:, at]
        if kept:
            q2_ref[t, :, at] = wsel * slope(a, h)
            h2f_ref[t, :, at] = h
        z = jnp.sum(wsel * h, axis=0, keepdims=True)
        return [z[:, i * 128:(i + 1) * 128] for i in range(n)]

    def staggered(tasks, first, second):
        out, held = [], []
        for task in tasks:
            held.append((task, first(*task)))
            if len(held) > DEPTH:
                done, x = held.pop(0)
                out.append(second(*done, x))
        for done, x in held:
            out.append(second(*done, x))
        return out

    def layers(*tasks):
        return staggered(tasks, first_layer, second_layer)

    def settle(t, units):
        for part in pairs(units):
            at = pl.ds(part[0] * 128, len(part) * 128)
            Hh, Hl = split(h2f_ref[t, :, at])
            h2_ref[t, 0:128, at] = Hh
            h2_ref[t, 128:256, at] = Hl

    def put_features(V, near):
        for f in range(4):
            for part, x in enumerate((V[f],) + tuple(near[f])):
                feat_ref[(4 * part + f) * 8:(4 * part + f + 1) * 8, :] = x

    def feats_of(*rows):
        return [feat_ref[pl.ds(r, 32, stride=8), :] for r in rows]

    def own_layers(t, first, last):
        rows = [ROW_OF_UNIT[u:u + 2] for u in range(first, last, 2)]
        tasks = [(t, u, feats_of(*r), True) for u, r in zip(range(first, last, 2), rows)]
        for pair, out in zip(rows, layers(*tasks)):
            for r, z in zip(pair, out):
                z_ref[r:r + 1, :] = z

    in0_col[0] = column(1, 2)
    in0_col[1] = column(126, 125)
    dfeat_ref[...] = jnp.zeros_like(dfeat_ref)
    feat_ref[160:256, :] = storm_ref[...]
    put_features(V0, [
        (turn(V0[f], 1, 0), turn(V0[f], 7, 0), turn(V0[f], 1, 1), turn(V0[f], 127, 1)) for f in range(4)
    ])
    own_layers(0, 0, INNER)
    settle(0, inner_units)
    for ref, rows in ((f_ref, 64), (h1_ref, 256)):
        ref[:, rows:rows + 16, :] = jnp.ones((2, 16, ref.shape[2]), bf16)
    for ref in (zx_ref, cidx_ref, wetx_ref, dunex_ref):
        ref[...] = jnp.zeros_like(ref)
    spare = acc_ref.shape[0] - ROWS
    if spare:
        acc_ref[ROWS:, :] = jnp.zeros((spare, 128), f32)

    each(has_src, lambda d: copy0_of(d).wait_recv())
    each(diag_src, lambda e: diag_of(e).wait_recv())
    relay(0)

    halo0 = Halo(rcv0_row, rcv0_col)
    near0 = [halo0.around(V0[f], f) for f in range(12)]
    put_features(V0, near0)
    sides = jnp.concatenate(
        [
            rcv0_col[1], rcv0_col[0], snd0_col[0], snd0_col[1], in0_col[0], in0_col[1],
            jnp.zeros((80, 128), f32),
        ], axis=0
    )
    T = jnp.transpose(sides)
    SE, SW, NE, NW = [rcv_diag[e] for e in range(4)]
    RS, RN = rcv0_row[0, 0:16, :], rcv0_row[1, 0:16, :]
    group = lane16 // 8
    V, far = T[0:16], T[NEXT:NEXT + 16]
    plus, minus = turn(V, 16, 1), turn(V, -16, 1)
    N, S = turn(V, 1, 1), turn(V, -1, 1)
    for at, x, c in ((0, NW, 127), (8, NE, 0), (16, RN, 0), (24, RN, 127), (32, RN, 1), (40, RN, 126)):
        N = jnp.where(lane16 == at, turn(x, at - c, 1), N)
    for at, x, c in ((7, SW, 127), (15, SE, 0), (23, RS, 0), (31, RS, 127), (39, RS, 1), (47, RS, 126)):
        S = jnp.where(lane16 == at, turn(x, at - c, 1), S)
    W = jnp.where(group == 1, minus, jnp.where(jnp.logical_or(group == 2, group == 4), plus, far))
    E = jnp.where(group == 0, minus, jnp.where(jnp.logical_or(group == 3, group == 5), plus, far))
    outer = [(V, N, S, W, E)]
    for V, N, S, west, east in (
        (RN, rcv0_row[1, NEXT:NEXT + 16, :], snd0_row[0, 0:16, :], NW, NE),
        (RS, snd0_row[1, 0:16, :], rcv0_row[0, NEXT:NEXT + 16, :], SW, SE),
    ):
        W = jnp.where(lane16 == 0, turn(west, 1, 1), turn(V, 1, 1))
        E = jnp.where(lane16 == 127, turn(east, 127, 1), turn(V, 127, 1))
        outer.append((V, N, S, W, E))
    storms = [T[COL_STORM:COL_STORM + 12], rcv0_row[1, STORM:STORM + 12, :], rcv0_row[0, STORM:STORM + 12, :]]
    mask_rows = [
        [T[COL_MASK + m:COL_MASK + m + 1] for m in range(3)],
        [rcv0_row[1, 12 + m:13 + m, :] for m in range(3)],
        [rcv0_row[0, 12 + m:13 + m, :] for m in range(3)],
    ]
    for w in range(3):
        for part in range(5):
            fx_ref[w, 4 * part:4 * part + 4, :] = outer[w][part][0:4]
        fx_ref[w, 20:32, :] = storms[w]
        wetx_ref[w:w + 1, :] = mask_rows[w][0]
        dunex_ref[w:w + 1, :] = mask_rows[w][1]
        ids = mask_rows[w][2].astype(jnp.int32)
        cidx_ref[w:w + 1, :] = ids
        choose(STRIP + w, ids)
    cidx = cidx_ref[...]
    (z_top, z_low), (z_strip,), (z_north, z_south) = layers(
        (0, INNER, feats_of(0, 7), True), (0, STRIP, [fx_ref[0]], True),
        (0, STRIP + 1, [fx_ref[1], fx_ref[2]], False),
    )
    z_ref[0:1, :] = z_top
    z_ref[7:8, :] = z_low
    zx_ref[0:1, :] = z_strip
    zx_ref[1:2, :] = z_north
    zx_ref[2:3, :] = z_south
    biasx = bias_of(cidx)
    zx = zx_ref[...] + biasx
    pickx = pickup_gain * softplus(zx) * (1.0 - dunex_ref[...])

    def from_strip(x, start):
        return jnp.sum(jnp.where(lane == start + row, x, 0.0), axis=1, keepdims=True)

    inside = jnp.logical_and(row > 0, row < 7)
    at_west = jnp.logical_and(inside, lane == 0)
    at_east = jnp.logical_and(inside, lane == 127)

    def with_strip(z, strip):
        z = jnp.where(at_west, from_strip(strip, 16), z)
        return jnp.where(at_east, from_strip(strip, 24), z)

    def to_strip(x):
        out = jnp.where(lane == 16 + row, x[:, 0:1], jnp.where(lane == 24 + row, x[:, 127:128], 0.0))
        return jnp.sum(jnp.where(inside, out, 0.0), axis=0, keepdims=True)

    z0 = with_strip(z_ref[...] + bsel, zx[0:1, :])

    def advanced(w):
        V, N, S, W, E = outer[w]
        pick, wet = pickx[w:w + 1, :], wetx_ref[w:w + 1, :]
        lap = N + S + W + E - 4.0 * V
        ad, cd = S - N, E - W
        spread = jnp.where(field == 3, bed_diffusion, diffusion) * lap
        sediment = spread - advection * (V[1:2] * ad + V[2:3] * cd) - settling * V
        sediment = sediment + jnp.where(field - 4 == cidx[w:w + 1, :], pick, 0.0)
        total = jnp.sum(
            jnp.where(jnp.logical_and(field >= 4, field < 12), V, 0.0), axis=0, keepdims=True
        )
        first = jnp.where(field == 0, -advection * (ad[1:2] + cd[2:3]), settling * total - pick)
        first = jnp.where(field == 1, -advection * ad[0:1] - friction * V[1:2], first)
        first = jnp.where(field == 2, -advection * cd[0:1] - friction * V[2:3], first)
        return V + wet * jnp.where(field < 4, spread + first, sediment)

    strip1, RN, RS = advanced(0), advanced(1), advanced(2)
    ring_row[1] = RN
    ring_row[0] = RS
    back = jnp.transpose(jnp.concatenate([strip1, jnp.zeros((112, 128), f32)], axis=0))
    ring_col[1] = back[0:8]
    ring_col[0] = back[8:16]

    pickup = softplus(z0) * wash[0]
    lap = []
    for f in range(12):
        n, s, w, e = near0[f]
        lap.append(n + s + w + e - 4.0 * V0[f])
    total = V0[4]
    for k in range(1, 8):
        total = total + V0[4 + k]
    ad = [near0[f][1] - near0[f][0] for f in range(12)]
    cd = [near0[f][3] - near0[f][2] for f in range(12)]
    tend = [
        diffusion * lap[0] - advection * (ad[1] + cd[2]),
        diffusion * lap[1] - advection * ad[0] - friction * V0[1],
        diffusion * lap[2] - advection * cd[0] - friction * V0[2],
        bed_diffusion * lap[3] - pickup_gain * pickup + settling * total,
    ]
    for k in range(8):
        x = diffusion * lap[4 + k] - advection * (V0[1] * ad[4 + k] + V0[2] * cd[4 + k])
        x = x + jnp.where(cid == k, pickup_gain * pickup, 0.0) - settling * V0[4 + k]
        tend.append(x)
    V1 = [V0[f] + wets[0] * tend[f] for f in range(12)]

    halo1 = Halo(ring_row, ring_col)
    near1 = [halo1.around(V1[f], f) for f in range(12)]
    put_features(V1, near1)
    plus, minus = turn(strip1, 16, 1), turn(strip1, -16, 1)
    N, S = turn(strip1, 1, 1), turn(strip1, -1, 1)
    for at, c in ((16, 0), (24, 127)):
        N = jnp.where(lane16 == at, turn(RN, at - c, 1), N)
        S = jnp.where(lane16 == at + 7, turn(RS, at + 7 - c, 1), S)
    W, E = jnp.where(group == 2, plus, minus), jnp.where(group == 2, minus, plus)
    for part, x in enumerate((strip1, N, S, W, E)):
        fx_ref[0, 4 * part:4 * part + 4, :] = x[0:4]
    (z_top, z_low), (z_strip,) = layers(
        (1, INNER, feats_of(0, 7), True), (1, STRIP, [fx_ref[0]], True)
    )
    z_ref[0:1, :] = z_top
    z_ref[7:8, :] = z_low
    z_strip = z_strip + biasx[0:1, :]
    z1 = with_strip(z_ref[...] + bsel, z_strip)
    lam2 = [cot_ref[f * 8:(f + 1) * 8, :] for f in range(12)]

    def closure_cotangent(t, gate, lam):
        G = [None] * 3 + [wets[t] * lam[f] for f in range(3, 12)]
        picked = G[4]
        for k in range(1, 8):
            picked = jnp.where(cid == k, G[4 + k], picked)
        return pickup_gain * (picked - G[3]) * wash[t] * gate

    def sigmoid(z):
        return 1.0 / (1.0 + jnp.exp(-z))

    def adjoint_two(t, units, drows):
        for part in pairs(list(zip(units, drows))):
            at = pl.ds(part[0][0] * 128, len(part) * 128)
            drow = 0.5 * jnp.concatenate([d for _, d in part], axis=1)
            Dh, Dl = split(q2_ref[t, :, at] * drow)
            d2_ref[t, 0:128, at] = Dh
            d2_ref[t, 128:256, at] = Dl

    def adjoint_one(t, units):
        def product(part):
            at = pl.ds(part[0] * 128, len(part) * 128)
            return mm(w2_cat, jnp.concatenate([d2_ref[t, :, at], d2_ref[t, 0:128, at]], axis=0))

        def rest(part, d1):
            at = pl.ds(part[0] * 128, len(part) * 128)
            Dh, Dl = split(d1 * act1_ref[t, :, at])
            d1_ref[t, 0:128, at] = Dh
            d1_ref[t, 128:256, at] = Dl

        staggered([(part,) for part in pairs(units)], product, rest)

    def feature_cotangent(t, units):
        out = []

        def product(part):
            at = pl.ds(part[0] * 128, len(part) * 128)
            return mm(w1_cat, jnp.concatenate([d1_ref[t, :, at], d1_ref[t, 0:128, at]], axis=0))

        def rest(part, dF):
            for i, u in enumerate(part):
                one = dF[:, i * 128:(i + 1) * 128]
                if u < OWN:
                    dfeat_ref[pl.ds(ROW_OF_UNIT[u], 32, stride=8), :] = one
                else:
                    out.append(one)

        staggered([(part,) for part in pairs(units)], product, rest)
        return out

    def adjoint_cells(D, G, near, V, lam):
        lap = [bed_diffusion if f == 3 else diffusion for f in range(12)]
        lg = [lap[f] * G[f] for f in range(12)]
        c = [lam[f] - 4.0 * lg[f] for f in range(12)]
        alongs = jnp.zeros((8, 128), f32)
        crosses = jnp.zeros((8, 128), f32)
        along_part = [advection * G[1], advection * G[0], None, None]
        cross_part = [advection * G[2], None, advection * G[0], None]
        for k in range(8):
            n, s, w, e = near[4 + k]
            alongs = alongs + (s - n) * G[4 + k]
            crosses = crosses + (e - w) * G[4 + k]
            c[4 + k] = c[4 + k] + settling * (G[3] - G[4 + k])
            ag = advection * G[4 + k]
            along_part.append(V[1] * ag)
            cross_part.append(V[2] * ag)
        c[1] = c[1] - friction * G[1] - advection * alongs
        c[2] = c[2] - friction * G[2] - advection * crosses
        to = [[], [], [], []]
        for f in range(12):
            for d, part, sign in ((0, along_part, 1), (1, along_part, -1), (2, cross_part, 1), (3, cross_part, -1)):
                x = lg[f]
                if part[f] is not None:
                    x = x + part[f] if sign > 0 else x - part[f]
                if f < 4:
                    x = x + D[4 + 4 * d + f]
                to[d].append(x)
            if f < 4:
                c[f] = c[f] + D[f]
        return c, to

    def gather(c, to, halo):
        return [
            c[f] + halo.south(to[0][f], f) + halo.north(to[1][f], f)
            + halo.east(to[2][f], f) + halo.west(to[3][f], f)
            for f in range(12)
        ]

    def keep(start, part, first):
        at = pl.ds(start, part.shape[0])
        acc_ref[at, :] = part if first else acc_ref[at, :] + part

    def weights_two(t, units, ids, drows, first):
        at = pl.ds(units[0] * 128, len(units) * 128)
        width = len(units) * 128
        dr = jnp.concatenate(
            [jnp.where(row == k, d, 0.0) for k, d in zip(ids, drows)], axis=1
        )
        dbo = jnp.sum(
            jnp.where(row == lane, jnp.sum(dr, axis=1, keepdims=True), 0.0), axis=0, keepdims=True
        )
        drh, drl = split(jnp.concatenate([dr, jnp.zeros((8, width), f32)], axis=0))
        top = mm_nt(jnp.concatenate([drh, drl], axis=0), h2_ref[t, :, at])
        dwo = top[:8, :128] + top[16:24, :128] + top[:8, 128:]
        top = mm_nt(h1_ref[t, :, at], d2_ref[t, :, at])
        keep(0, top[:128, :128] + top[128:256, :128] + top[:128, 128:], first)
        keep(ROW_WO, dwo, first)
        ones = top[256:264, :128] + top[256:264, 128:]
        keep(ROW_BIAS, jnp.where(row == 1, ones, jnp.where(row == 2, dbo, 0.0)), first)

    def weights_one(t, units, first):
        at = pl.ds(units[0] * 128, len(units) * 128)
        top = mm_nt(f_ref[t, :, at], d1_ref[t, :, at])
        keep(ROW_W1, top[:32, :128] + top[32:64, :128] + top[:32, 128:], first)
        ones = top[64:72, :128] + top[64:72, 128:]
        keep(ROW_BIAS, jnp.where(row == 0, ones, 0.0), False)

    def rows_of(x, units):
        return [x[ROW_OF_UNIT[u]:ROW_OF_UNIT[u] + 1, :] for u in units]

    G1 = [wets[1] * lam2[f] for f in range(12)]
    columns = jnp.logical_and(lane > 0, lane < 127)

    def patched(strip_back):
        turned = jnp.transpose(jnp.concatenate([strip_back, jnp.zeros((96, 128), f32)], axis=0))
        at_w, at_e = turned[16:24], turned[24:32]
        out = []
        for f in range(20):
            x = dfeat_ref[f * 8:(f + 1) * 8, :]
            x = jnp.where(at_west, turn(at_w, -f, 1), x)
            out.append(jnp.where(at_east, turn(at_e, 127 - f, 1), x))
        return out

    dz1 = closure_cotangent(1, sigmoid(z1), lam2)
    edge_rows1 = [dz1[0:1, :], dz1[7:8, :], to_strip(dz1)]
    adjoint_two(1, edge_units, edge_rows1)
    adjoint_one(1, edge_units)
    strip_back = feature_cotangent(1, edge_units)[0]
    _, to1 = adjoint_cells(patched(strip_back), G1, near1, V1, lam2)
    fill(1, *to1)
    each(has_dst, lambda d: copy0_of(d).wait_send())
    each(has_dst, lambda d: copy_of(1, d).start())
    relayed(0)
    relay(1)

    own_layers(1, 0, INNER)
    dz1 = closure_cotangent(1, sigmoid(z_ref[...] + bsel), lam2)
    dz_ref[...] = jnp.where(columns, dz1, 0.0)
    drows1 = rows_of(dz_ref, inner_units)
    adjoint_two(1, inner_units, drows1)
    adjoint_one(1, inner_units)
    feature_cotangent(1, inner_units)
    c1, to1 = adjoint_cells(patched(strip_back), G1, near1, V1, lam2)
    gate0 = sigmoid(z0)
    settle(1, inner_units + edge_units)
    settle(0, edge_units)
    ids_edge = [cid[0:1, :], cid[7:8, :], cidx_ref[0:1, :]]
    weights_two(
        1, inner_units + edge_units, rows_of(cid, inner_units) + ids_edge, drows1 + edge_rows1, True
    )
    weights_one(1, inner_units + edge_units, True)
    lam1 = [
        c1[f] + turn(to1[0][f], 7, 0) + turn(to1[1][f], 1, 0) + turn(to1[2][f], 127, 1) + turn(to1[3][f], 1, 1)
        for f in range(12)
    ]
    dz0 = closure_cotangent(0, gate0, lam1)
    dz_ref[...] = jnp.where(columns, dz0, 0.0)
    drows0 = rows_of(dz_ref, inner_units)
    adjoint_two(0, inner_units, drows0)
    weights_two(0, inner_units, rows_of(cid, inner_units), drows0, False)
    adjoint_one(0, inner_units)
    weights_one(0, inner_units, False)
    feature_cotangent(0, inner_units)

    each(has_src, lambda d: copy_of(1, d).wait_recv())
    relayed(1)
    lam1 = gather(c1, to1, Halo(rcv_row.at[0], rcv_col.at[0]))
    dz0 = closure_cotangent(0, gate0, lam1)
    drows0 = [dz0[0:1, :], dz0[7:8, :], to_strip(dz0)]
    adjoint_two(0, edge_units, drows0)
    adjoint_one(0, edge_units)
    weights_two(0, edge_units, ids_edge, drows0, False)
    weights_one(0, edge_units, False)

    size = src_b.shape[0]
    last_core = nsu - 1
    owner = su == last_core
    mine = pl.ds(pl.multiple_of(cs * size, 8), size)
    spans = [(dz, dx) for dz in range(nal) for dx in range(ncr)]
    pieces = (rcv_a, rcv_e)
    low_rows = 2 * ncr * rcv_e.shape[1]

    sense = 1 - 2 * ((2 * al) // nal)

    def chip_at(span):
        return lax.rem(al + nal + sense * span[0], nal), lax.rem(cr + span[1], ncr)

    after = max(ncs, nal) - 1

    def is_end(a):
        return jnp.logical_or(a == 0, a == nal - 1)

    def piece_of(a, c, end):
        n = pieces[end].shape[1]
        start = ((a // (nal - 1)) * ncr + c) * n if end else low_rows + ((a - 1) * ncr + c) * n
        return pl.ds(pl.multiple_of(start, 8), n)

    def to_owner(k, end):
        a, c = chip_at(spans[k])
        source = lax.rem(al - a + nal, nal) * ncr + lax.rem(cr - c + ncr, ncr)
        slot = 2 * (source - 1) + su if k else 2 * (len(spans) - 1)
        return pltpu.make_async_remote_copy(
            src_ref=acc_ref.at[piece_of(a, c, end), :], dst_ref=pieces[end].at[slot],
            send_sem=load_sem.at[8], recv_sem=load_sem.at[10],
            device_id=(g, a, c, last_core), device_id_type=MESH,
        )

    def from_owner(k, core, end):
        a, c = chip_at(spans[k])
        own = full_ref.at[piece_of(al, cr, end), :]
        return pltpu.make_async_remote_copy(
            src_ref=own, dst_ref=own, send_sem=load_sem.at[9], recv_sem=load_sem.at[11],
            device_id=(g, a, c, core), device_id_type=MESH,
        )

    def share(k):
        ends = is_end(chip_at(spans[k])[0])

        @pl.when(ends)
        def _():
            to_owner(k, 1).start()

        @pl.when(jnp.logical_not(ends))
        def _():
            to_owner(k, 0).start()

    def each_owner(action):
        ends = is_end(al)

        @pl.when(jnp.logical_and(owner, ends))
        def _():
            action(1)

        @pl.when(jnp.logical_and(owner, jnp.logical_not(ends)))
        def _():
            action(0)

    def spread(end):
        ref = pieces[end]
        own = piece_of(al, cr, end)
        all_of(ref, load_sem.at[10]).wait_recv()
        total = acc_ref[own, :]
        for j in range(ref.shape[0]):
            total = total + ref[j]
        full_ref[own, :] = total * factor
        for k in range(others, -1, -1):
            for core in range(nsu):
                if k or core != last_core:
                    from_owner(k, core, end).start()

    def close(end):
        ref = pieces[end]
        rest = pl.ds(0, acc_ref.shape[0] - ref.shape[1])
        all_of(acc_ref.at[rest, :], load_sem.at[8]).wait_send()
        all_of(full_ref.at[rest, :], load_sem.at[11]).wait_recv()
        all_of(ref, load_sem.at[9]).wait_send()

    def all_of(ref, sem):
        return pltpu.make_async_remote_copy(
            src_ref=ref, dst_ref=ref, send_sem=sem, recv_sem=sem,
            device_id=(g, al, cr, nsu - 1 - su), device_id_type=MESH,
        )

    def copy_a(j):
        peer = lax.rem(cs + j, ncs)
        return pltpu.make_async_remote_copy(
            src_ref=acc_ref.at[pl.ds(pl.multiple_of(peer * size, 8), size), :],
            dst_ref=rcv_a.at[j - 1], send_sem=sum_sem.at[j - 1], recv_sem=sum_sem.at[after + j - 1],
            device_id=dev(al, peer), device_id_type=MESH,
        )

    def copy_b(j):
        return pltpu.make_async_remote_copy(
            src_ref=src_b, dst_ref=rcv_b.at[al], send_sem=sum_sem.at[j - 1],
            recv_sem=sum_sem.at[after + 2 * ncs + j - 3],
            device_id=dev(lax.rem(al + j, nal), cs), device_id_type=MESH,
        )

    def copy_c(j):
        return pltpu.make_async_remote_copy(
            src_ref=full_ref.at[mine, :], dst_ref=full_ref.at[mine, :],
            send_sem=sum_sem.at[j - 1], recv_sem=sum_sem.at[after + ncs + j - 2],
            device_id=dev(al, lax.rem(cs + j, ncs)), device_id_type=MESH,
        )

    others = len(spans) - 1
    if direct:
        for k in range(others, 0, -1):
            share(k)

        @pl.when(jnp.logical_not(owner))
        def _():
            share(0)
    else:
        for j in range(1, ncs):
            copy_a(j).start()

    D0 = patched(feature_cotangent(0, edge_units)[0])
    G0 = [wets[0] * lam1[f] for f in range(12)]
    c0, to0 = adjoint_cells(D0, G0, near0, V0, lam1)
    fill(2, *to0)
    each(has_dst, lambda d: copy_of(1, d).wait_send())
    each(has_dst, lambda d: copy_of(2, d).start())

    if direct:
        each_owner(spread)
    else:
        total = acc_ref[mine, :]
        for j in range(1, ncs):
            copy_a(j).wait_recv()
            total = total + rcv_a[j - 1]
        src_b[...] = total
        rcv_b[al] = total
        for j in range(1, ncs):
            copy_a(j).wait_send()
        for j in range(1, nal):
            copy_b(j).start()
    each(has_src, lambda d: copy_of(2, d).wait_recv())
    last = gather(c0, to0, Halo(rcv_row.at[1], rcv_col.at[1]))
    for f in range(12):
        gstate_ref[f] = last[f]
    each(has_dst, lambda d: copy_of(2, d).wait_send())
    each(diag_dst, lambda e: diag_of(e).wait_send())
    if direct:
        each_owner(close)

        @pl.when(jnp.logical_not(owner))
        def _():
            all_of(acc_ref, load_sem.at[8]).wait_send()
            all_of(full_ref, load_sem.at[11]).wait_recv()
    else:
        for j in range(1, nal):
            copy_b(j).wait_recv()
        total = rcv_b[0]
        for j in range(1, nal):
            total = total + rcv_b[j]
        full_ref[mine, :] = total * factor
        for j in range(1, nal):
            copy_b(j).wait_send()
        for j in range(1, ncs):
            copy_c(j).start()
        for j in range(1, ncs):
            copy_c(j).wait_recv()
        for j in range(1, ncs):
            copy_c(j).wait_send()


def unpack(
    state_ref, full_ref,
    gs_hbm, gw1_hbm, gb1_hbm, gw2_hbm, gb2_hbm, gwo_hbm, gbo_hbm, gbo_ref, sem,
):
    gbo_ref[...] = full_ref[ROW_BIAS + 2:ROW_BIAS + 3, 0:8]
    parts = (
        (full_ref.at[0:128], gw2_hbm), (state_ref, gs_hbm), (full_ref.at[ROW_W1:ROW_W1 + 32], gw1_hbm),
        (full_ref.at[ROW_WO:ROW_WO + 8], gwo_hbm), (full_ref.at[ROW_BIAS:ROW_BIAS + 1], gb1_hbm),
        (full_ref.at[ROW_BIAS + 1:ROW_BIAS + 2], gb2_hbm), (gbo_ref, gbo_hbm),
    )
    copies = [pltpu.make_async_copy(src, dst, sem.at[i]) for i, (src, dst) in enumerate(parts)]
    for copy in copies:
        copy.start()
    for copy in copies:
        copy.wait()


def solution(mesh):
    nal, ncr, nsu = mesh.shape["along"], mesh.shape["cross"], mesh.shape["sub"]
    ncs = ncr * nsu
    near_only = nal <= 4 and ncs <= 4
    direct = near_only and nsu == 2 and nal == 4
    size = 8 * (-(-ROWS // (8 * ncs)))
    at_end = 8
    left = ROWS - 2 * ncr * at_end
    middle = 8 * (-(-left // (8 * 2 * ncr)))
    rows_sum = 2 * ncr * (at_end + middle) if direct else ncs * size
    sources = 2 * nal * ncr - 1

    def per_device(state, storm, wet, dune, cid, w1, b1, w2, b2, wo, bo, cot):
        rows, cols = state.shape[1], state.shape[2]
        factor = 1.0 / math.sqrt(rows * nal * cols * ncs)
        vmem = pl.BlockSpec(memory_space=pltpu.VMEM)
        hbm = pl.BlockSpec(memory_space=pl.ANY)
        flat = lambda x: x.reshape(-1, 128)
        operands = (
            flat(state), cid, w1, b1.reshape(1, 128), w2, b2.reshape(1, 128), wo.T, bo.reshape(1, 8),
            flat(storm), flat(wet), flat(dune), flat(cot),
        )
        dma = pltpu.SemaphoreType.DMA
        tile = pltpu.VMEM((8, 128), f32)
        big = lambda n, kind: pltpu.VMEM((2, n, (OWN + 1) * 128), kind)
        out = pl.pallas_call(
            functools.partial(kernel, nal, ncr, nsu, near_only, direct, factor),
            out_shape=(pltpu.VMEM((12, 8, 128), f32), pltpu.VMEM((rows_sum, 128), f32)),
            in_specs=[hbm] * 12,
            out_specs=(vmem,) * 2,
            scratch_shapes=[
                *[pltpu.VMEM(x.shape, x.dtype) for x in operands],
                dma((12,)),
                pltpu.VMEM((2, 40, 128), f32),
                pltpu.VMEM((2, 8, 128), f32),
                pltpu.VMEM((2, 8, 128), f32),
                pltpu.VMEM((2, 40, 128), f32),
                pltpu.VMEM((2, 8, 128), f32),
                pltpu.VMEM((4, 16, 128), f32),
                pltpu.VMEM((2, 2, 16, 128), f32),
                pltpu.VMEM((2, 2, 8, 128), f32),
                pltpu.VMEM((2, 2, 16, 128), f32),
                pltpu.VMEM((2, 2, 8, 128), f32),
                pltpu.VMEM((2, 16, 128), f32),
                pltpu.VMEM((2, 8, 128), f32),
                dma((2, 4)), dma((4,)), pltpu.SemaphoreType.REGULAR((2,)),
                pltpu.VMEM((256, 128), f32),
                pltpu.VMEM((256, 128), f32),
                pltpu.VMEM((3, 32, 128), f32),
                tile, tile, tile, pltpu.VMEM((8, 128), jnp.int32), tile, tile,
                pltpu.VMEM((128, (OWN + 3) * 128), f32), big(128, f32),
                big(80, bf16), big(272, bf16), big(256, bf16), big(128, f32), big(128, f32),
                big(256, bf16), big(256, bf16),
                pltpu.VMEM((rows_sum, 128), f32),
                pltpu.VMEM((sources, middle, 128) if direct else (ncs - 1, size, 128), f32),
                pltpu.VMEM((sources if direct else 1, at_end, 128), f32),
                pltpu.VMEM((size, 128), f32),
                pltpu.VMEM((1 if direct else nal, size, 128), f32),
                dma((1 if direct else max(ncs, nal) + 2 * ncs + nal - 4,)),
            ],
            compiler_params=pltpu.CompilerParams(collective_id=0, has_side_effects=True),
        )(*operands)
        gs, gw1, gb1, gw2, gb2, gwo, gbo = pl.pallas_call(
            unpack,
            out_shape=(
                jax.ShapeDtypeStruct((12, 8, 128), f32),
                jax.ShapeDtypeStruct((32, 128), f32),
                jax.ShapeDtypeStruct((1, 128), f32),
                jax.ShapeDtypeStruct((128, 128), f32),
                jax.ShapeDtypeStruct((1, 128), f32),
                jax.ShapeDtypeStruct((8, 128), f32),
                jax.ShapeDtypeStruct((1, 8), f32),
            ),
            in_specs=[vmem] * 2,
            out_specs=(hbm,) * 7,
            scratch_shapes=[pltpu.VMEM((1, 8), f32), dma((7,))],
        )(*[pltpu.with_memory_space_constraint(x, pltpu.VMEM) for x in out])
        return gs, gw1, gb1.reshape(128), gw2, gb2.reshape(128), gwo.T, gbo.reshape(8)

    tile = P(None, ("groups", "along"), ("cross", "sub"))
    return jax.shard_map(
        per_device,
        mesh=mesh,
        in_specs=(
            tile, tile, tile, tile, P(("groups", "along"), ("cross", "sub")),
            P(), P(), P(), P(), P(), P(), tile,
        ),
        out_specs=(
            tile, P("groups", None), P("groups"), P("groups", None), P("groups"),
            P("groups", None), P("groups"),
        ),
        check_vma=False,
    )
```
